32 devices in a mesh: dp: 2 (over y), hid: 4 (over x, core), wid: 4 (over z).
Axes of the slice: x: 2, y: 2, z: 4, core: 2. Of those that a mesh axis runs over, the one named last changes fastest.
Arguments:
- tokens: bfloat16 [2, 3072, 1536], P(None, ('dp', 'wid'), 'hid'), may hold values from -6 to 6
- cotangent: bfloat16 [2, 3072, 1536], P(None, ('dp', 'wid'), 'hid'), may hold values from -6 to 6
- lengths: int32 [2, 8, 3], P(None, ('dp', 'wid')), may hold values from 1 to 256, 384 in all within a row
- keep: int32 [2, 3072], P(None, ('dp', 'wid')), may hold values 0 or 1
- norm_one: bfloat16 [1, 1536], P(None, 'hid'), may hold values from 0.5 to 1.5
- w_query: bfloat16 [1536, 1536], P(('dp', 'wid'), 'hid'), may hold values from -0.15625 to 0.15625
- w_key: bfloat16 [1536, 1536], P(('dp', 'wid'), 'hid'), may hold values from -0.15625 to 0.15625
- w_value: bfloat16 [1536, 1536], P(('dp', 'wid'), 'hid'), may hold values from -0.15625 to 0.15625
- w_house: bfloat16 [1536, 1536], P(('dp', 'wid'), 'hid'), may hold values from -0.15625 to 0.15625
- w_beta: bfloat16 [1536, 12], P(('dp', 'wid'), 'hid'), may hold values from -0.15625 to 0.15625
- w_out: bfloat16 [1536, 1536], P('hid', ('dp', 'wid')), may hold values from -0.75 to 0.75
- norm_two: bfloat16 [1, 1536], P(None, 'hid'), may hold values from 0.5 to 1.5
- w_gate: bfloat16 [1536, 4096], P(('dp', 'wid'), 'hid'), may hold values from -0.15625 to 0.15625
- w_up: bfloat16 [1536, 4096], P(('dp', 'wid'), 'hid'), may hold values from -0.15625 to 0.15625
- w_down: bfloat16 [4096, 1536], P('hid', ('dp', 'wid')), may hold values from -0.09375 to 0.09375
Outputs:
- layer_out: bfloat16 [2, 3072, 1536], P(None, ('dp', 'wid'), 'hid')
- tokens_grad: bfloat16 [2, 3072, 1536], P(None, ('dp', 'wid'), 'hid')
- norm_one_grad: float32 [1, 1536], P(None, 'hid')
- w_query_grad: float32 [1536, 1536], P(('dp', 'wid'), 'hid')
- w_key_grad: float32 [1536, 1536], P(('dp', 'wid'), 'hid')
- w_value_grad: float32 [1536, 1536], P(('dp', 'wid'), 'hid')
- w_house_grad: float32 [1536, 1536], P(('dp', 'wid'), 'hid')
- w_beta_grad: float32 [1536, 12], P(('dp', 'wid'), 'hid')
- w_out_grad: float32 [1536, 1536], P('hid', ('dp', 'wid'))
- norm_two_grad: float32 [1, 1536], P(None, 'hid')
- w_gate_grad: float32 [1536, 4096], P(('dp', 'wid'), 'hid')
- w_up_grad: float32 [1536, 4096], P(('dp', 'wid'), 'hid')
- w_down_grad: float32 [4096, 1536], P('hid', ('dp', 'wid'))
The draws below stay inside these ranges and needn't reach their ends.
Inputs may be any that keep to these rules, and one draw needn't show every extreme that they name: Each buffer holds 3 sequences packed in order, their lengths summing to 384, the longest exactly 256 tokens.
All inputs are finite; a program needn't handle non-finite values. No bound on the sum of `keep` on one device may be relied on, other than what follows from the above.
Results may differ from the reference program's by a relative error of at most 0.025.
Values may be sent and summed in bfloat16 or wider, within the bound.
A program may use at most 128 MiB of HBM per device.

```python
import math
import jax
import jax.numpy as jnp
import numpy as np
from jax import lax

D = 1536
HEADS = 12
HEAD = 128
FF = 4096
MICRO = 2
LONGEST = 256
SEGS = 3
BLK = 128
HD = 1536
BUF = 384
GROUPS = 8
TOKENS = 3072


def with_ends(values, rng, low, top_value):
    index_at = [jax.random.randint(jax.random.fold_in(rng, axis), (), 0, length) for axis, length in enumerate(values.shape)]
    main_axis = values.shape.index(max(values.shape))
    neighbour = index_at[:main_axis] + [(index_at[main_axis] + 1) % values.shape[main_axis]] + index_at[main_axis + 1:]
    return values.at[tuple(index_at)].set(low).at[tuple(neighbour)].set(top_value)


def block_levels(stream_key, shape, cuts, least, top_value):
    loudness = 1.0
    for dim, blocks in cuts:
        heights = jax.random.uniform(jax.random.fold_in(jax.random.fold_in(stream_key, 6), dim), (blocks,), jnp.float32, least / len(cuts), top_value / len(cuts))
        loudness = loudness * jnp.repeat(jnp.exp(heights), shape[dim] // blocks).reshape((-1,) + (1,) * (len(shape) - 1 - dim))
    return loudness


def profile(number_of, total, limit, lean):
    loads = [(1 << 20) // math.isqrt(rank ** lean) + 1 for rank in range(2, number_of + 1)]
    rest, counts = total - limit - (number_of - 1), [1] * (number_of - 1)
    while rest > 0:
        candidates = [i for i in range(number_of - 1) if counts[i] < limit]
        mass, budget = sum([loads[i] for i in candidates]), rest
        for i in candidates:
            addition = min(limit - counts[i], max(1, budget * loads[i] // mass), rest)
            counts[i] = counts[i] + addition
            rest = rest - addition
    return np.array([limit] + counts)


def uneven_parts(stream_key, count, total, most, lean):
    if count == 2:
        one = jax.random.randint(stream_key, (), max(1, total - most), min(most, total - 1) + 1)
        return jnp.stack([one, total - one])
    sizes = jnp.asarray(profile(count, total, most, lean), jnp.int32)
    couples = (count - 1) // 2
    giver, receiver = sizes[1:1 + 2 * couples:2], sizes[2:2 + 2 * couples:2]
    slack = jnp.minimum(giver - 1, most - receiver)
    moved = jax.random.randint(jax.random.fold_in(stream_key, 1), (couples,), 0, 1 << 20) % (slack + 1)
    sizes = sizes.at[1:1 + 2 * couples:2].set(giver - moved).at[2:2 + 2 * couples:2].set(receiver + moved)
    return sizes[jax.random.permutation(jax.random.fold_in(stream_key, 2), count)]


def noise(stream_key, dims, width, most, pieces=(), kind=jnp.bfloat16):
    array = jax.random.normal(stream_key, dims, jnp.float32) * width
    if len(pieces) > 0:
        array = block_levels(stream_key, dims, pieces, -0.22, 0.18) * array
    return jnp.clip(array, min=-most, max=most).astype(kind)


def setup_inputs(seed: int = 0) -> dict:
    seeds = jax.random.split(jax.random.key(seed), 16)
    return {
        "tokens": noise(seeds[0], (MICRO, TOKENS, D), 1.0, 6.0, ((1, 8), (2, 4))),
        "cotangent": noise(seeds[1], (MICRO, TOKENS, D), 1.0, 6.0, ((1, 8), (2, 4))),
        "lengths": jax.vmap(lambda own: uneven_parts(own, SEGS, BUF, LONGEST, 2))(jax.random.split(seeds[2], MICRO * GROUPS)).reshape((MICRO, GROUPS, SEGS)).astype(jnp.int32),
        "keep": with_ends((jax.random.randint(seeds[3], (MICRO, TOKENS), 0, 8) < 7).astype(jnp.int32), jax.random.fold_in(seeds[3], 1), 0, 1),
        "norm_one": jnp.clip(1.0 + 0.1 * jax.random.normal(seeds[4], (1, D), jnp.float32), 0.5, 1.5).astype(jnp.bfloat16),
        "w_query": noise(seeds[5], (D, HD), D ** -0.5, 0.15625, ((0, 8), (1, 4))),
        "w_key": noise(seeds[6], (D, HD), D ** -0.5, 0.15625, ((0, 8), (1, 4))),
        "w_value": noise(seeds[7], (D, HD), D ** -0.5, 0.15625, ((0, 8), (1, 4))),
        "w_house": noise(seeds[8], (D, HD), D ** -0.5, 0.15625, ((0, 8), (1, 4))),
        "w_beta": noise(seeds[9], (D, HEADS), D ** -0.5, 0.15625, ((0, 8), (1, 4))),
        "w_out": noise(seeds[10], (HD, D), (max(HD // 24, 1)) ** -0.5, 0.75, ((0, 4), (1, 8))),
        "norm_two": jnp.clip(1.0 + 0.1 * jax.random.normal(seeds[11], (1, D), jnp.float32), 0.5, 1.5).astype(jnp.bfloat16),
        "w_gate": noise(seeds[12], (D, FF), D ** -0.5, 0.15625, ((0, 8), (1, 4))),
        "w_up": noise(seeds[13], (D, FF), D ** -0.5, 0.15625, ((0, 8), (1, 4))),
        "w_down": noise(seeds[14], (FF, D), FF ** -0.5, 0.09375, ((0, 4), (1, 8))),
    }


PRECISE = lax.Precision.HIGHEST
EPSILON = 1e-06

@jax.custom_vjp
def low(v):
    return lax.optimization_barrier(v.astype(jnp.bfloat16)).astype(jnp.float32)

@jax.custom_vjp
def low_back(v):
    return v

def low_keep(v):
    return (low(v), None)

def low_pass(kept, grad):
    return (grad,)

def back_keep(v):
    return (v, None)

def back_low(kept, grad):
    return (low(grad),)
low.defvjp(low_keep, low_pass)
low_back.defvjp(back_keep, back_low)

def product(left, right):
    return jnp.dot(left.astype(jnp.float32), right.astype(jnp.float32), precision=PRECISE, preferred_element_type=jnp.float32)

def segment_ids(length_row, length):
    ends = jnp.cumsum(length_row).astype(jnp.int32)
    places = jnp.arange(length, dtype=jnp.int32)
    return lax.optimization_barrier(jnp.sum((places[:, None] >= ends[None, :]).astype(jnp.int32), axis=1)).astype(jnp.int32)

def split_heads(matrix):
    return matrix.reshape(matrix.shape[0], matrix.shape[1] // HEAD, HEAD).transpose(1, 0, 2)

def merge_heads(stacked):
    return stacked.transpose(1, 0, 2).reshape(stacked.shape[1], stacked.shape[0] * stacked.shape[2])

def normalize_heads(stacked):
    return stacked * lax.rsqrt(lax.optimization_barrier(jnp.sum(stacked * stacked, axis=2, keepdims=True)) + EPSILON)

def path_head(queries, key_rows, value_rows, house_rows, beta_row, segment, keep_key, block_size):
    length, head_width = queries.shape
    block_count = length // block_size
    query_b = queries.reshape(block_count, block_size, head_width)
    key_b = key_rows.reshape(block_count, block_size, head_width)
    value_b = value_rows.reshape(block_count, block_size, head_width)
    house_b = house_rows.reshape(block_count, block_size, head_width)
    beta_b = beta_row.reshape(block_count, block_size)
    within = jnp.arange(block_size, dtype=jnp.int32)
    lower_eq = (within[:, None] >= within[None, :]).astype(jnp.float32)
    lower_st = (within[:, None] > within[None, :]).astype(jnp.float32)
    identity = jnp.eye(block_size, dtype=jnp.float32)
    inner = jnp.einsum('asd,atd->ast', house_b, house_b, precision=PRECISE)
    triangle = inner * lower_st + identity[None] / beta_b[:, :, None]
    inverse = jax.vmap(lambda matrix: jax.scipy.linalg.solve_triangular(matrix, identity, lower=True))(triangle)
    masked_qw = jnp.einsum('aid,asd->ais', query_b, house_b, precision=PRECISE) * lower_eq
    left_part = jnp.einsum('ais,ast->ait', masked_qw, inverse, precision=PRECISE)
    masked_wk = jnp.einsum('atd,ajd->atj', house_b, key_b, precision=PRECISE) * lower_st
    right_part = jnp.einsum('ast,atj->asj', inverse, masked_wk, precision=PRECISE)
    moved_q = query_b - jnp.einsum('ait,atd->aid', left_part, house_b, precision=PRECISE)
    moved_k = key_b - jnp.einsum('asj,asd->ajd', right_part, house_b, precision=PRECISE)
    near_scores = jnp.einsum('aid,ajd->aij', query_b, key_b, precision=PRECISE) - jnp.einsum('ait,atj->aij', left_part, masked_wk, precision=PRECISE)
    block_maps = jnp.eye(head_width, dtype=jnp.float32)[None] - jnp.einsum('asd,ast,ate->ade', house_b, inverse, house_b, precision=PRECISE)
    seg_blocks = segment.reshape(block_count, block_size)
    keep_blocks = keep_key.reshape(block_count, block_size)
    causal = within[:, None] >= within[None, :]
    same_pos = within[:, None] == within[None, :]
    scale = 1.0 / math.sqrt(head_width)
    valid_list = []
    masked_list = []
    top_list = []
    carried = moved_q
    for offset in range(block_count):
        count = block_count - offset
        same_seg = seg_blocks[offset:][:, :, None] == seg_blocks[:count][:, None, :]
        key_ok = keep_blocks[:count][:, None, :] == 1
        if offset == 0:
            scores = near_scores
            valid = same_seg & causal[None] & (key_ok | same_pos[None])
        else:
            scores = jnp.einsum('aid,ajd->aij', carried, moved_k[:count], precision=PRECISE)
            valid = same_seg & key_ok
            if offset + 1 < block_count:
                carried = jnp.einsum('aid,ade->aie', carried[1:], block_maps[1:count], precision=PRECISE)
        if offset == 0:
            carried = moved_q[1:]
        masked = jnp.where(valid, scores * scale, -1e+30)
        valid_list.append(valid)
        masked_list.append(masked)
        top_list.append(jnp.pad(lax.optimization_barrier(jnp.max(masked, axis=2)), ((offset, 0), (0, 0)), constant_values=-1e+30))
    top_score = lax.optimization_barrier(jnp.max(jnp.stack(top_list, axis=0), axis=0))
    expo_list = []
    total = jnp.zeros((block_count, block_size), jnp.float32)
    for offset in range(block_count):
        expo = jnp.where(valid_list[offset], jnp.exp(masked_list[offset] - top_score[offset:][:, :, None]), 0.0)
        expo_list.append(expo)
        total = total + jnp.pad(lax.optimization_barrier(jnp.sum(expo, axis=2)), ((offset, 0), (0, 0)))
    mixed = jnp.zeros((block_count, block_size, head_width), jnp.float32)
    for offset in range(block_count):
        count = block_count - offset
        probs = expo_list[offset] / total[offset:][:, :, None]
        part = jnp.einsum('aij,ajd->aid', probs, value_b[:count], precision=PRECISE)
        mixed = mixed + jnp.pad(part, ((offset, 0), (0, 0), (0, 0)))
    return mixed.reshape(length, head_width)

def layer_forward(tokens_in, params, segment, keep_row):
    norm_one, w_query, w_key, w_value, w_house, w_beta, w_out, norm_two, w_gate, w_up, w_down = params
    rms_one = lax.rsqrt(lax.optimization_barrier(jnp.mean(tokens_in * tokens_in, axis=1, keepdims=True)) + EPSILON)
    normed_one = low(tokens_in * rms_one * norm_one)
    queries = low(low_back(product(normed_one, w_query)))
    keys_all = low(low_back(product(normed_one, w_key)))
    values_all = low(low_back(product(normed_one, w_value)))
    house_raw = low_back(product(normed_one, w_house))
    beta_all = 2.0 * jax.nn.sigmoid(low_back(product(normed_one, w_beta)))
    house_hat = low(normalize_heads(split_heads(house_raw)))

    def one_head(parts):
        return path_head(parts[0], parts[1], parts[2], parts[3], parts[4], segment, keep_row, BLK)
    mixed_heads = lax.map(jax.checkpoint(one_head), (split_heads(queries), split_heads(keys_all), split_heads(values_all), house_hat, beta_all.T))
    mixed = low(merge_heads(mixed_heads))
    branch = low_back(product(mixed, w_out))
    hidden_res = tokens_in + branch
    hidden_low = low(hidden_res)
    rms_two = lax.rsqrt(lax.optimization_barrier(jnp.mean(hidden_low * hidden_low, axis=1, keepdims=True)) + EPSILON)
    normed_two = low(hidden_low * rms_two * norm_two)
    gate_proj = low_back(product(normed_two, w_gate))
    up_proj = low_back(product(normed_two, w_up))
    activated = low(jax.nn.silu(gate_proj) * up_proj)
    ffn_out = low_back(product(activated, w_down))
    return hidden_res + ffn_out

def reference(tokens, cotangent, lengths, keep, norm_one, w_query, w_key, w_value, w_house, w_beta, w_out, norm_two, w_gate, w_up, w_down):
    params = tuple((weight.astype(jnp.float32) for weight in (norm_one, w_query, w_key, w_value, w_house, w_beta, w_out, norm_two, w_gate, w_up, w_down)))
    buffers = MICRO * GROUPS
    tokens_all = tokens.astype(jnp.float32).reshape(buffers, BUF, D)
    cot_all = cotangent.astype(jnp.float32).reshape(buffers, BUF, D)
    length_all = lengths.reshape(buffers, SEGS)
    keep_all = keep.reshape(buffers, BUF)

    def one_buffer(grad_sums, buffer_in):
        tokens_in, cot_in, length_row, keep_row = buffer_in
        segment = segment_ids(length_row, BUF)

        def forward(tokens_arg, params_arg):
            return layer_forward(tokens_arg, params_arg, segment, keep_row)
        output, pullback = jax.vjp(forward, tokens_in, params)
        tokens_back, params_back = pullback(cot_in)
        grad_sums = jax.tree.map(jnp.add, grad_sums, params_back)
        return (grad_sums, (output.astype(jnp.bfloat16), tokens_back.astype(jnp.bfloat16)))
    zero_grads = tuple((jnp.zeros(weight.shape, jnp.float32) for weight in params))
    grad_sums, (outputs_all, grads_in) = lax.scan(one_buffer, zero_grads, (tokens_all, cot_all, length_all, keep_all))
    outputs_all = outputs_all.reshape(MICRO, GROUPS * BUF, D)
    grads_in = grads_in.reshape(MICRO, GROUPS * BUF, D)
    return (outputs_all, grads_in, grad_sums[0], grad_sums[1], grad_sums[2], grad_sums[3], grad_sums[4], grad_sums[5], grad_sums[6], grad_sums[7], grad_sums[8], grad_sums[9], grad_sums[10])
```

```python
import functools
import math

import jax
import jax.numpy as jnp
from jax import lax
from jax.experimental import pallas as pl
from jax.experimental.pallas import tpu as pltpu
from jax.sharding import PartitionSpec as P

BLK = 128
BUF = 384
EPSILON = 1e-06
F32 = jnp.float32
BF = jnp.bfloat16
MESH = pl.DeviceIdType.MESH
ANY = pl.BlockSpec(memory_space=pl.ANY)
VM = pl.BlockSpec(memory_space=pltpu.VMEM)
SM = pl.BlockSpec(memory_space=pltpu.SMEM)
DMA = pltpu.SemaphoreType.DMA
NRES = 30


def _dot(a,b,ca,cb): return lax.dot_general(a,b,(((ca,),(cb,)),((),())),preferred_element_type=F32)
def nn(a,b): return _dot(a.astype(BF),b.astype(BF),1,0)
def nt(a,b): return _dot(a.astype(BF),b.astype(BF),1,1)
def tn(a,b): return _dot(a.astype(BF),b.astype(BF),0,0)
def split(a):
    hi=a.astype(BF); return hi,(a-hi.astype(F32)).astype(BF)
def nn3(a,b):
    ah,al=split(a); bh,bl=split(b)
    return _dot(ah,bh,1,0)+(_dot(ah,bl,1,0)+_dot(al,bh,1,0))
INV=nn3
def iotas():
    return lax.broadcasted_iota(jnp.int32,(BLK,BLK),0), lax.broadcasted_iota(jnp.int32,(BLK,BLK),1)
def tri_inverse(inner, beta_col, row, col):
    diag=jnp.where(row==col, beta_col, 0.0)
    beta_lane=jnp.sum(diag,axis=0,keepdims=True)
    first=((row>>1)==(col>>1))&(row>col)
    x=diag-jnp.where(first, inner*beta_col*beta_lane, 0.0)
    lb=1
    while (1<<lb)<BLK:
        m=((row>>(lb+1))==(col>>(lb+1)))&((row>>lb)>(col>>lb))
        low=jnp.where(m,inner,0.0)
        x=x-INV(INV(x,low),x)
        lb+=1
    return x
def masks(a,c,e0,e1,keep_row,row,col):
    qp=row+BLK*a; kp=col+BLK*c
    segq=(qp>=e0).astype(jnp.int32)+(qp>=e1).astype(jnp.int32)
    segk=(kp>=e0).astype(jnp.int32)+(kp>=e1).astype(jnp.int32)
    ok=(segq==segk)
    if a==c: return ok&(row>=col)&((keep_row==1)|(row==col))
    return ok&(keep_row==1)
def fwd_unit(q,k,v,h,beta,keep,e0,e1):
    nb=len(q); row,col=iotas(); le=row>=col; st=row>col
    X,A1,L,W,R,Qm,Km=[],[],[],[],[],[],[]
    for a in range(nb):
        x=tri_inverse(nt(h[a],h[a]),beta[a],row,col).astype(BF)
        a1=jnp.where(le,nt(q[a],h[a]),0.0).astype(BF)
        w=jnp.where(st,nt(h[a],k[a]),0.0).astype(BF)
        l=nn(a1,x).astype(BF); r=nn(x,w).astype(BF)
        X.append(x);A1.append(a1);W.append(w);L.append(l);R.append(r)
        Qm.append((q[a].astype(F32)-nn(l,h[a])).astype(BF))
        Km.append((k[a].astype(F32)-tn(r,h[a])).astype(BF))
    scale=1.0/math.sqrt(BLK)
    S={}
    for a in range(nb):
        S[a,a]=nt(q[a],k[a])-nn(L[a],W[a])
    S[1,0]=nt(Qm[1],Km[0]); S[2,1]=nt(Qm[2],Km[1])
    u=nt(Qm[2],h[1]).astype(BF); ux=nn(u,X[1]).astype(BF)
    cq=(Qm[2].astype(F32)-nn(ux,h[1])).astype(BF)
    S[2,0]=nt(cq,Km[0])
    P={}; out=[]
    for a in range(nb):
        sc={c:jnp.where(masks(a,c,e0,e1,keep[c],row,col),S[a,c]*scale,-1e30) for c in range(a+1)}
        top=jnp.max(sc[0],axis=1,keepdims=True)
        for c in range(1,a+1): top=jnp.maximum(top,jnp.max(sc[c],axis=1,keepdims=True))
        ex={c:jnp.exp(sc[c]-top) for c in sc}
        tot=sum(jnp.sum(e,axis=1,keepdims=True) for e in ex.values())
        inv=1.0/tot
        o=0.0
        for c in sc:
            P[a,c]=(ex[c]*inv).astype(BF); o=o+nn(P[a,c],v[c])
        out.append(o)
    res=X+A1+L+W+R+Qm+Km+[u,ux,cq]+[P[0,0],P[1,0],P[1,1],P[2,0],P[2,1],P[2,2]]
    return out,res
def bwd_unit(q,k,v,h,do,res):
    nb=3; row,col=iotas(); le=row>=col; st=row>col
    X,A1,L,W,R,Qm,Km=[res[3*i:3*i+3] for i in range(7)]
    u,ux,cq=res[21:24]; pl_=res[24:30]
    P={(0,0):pl_[0],(1,0):pl_[1],(1,1):pl_[2],(2,0):pl_[3],(2,1):pl_[4],(2,2):pl_[5]}
    scale=1.0/math.sqrt(BLK)
    G={}; dv=[0.0]*nb
    for a in range(nb):
        dp={c:nt(do[a],v[c]) for c in range(a+1)}
        delta=sum(jnp.sum(P[a,c].astype(F32)*dp[c],axis=1,keepdims=True) for c in range(a+1))
        for c in range(a+1):
            G[a,c]=(P[a,c].astype(F32)*(dp[c]-delta)*scale).astype(BF)
            dv[c]=dv[c]+tn(P[a,c],do[a])
    dq=[nn(G[a,a],k[a]) for a in range(nb)]
    dk=[tn(G[a,a],q[a]) for a in range(nb)]
    dL=[-nt(G[a,a],W[a]) for a in range(nb)]
    dW=[-tn(L[a],G[a,a]) for a in range(nb)]
    dh=[0.0]*nb; dX=[0.0]*nb
    dcq=nn(G[2,0],Km[0]).astype(BF)
    dQm=[None, nn(G[1,0],Km[0]), nn(G[2,1],Km[1])+dcq.astype(F32)]
    dKm=[tn(G[1,0],Qm[1])+tn(G[2,0],cq), tn(G[2,1],Qm[2]), None]
    dux=(-nt(dcq,h[1])).astype(BF)
    dh[1]=dh[1]-tn(ux,dcq)
    du=nt(dux,X[1]).astype(BF)
    dX[1]=dX[1]+tn(u,dux)
    dQm[2]=dQm[2]+nn(du,h[1])
    dh[1]=dh[1]+tn(du,Qm[2])
    dbeta=[]
    for a in range(nb):
        if dQm[a] is not None:
            d_=dQm[a].astype(BF)
            dq[a]=dq[a]+d_.astype(F32); dL[a]=dL[a]-nt(d_,h[a]); dh[a]=dh[a]-tn(L[a],d_)
        if dKm[a] is not None:
            d_=dKm[a].astype(BF)
            dk[a]=dk[a]+d_.astype(F32); dR=(-nt(h[a],d_)).astype(BF); dh[a]=dh[a]-nn(R[a],d_)
            dX[a]=dX[a]+nt(dR,W[a]); dW[a]=dW[a]+tn(X[a],dR)
        dl=dL[a].astype(BF)
        dA=jnp.where(le,nt(dl,X[a]),0.0).astype(BF)
        dX[a]=dX[a]+tn(A1[a],dl)
        dw=jnp.where(st,dW[a],0.0).astype(BF)
        dh[a]=dh[a]+nn(dw,k[a]); dk[a]=dk[a]+tn(dw,h[a])
        dq[a]=dq[a]+nn(dA,h[a]); dh[a]=dh[a]+tn(dA,q[a])
        dM=nt(tn(X[a],dX[a]),X[a])
        dn=jnp.where(st,-dM,0.0).astype(BF)
        dh[a]=dh[a]+nn(dn,h[a])+tn(dn,h[a])
        dbeta.append(jnp.sum(jnp.where(row==col,dM,0.0),axis=1,keepdims=True))
    return dq,dk,dv,dh,dbeta


def spans(rows, step):
    return pl.ds(pl.multiple_of(rows, step), step)


class Place:
    def __init__(self, names, sizes):
        self.names, self.sizes = names, sizes
        self.d, self.h, self.w = (lax.axis_index(n) for n in ("dp", "hid", "wid"))
        self.dp, self.wid = sizes["dp"], sizes["wid"]
        self.c = lax.rem(self.h, 2)
        self.x = lax.div(self.h, 2)
        self.sib = self.at(h=self.h + 1 - 2 * self.c)
        self.xpeer = self.at(h=lax.rem(self.h + 2, 4))

    def at(self, d=None, h=None, w=None):
        where = {"dp": self.d if d is None else d, "hid": self.h if h is None else h, "wid": self.w if w is None else w}
        return tuple(where[n] for n in self.names)

    def greet(self, peers):
        barrier = pltpu.get_barrier_semaphore()
        for peer in peers:
            pl.semaphore_signal(barrier, inc=1, device_id=peer, device_id_type=MESH)
        pl.semaphore_wait(barrier, len(peers))

    def dp_peer(self, j):
        return self.at(d=lax.rem(self.d + j, self.dp))

    def wid_peer(self, k):
        return self.at(w=lax.rem(self.w + k, self.wid))

    def hid_peer(self, k):
        return self.at(h=lax.rem(self.h + k, 4))

    def group(self):
        return [
            self.at(d=lax.rem(self.d + i, self.dp), w=lax.rem(self.w + k, self.wid))
            for i in range(self.dp)
            for k in range(self.wid)
            if i + k > 0
        ]


def send(src, dst, sent, got, peer):
    return pltpu.make_async_remote_copy(
        src_ref=src, dst_ref=dst, send_sem=sent, recv_sem=got, device_id=peer, device_id_type=MESH
    )


class Gather:
    def __init__(self, me, rows, pack, full, col, source_col, width, ch, sz, rz, sy, ry):
        self.me, self.rows, self.full, self.ch = me, rows, full, ch
        self.col, self.width = col, width
        self.own = pack.at[:, pl.ds(source_col, width)]
        self.sz, self.rz, self.sy, self.ry = sz, rz, sy, ry

    def piece(self, d, o):
        return self.full.at[
            pl.ds(pl.multiple_of((d * self.me.wid + o) * self.rows, 16), self.rows), pl.ds(self.col, self.width)
        ]

    def zcopy(self, way, step):
        me, side = self.me, (way + 1) // 2
        origin = lax.clamp(0, me.w - way * step, me.wid - 1)
        src = self.own if step == 0 else self.piece(me.d, origin)
        return send(
            src,
            self.piece(me.d, origin),
            self.sz.at[self.ch, side, step],
            self.rz.at[self.ch, side, step],
            me.at(w=lax.clamp(0, me.w + way, me.wid - 1)),
        )

    def zrecv(self, way, step):
        me, side = self.me, (way + 1) // 2
        origin = lax.clamp(0, me.w - way * step, me.wid - 1)
        send(
            self.own,
            self.piece(me.d, origin),
            self.sz.at[self.ch, side, step - 1],
            self.rz.at[self.ch, side, step - 1],
            me.at(w=lax.clamp(0, me.w + way, me.wid - 1)),
        ).wait_recv()

    def ycopy(self, origin, j, src):
        me = self.me
        return send(
            src,
            self.piece(me.d, origin),
            self.sy.at[self.ch, origin, j - 1],
            self.ry.at[self.ch, origin, j - 1],
            me.dp_peer(j),
        )

    def has_next(self, way):
        return self.me.w < self.me.wid - 1 if way == 1 else self.me.w > 0

    def has_piece(self, way, step):
        return self.me.w - step >= 0 if way == 1 else self.me.w + step < self.me.wid

    def start_z(self):
        for way in (1, -1):

            @pl.when(self.has_next(way))
            def _():
                self.zcopy(way, 0).start()

    def start_y(self):
        for j in range(1, self.me.dp):
            self.ycopy(self.me.w, j, self.own).start()

    def step(self):
        me = self.me
        for step in range(1, me.wid):
            for way in (1, -1):

                @pl.when(self.has_piece(way, step))
                def _():
                    self.zrecv(way, step)

                    @pl.when(self.has_next(way))
                    def _():
                        self.zcopy(way, step).start()

                    origin = lax.clamp(0, me.w - way * step, me.wid - 1)
                    for j in range(1, me.dp):
                        self.ycopy(origin, j, self.piece(me.d, origin)).start()

    def finish(self):
        me = self.me
        for j in range(1, me.dp):
            for o in range(me.wid):
                send(
                    self.own,
                    self.piece(lax.rem(me.d + me.dp - j, me.dp), o),
                    self.sy.at[self.ch, o, j - 1],
                    self.ry.at[self.ch, o, j - 1],
                    me.dp_peer(j),
                ).wait_recv()

    def drain(self):
        me = self.me
        for way in (1, -1):

            @pl.when(self.has_next(way))
            def _():
                self.zcopy(way, 0).wait_send()

            for step in range(1, me.wid):

                @pl.when(self.has_piece(way, step) & self.has_next(way))
                def _():
                    self.zcopy(way, step).wait_send()

        for j in range(1, me.dp):
            for o in range(me.wid):
                self.ycopy(o, j, self.own).wait_send()


def column(values, lane_index):
    lanes = lax.broadcasted_iota(jnp.int32, values.shape, 1)
    return jnp.sum(jnp.where(lanes == lane_index, values, 0.0), axis=1, keepdims=True)


def forward_kernel(
    cfg, lens, keep, tok, cot, gains, pack,
    layer_out, hgrad, gain2, mgrad, qs, ks, vs, hs, hraw, beta, gf, res_o, n1_o, tok_o, wa_o, g_o,
    WA, WB, tokf, cotf, n1, n2, hlow, ng, mix, act, gg, ug, resb, s1, r1, s2, r2, acc, t2, q2, stage, hidown,
    local, hx_s, hx_r, sz, rz, sy, ry, s1s, s1r, s2s, s2r, s3s, s3r, outs, ress, stages,
):
    me = Place(cfg["names"], cfg["sizes"])
    T, D, CB, HL, HD, FL, RS = (cfg[k] for k in ("T", "D", "CB", "HL", "HD", "FL", "RS"))
    NCH = (HD + 3 * FL) // HD
    WAC = 4 * HD + BLK
    NB = T // BUF
    own_cols = pl.ds(pl.multiple_of(me.h * CB, BLK), CB)
    own_rows = pl.ds(pl.multiple_of((me.d * me.wid + me.w) * RS, 16), RS)
    c = me.c
    me.greet(
        [me.dp_peer(j) for j in range(1, me.dp)]
        + [me.wid_peer(k) for k in range(1, me.wid)]
        + [me.hid_peer(k) for k in range(1, 4)]
    )
    hid = []
    for i, (src, dst) in enumerate(((tok, tokf), (gains, gf), (cot, cotf))):
        here = pltpu.make_async_copy(src, dst.at[:, own_cols], local.at[i])
        away = [
            send(src, dst.at[:, own_cols], hx_s.at[i, k - 1], hx_r.at[i, k - 1], me.hid_peer(k)) for k in range(1, 4)
        ]
        hid.append([here] + away)
    for i in range(2):
        for copy in hid[i]:
            copy.start()
    sems = (sz, rz, sy, ry)
    first = [
        Gather(me, RS, pack, WA, a * HD, a * HD, HD + (BLK if a == 3 else 0), a, *sems) for a in range(4)
    ]

    def late(i):
        col = i * HD if isinstance(i, int) else pl.multiple_of(i * HD, BLK)
        source = WAC + i * HD if isinstance(i, int) else pl.multiple_of(WAC + i * HD, BLK)
        return Gather(me, RS, pack, WB, col, source, HD, 4 + i, *sems)

    for g in first:
        g.start_z()
        g.start_y()
    own_a = pltpu.make_async_copy(pack.at[:, pl.ds(0, WAC)], WA.at[own_rows, :], local.at[3])
    own_b = pltpu.make_async_copy(pack.at[:, pl.ds(WAC, HD + 3 * FL)], WB.at[own_rows, :], local.at[4])
    own_a.start()
    own_b.start()

    def start_late(i, carry):
        late(i).start_z()
        late(i).start_y()
        return carry

    lax.fori_loop(0, NCH, start_late, 0)
    for copy in hid[2]:
        copy.start()
    for i in range(2):
        for copy in hid[i]:
            copy.wait()
    outputs = []

    def save(src, dst, i):
        copy = pltpu.make_async_copy(src, dst, outs.at[i])
        copy.start()
        outputs.append(copy)

    save(tokf, tok_o, 0)
    RB = 32

    def norm(src, dst, gain, base):
        def body(i, carry):
            rows = spans(base + i * RB, RB)
            wide = src[rows, :].astype(F32)
            scale = lax.rsqrt(jnp.mean(wide * wide, axis=1, keepdims=True) + EPSILON)
            dst[rows, :] = (wide * scale * gf[gain : gain + 1, :]).astype(BF)
            return carry

        lax.fori_loop(0, BUF // RB, body, 0)

    for m in range(NB):
        norm(tokf, n1, 0, m * BUF)
    save(n1, n1_o, 1)

    def project(a):
        g = first[a]
        for m in range(NB):
            rows = n1[m * BUF : (m + 1) * BUF, :]
            made = nn(rows, WA[:, a * HD : (a + 1) * HD])
            for hd in range(HL):
                part = made[:, hd * BLK : (hd + 1) * BLK]
                u = m * HL + hd
                if a < 3:
                    (qs, ks, vs)[a][u] = part.astype(BF)
                else:
                    hraw[u] = part
                    hs[u] = (part * lax.rsqrt(jnp.sum(part * part, axis=1, keepdims=True) + EPSILON)).astype(BF)
            if a == 3:
                beta[m * BUF : (m + 1) * BUF, :] = 2.0 * jax.nn.sigmoid(nn(rows, WA[:, 4 * HD :]))

    own_a.wait()
    first[0].step()
    first[1].step()
    first[0].finish()
    project(0)
    first[2].step()
    first[1].finish()
    project(1)
    first[3].step()
    first[2].finish()
    project(2)
    first[3].finish()
    project(3)
    save(WA, wa_o, 2)
    own_b.wait()

    def attend(u, carry):
        m, hd = lax.div(u, HL), lax.rem(u, HL)
        slot = lax.rem(u, 2)
        e0 = lens[m, 0]
        e1 = e0 + lens[m, 1]
        parts = [slice(a * BLK, (a + 1) * BLK) for a in range(3)]
        strength = [column(beta[spans(m * BUF + a * BLK, BLK), :], hd) for a in range(3)]
        keys = [keep[m, :, p] for p in parts]
        out, res = fwd_unit(
            [qs[u, p, :] for p in parts], [ks[u, p, :] for p in parts], [vs[u, p, :] for p in parts],
            [hs[u, p, :] for p in parts], strength, keys, e0, e1,
        )
        for a in range(3):
            mix[spans(m * BUF + a * BLK, BLK), pl.ds(pl.multiple_of(hd * BLK, BLK), BLK)] = out[a].astype(BF)

        @pl.when(u >= 2)
        def _():
            pltpu.make_async_copy(resb.at[slot], res_o.at[u], ress.at[slot]).wait()

        for i, value in enumerate(res):
            resb[slot, i] = value
        pltpu.make_async_copy(resb.at[slot], res_o.at[u], ress.at[slot]).start()

        @pl.when(u < NCH)
        def _():
            late(u).step()

        return carry

    U = NB * HL
    lax.fori_loop(0, U, attend, 0)
    for slot in range(2):
        pltpu.make_async_copy(resb.at[slot], res_o.at[0], ress.at[slot]).wait()

    def hop1(tag, m, j):
        return send(s1.at[m, j], r1.at[tag // 2, m, j], s1s.at[tag, m, j], s1r.at[tag, m, j], me.sib)

    def hop2(tag, m, j):
        return send(s2.at[m, j], r2.at[tag, m, j], s2s.at[tag, m, j], s2r.at[tag, m, j], me.xpeer)

    def block(b):
        return pl.ds(pl.multiple_of(b * CB, BLK), CB)

    def first_hop(tag, m, partial):
        for j in range(2):
            s1[m, j] = partial((1 - c) + 2 * j).astype(BF)
            hop1(tag, m, j).start()
        for j in range(2):
            acc[m, j] = partial(c + 2 * j)

    def second_hop(tag, m):
        for j in range(2):
            hop1(tag, m, j).wait()
            s2[m, j] = (acc[m, j] + r1[tag // 2, m, j].astype(F32)).astype(BF)
            hop2(tag, m, j).start()

    def total(tag, m, j):
        return s2[m, j].astype(F32) + r2[tag, m, j].astype(F32)

    def third(tag, full, m, b):
        part = full.at[m * BUF : (m + 1) * BUF, block(b)]
        return send(part, part, s3s.at[tag, m, lax.div(b, 2)], s3r.at[tag, m, lax.div(b, 2)], me.sib)

    def wait_third(tag, full, m):
        for j in range(2):
            third(tag, full, m, (1 - c) + 2 * j).wait_recv()
            third(tag, full, m, c + 2 * j).wait_send()

    def rows_of(m):
        return slice(m * BUF, (m + 1) * BUF)

    def branch(m):
        return lambda b: nt(mix[rows_of(m), :], WB[block(b), 0:HD])

    GC, UC, DC = HD, HD + FL, HD + 2 * FL
    late(0).finish()
    for m in range(NB):
        first_hop(0, m, branch(m))
    rest = list(range(min(U, NCH), NCH))
    half = (len(rest) + 1) // 2
    for i in rest[:half]:
        late(i).step()
    for m in range(NB):
        second_hop(0, m)
    for i in rest[half:]:
        late(i).step()

    def residual(m):
        for j in range(2):
            hop2(0, m, j).wait()
            b = c + 2 * j
            hidden = tokf[rows_of(m), block(b)].astype(F32) + total(0, m, j)
            hlow[rows_of(m), block(b)] = hidden.astype(BF)
            third(0, hlow, m, b).start()
        hidown[rows_of(m), :] = tokf[rows_of(m), own_cols].astype(F32) + (
            s2[m, me.x].astype(F32) + r2[0, m, me.x].astype(F32)
        )

    for m in range(NB):
        residual(m)
    for m in range(NB):
        wait_third(0, hlow, m)
        norm(hlow, n2, 8, m * BUF)
    for copy in hid[2]:
        copy.wait()

    def finish_late(i, carry):
        late(i).finish()
        return carry

    lax.fori_loop(1, NCH, finish_late, 0)
    NT = 256

    def ffn(m):
        def body(n, carry):
            at = pl.multiple_of(n * NT, NT)
            gate = nn(n2[rows_of(m), :], WB[:, pl.ds(pl.multiple_of(GC + at, BLK), NT)])
            up = nn(n2[rows_of(m), :], WB[:, pl.ds(pl.multiple_of(UC + at, BLK), NT)])
            back = nn(cotf[rows_of(m), :], WB[:, pl.ds(pl.multiple_of(DC + at, BLK), NT)])
            sig = jax.nn.sigmoid(gate)
            silu = gate * sig
            cols = pl.ds(at, NT)
            act[rows_of(m), cols] = (silu * up).astype(BF)
            gg[rows_of(m), cols] = (back * up * sig * (1.0 + gate * (1.0 - sig))).astype(BF)
            ug[rows_of(m), cols] = (back * silu).astype(BF)
            return carry

        lax.fori_loop(0, FL // NT, body, 0)

    def normed_back(m):
        return lambda b: nt(gg[rows_of(m), :], WB[block(b), GC : GC + FL]) + nt(
            ug[rows_of(m), :], WB[block(b), UC : UC + FL]
        )

    def down(m):
        return lambda b: nt(act[rows_of(m), :], WB[block(b), DC : DC + FL])

    for m in range(NB):
        ffn(m)
        first_hop(1, m, normed_back(m))
    for m in range(NB):
        second_hop(1, m)

    def staged(i, col, width):
        return pltpu.make_async_copy(
            stage.at[i, :, pl.ds(0, width)],
            g_o.at[pl.ds(pl.multiple_of(i * CB, BLK), CB), pl.ds(col, width)],
            stages.at[i],
        )

    busy = []

    def weight_term(left, right, col, width):
        before = busy[-1] if busy else None

        def body(i, carry):
            if before is not None:
                staged(i, *before).wait()
            stage[i, :, pl.ds(0, width)] = tn(left[:, pl.ds(pl.multiple_of(i * CB, BLK), CB)], right[...]).astype(BF)
            staged(i, col, width).start()
            return carry

        lax.fori_loop(0, D // CB, body, 0)
        busy.append((col, width))

    weight_term(cotf, act, DC, FL)

    def spread_back(m):
        for j in range(2):
            hop2(1, m, j).wait()
            b = c + 2 * j
            ng[rows_of(m), block(b)] = total(1, m, j).astype(BF)
            third(1, ng, m, b).start()

    def hop2_out(m):
        return send(t2.at[m], q2.at[m], s2s.at[2, m, 0], s2r.at[2, m, 0], me.xpeer)

    for m in range(NB):
        first_hop(2, m, down(m))
    for m in range(NB):
        spread_back(m)
    for m in range(NB):
        for j in range(2):
            hop1(2, m, j).wait()
        other = 1 - me.x
        t2[m] = (acc[m, other] + r1[1, m, other].astype(F32)).astype(BF)
        hop2_out(m).start()
    weight_term(n2, gg, GC, FL)
    gain2[...] = jnp.zeros_like(gain2)

    def branch_back(m):
        def body(i, carry):
            rows = spans(m * BUF + i * RB, RB)
            low = hlow[rows, :].astype(F32)
            scale = lax.rsqrt(jnp.mean(low * low, axis=1, keepdims=True) + EPSILON)
            scaled = ng[rows, :].astype(F32) * gf[8:9, :]
            row_total = jnp.sum(low * scaled, axis=1, keepdims=True)
            cube = scale * scale * scale * row_total / D
            low_own = hlow[rows, own_cols].astype(F32)
            ng_own = ng[rows, own_cols].astype(F32)
            hgrad[rows, :] = (
                cotf[rows, own_cols].astype(F32) + scale * gf[8:9, own_cols] * ng_own - low_own * cube
            )
            gain2[...] += jnp.broadcast_to(jnp.sum(low_own * scale * ng_own, axis=0, keepdims=True), gain2.shape)
            ng[rows, :] = (cotf[rows, :].astype(F32) + scale * scaled - low * cube).astype(BF)
            return carry

        lax.fori_loop(0, BUF // RB, body, 0)
        made = nn(ng[rows_of(m), :], WB[:, 0:HD])
        for hd in range(HL):
            mgrad[m * HL + hd] = made[:, hd * BLK : (hd + 1) * BLK].astype(BF)

    for m in range(NB):
        wait_third(1, ng, m)
        branch_back(m)
    weight_term(n2, ug, UC, FL)
    weight_term(ng, mix, 0, HD)
    for m in range(NB):
        hop2_out(m).wait()
        layer_out[rows_of(m), :] = (
            hidown[rows_of(m), :] + (acc[m, me.x] + r1[1, m, me.x].astype(F32) + q2[m].astype(F32))
        ).astype(BF)

    def last_stage(i, carry):
        staged(i, *busy[-1]).wait()
        return carry

    lax.fori_loop(0, D // CB, last_stage, 0)
    for copy in outputs:
        copy.wait()
    for g in first:
        g.drain()

    def drain_late(i, carry):
        late(i).drain()
        return carry

    lax.fori_loop(0, NCH, drain_late, 0)


def backward_kernel(
    cfg, tok_i, n1_i, gf, wa_i, q_i, k_i, v_i, h_i, hraw_i, beta, mgrad_i, res_i, g_i, hgrad, gain2,
    oA, oF, tgrad, one, two,
    tokf, n1, WA, qs, ks, vs, hs, hraw, mgrad, resb, dA, dbeta, ga, ry, gm, zr, rya, zra,
    s1, r1, acc, t2, q2, rts, rtr, rt, gbuf,
    local, ress, gms, sys, syr, szs, szr, ays, ayr, azs, azr, s1s, s1r, s2s, s2r, rs_s, rs_r, gs_s, gs_r,
):
    me = Place(cfg["names"], cfg["sizes"])
    T, D, CB, HL, HD, FL, RS = (cfg[k] for k in ("T", "D", "CB", "HL", "HD", "FL", "RS"))
    NCH = (HD + 3 * FL) // HD
    NB, U = T // BUF, T // BUF * HL
    DR = RS * me.wid
    c = me.c
    own_cols = pl.ds(pl.multiple_of(me.h * CB, BLK), CB)
    me.greet(me.group() + [me.hid_peer(k) for k in range(1, 4)])

    def dp_rows(j):
        return pl.ds(pl.multiple_of(lax.rem(me.d + j, me.dp) * DR, 16), DR)

    def late_cols(i):
        return pl.ds(pl.multiple_of(i * HD, BLK), HD)

    def late_y(i, j):
        return send(
            g_i.at[dp_rows(j), late_cols(i)], ry.at[i, j - 1], sys.at[i, j - 1], syr.at[i, j - 1], me.dp_peer(j)
        )

    def send_late(i, carry):
        for j in range(1, me.dp):
            late_y(i, j).start()
        return carry

    lax.fori_loop(0, NCH, send_late, 0)
    loads = [
        pltpu.make_async_copy(src, dst, local.at[i])
        for i, (src, dst) in enumerate(
            ((q_i, qs), (k_i, ks), (v_i, vs), (h_i, hs), (hraw_i, hraw), (mgrad_i, mgrad), (n1_i, n1), (tok_i, tokf))
        )
    ]
    loads.append(pltpu.make_async_copy(wa_i, WA, local.at[8]))

    def fetch_res(u):
        slot = lax.rem(u, 2)
        return pltpu.make_async_copy(res_i.at[u], resb.at[slot], ress.at[slot])

    def fetch_mine(i):
        slot = lax.rem(i, 2)
        return pltpu.make_async_copy(g_i.at[dp_rows(0), late_cols(i)], gm.at[slot], gms.at[slot])

    fetch_res(0).start()
    for copy in loads:
        copy.start()
    fetch_mine(0).start()
    for copy in loads[:6]:
        copy.wait()
    dbeta[...] = jnp.zeros_like(dbeta)

    def mine_of(o):
        return pl.ds(pl.multiple_of(o * RS, 16), RS)

    def late_z(i, k):
        o = lax.rem(me.w + k, me.wid)
        return send(ry.at[i, 0, mine_of(o), :], zr.at[i, k - 1], szs.at[i, k - 1], szr.at[i, k - 1], me.wid_peer(k))

    def late_stage(i):
        slot = lax.rem(i, 2)
        fetch_mine(i).wait()

        @pl.when(i + 1 < NCH)
        def _():
            fetch_mine(i + 1).start()

        for j in range(1, me.dp):
            late_y(i, j).wait_recv()
        for k in list(range(1, me.wid)) + [0]:
            rows = mine_of(lax.rem(me.w + k, me.wid))
            total = gm[slot, rows, :].astype(F32)
            for j in range(1, me.dp):
                total = total + ry[i, j - 1, rows, :].astype(F32)
            ry[i, 0, rows, :] = total.astype(BF)
            if k > 0:
                late_z(i, k).start()

    def attend_back(u, carry):
        m, hd = lax.div(u, HL), lax.rem(u, HL)
        slot = lax.rem(u, 2)
        parts = [slice(a * BLK, (a + 1) * BLK) for a in range(3)]
        fetch_res(u).wait()

        @pl.when(u + 1 < U)
        def _():
            fetch_res(u + 1).start()

        dq, dk, dv, dh, db = bwd_unit(
            [qs[u, p, :] for p in parts], [ks[u, p, :] for p in parts], [vs[u, p, :] for p in parts],
            [hs[u, p, :] for p in parts], [mgrad[u, p, :] for p in parts], [resb[slot, i] for i in range(NRES)],
        )
        for a in range(3):
            rows = spans(m * BUF + a * BLK, BLK)
            for n, value in enumerate((dq[a], dk[a], dv[a])):
                dA[rows, pl.ds(pl.multiple_of(n * HD + hd * BLK, BLK), BLK)] = value.astype(BF)
            raw = hraw[u, parts[a], :]
            scale = lax.rsqrt(jnp.sum(raw * raw, axis=1, keepdims=True) + EPSILON)
            along = jnp.sum(raw * dh[a], axis=1, keepdims=True)
            dA[rows, pl.ds(pl.multiple_of(3 * HD + hd * BLK, BLK), BLK)] = (
                scale * dh[a] - raw * (scale * scale * scale * along)
            ).astype(BF)
            strength = column(beta[rows, :], hd)
            pull = db[a] * (1.0 / jnp.maximum(strength, 1e-30) - 0.5)
            lanes = lax.broadcasted_iota(jnp.int32, (BLK, BLK), 1)
            dbeta[rows, :] += jnp.where(lanes == hd, pull, 0.0)

        @pl.when(u < NCH)
        def _():
            late_stage(u)

        return carry

    lax.fori_loop(0, U, attend_back, 0)
    dA[:, 4 * HD :] = dbeta[...].astype(BF)
    for copy in loads[6:]:
        copy.wait()

    bounds = [(a * HD, HD + (BLK if a == 3 else 0)) for a in range(4)]

    def first_y(a, j):
        col, width = bounds[a]
        return send(
            ga.at[dp_rows(j), pl.ds(col, width)], rya.at[j - 1, :, pl.ds(col, width)],
            ays.at[a, j - 1], ayr.at[a, j - 1], me.dp_peer(j),
        )

    whole = DR % CB == 0
    for a, (col, width) in enumerate(bounds):
        for j in list(range(1, me.dp)) + [0]:
            if whole:
                for i in range(DR // CB):
                    at = pl.multiple_of(lax.rem(me.d + j, me.dp) * DR + i * CB, BLK)
                    ga[pl.ds(at, CB), col : col + width] = tn(n1[:, pl.ds(at, CB)], dA[:, col : col + width]).astype(BF)
            elif j == min(1, me.dp - 1):
                for i in range(D // CB):
                    at = slice(i * CB, (i + 1) * CB)
                    ga[at, col : col + width] = tn(n1[:, at], dA[:, col : col + width]).astype(BF)
            if j > 0:
                first_y(a, j).start()

    def block(b):
        return pl.ds(pl.multiple_of(b * CB, BLK), CB)

    def hop1(j):
        return send(s1.at[j], r1.at[j], s1s.at[j], s1r.at[j], me.sib)

    hop2 = send(t2, q2, s2s, s2r, me.xpeer)
    rt[...] = jnp.zeros_like(rt)

    def partial(b, m):
        rows = slice(m * BUF, (m + 1) * BUF)
        made = nt(dA[rows, :], WA[block(b), :])
        along = jnp.sum(made * tokf[rows, block(b)].astype(F32) * gf[0:1, block(b)], axis=1, keepdims=True)
        rt[rows, :] += jnp.broadcast_to(along, (BUF, BLK))
        return made

    for j in range(2):
        for m in range(NB):
            s1[j, m * BUF : (m + 1) * BUF, :] = partial((1 - c) + 2 * j, m).astype(BF)
        hop1(j).start()
    for j in range(2):
        for m in range(NB):
            acc[j, m * BUF : (m + 1) * BUF, :] = partial(c + 2 * j, m)
    for i in range(T // BLK):
        rts[:, i * BLK : (i + 1) * BLK] = rt[i * BLK : (i + 1) * BLK, :].T[0:8, :]
    rt_copies = [send(rts, rtr.at[k - 1], rs_s.at[k - 1], rs_r.at[k - 1], me.hid_peer(k)) for k in range(1, 4)]
    for copy in rt_copies:
        copy.start()
    for j in range(2):
        hop1(j).wait()
    other = 1 - me.x
    t2[...] = (acc[other] + r1[other].astype(F32)).astype(BF)
    hop2.start()
    for i in range(min(U, NCH), NCH):
        late_stage(jnp.int32(i))
    hop2.wait()
    for copy in rt_copies:
        copy.wait()
    slot = me.d * me.wid + me.w
    gbuf[slot] = jnp.concatenate([jnp.zeros_like(gain2), gain2[...]], axis=0)

    def token_rows(i, carry):
        rows = spans(i * BLK, BLK)
        lane = rts[0:1, rows] + rtr[0, 0:1, rows] + rtr[1, 0:1, rows] + rtr[2, 0:1, rows]
        row_total = jnp.broadcast_to(lane, (BLK, BLK)).T[:, 0:1]
        wide = tokf[rows, :].astype(F32)
        scale = lax.rsqrt(jnp.mean(wide * wide, axis=1, keepdims=True) + EPSILON)
        made = acc[me.x, rows, :] + r1[me.x, rows, :].astype(F32) + q2[rows, :].astype(F32)
        own = tokf[rows, own_cols].astype(F32)
        back = scale * gf[0:1, own_cols] * made - own * (scale * scale * scale * row_total / D)
        tgrad[rows, :] = (hgrad[rows, :] + back).astype(BF)
        gbuf[slot, 0:8, :] += jnp.broadcast_to(jnp.sum(own * scale * made, axis=0, keepdims=True), (8, CB))
        return carry

    lax.fori_loop(0, T // BLK, token_rows, 0)
    gain_copies = []
    for n, peer in enumerate(me.group()):
        copy = send(gbuf.at[slot], gbuf.at[slot], gs_s.at[n], gs_r.at[n], peer)
        copy.start()
        gain_copies.append(copy)

    def first_z(a, k):
        col, width = bounds[a]
        o = lax.rem(me.w + k, me.wid)
        return send(
            rya.at[0, mine_of(o), pl.ds(col, width)], zra.at[k - 1, :, pl.ds(col, width)],
            azs.at[a, k - 1], azr.at[a, k - 1], me.wid_peer(k),
        )

    for a, (col, width) in enumerate(bounds):
        for j in range(1, me.dp):
            first_y(a, j).wait_recv()
        cols = slice(col, col + width)
        for k in list(range(1, me.wid)) + [0]:
            o = lax.rem(me.w + k, me.wid)
            rows = mine_of(o)
            total = ga[pl.ds(pl.multiple_of(me.d * DR + o * RS, 16), RS), cols].astype(F32)
            for j in range(1, me.dp):
                total = total + rya[j - 1, rows, cols].astype(F32)
            rya[0, rows, cols] = total.astype(BF)
            if k > 0:
                first_z(a, k).start()

    def late_sum(i, carry):
        total = ry[i, 0, mine_of(me.w), :].astype(F32)
        for k in range(1, me.wid):
            late_z(i, k).wait()
            total = total + zr[i, k - 1].astype(F32)
        oF[:, late_cols(i)] = total
        for j in range(1, me.dp):
            late_y(i, j).wait_send()
        return carry

    lax.fori_loop(0, NCH, late_sum, 0)
    for copy in gain_copies:
        copy.wait()
    both = gbuf[0]
    for n in range(1, me.dp * me.wid):
        both = both + gbuf[n]
    one[...] = both[0:1, :]
    two[...] = both[8:9, :]
    for a, (col, width) in enumerate(bounds):
        cols = slice(col, col + width)
        total = rya[0, mine_of(me.w), cols].astype(F32)
        for k in range(1, me.wid):
            first_z(a, k).wait()
            total = total + zra[k - 1, :, cols].astype(F32)
        oA[:, cols] = total
        for j in range(1, me.dp):
            first_y(a, j).wait_send()


def solution(mesh):
    names = tuple(mesh.axis_names)
    sizes = {n: mesh.shape[n] for n in names}
    dp, wid = sizes["dp"], sizes["wid"]
    assert sizes["hid"] == 4

    def shards(
        tokens, cotangent, lengths, keep, norm_one, w_query, w_key, w_value, w_house, w_beta, w_out, norm_two,
        w_gate, w_up, w_down,
    ):
        micro, rows, CB = tokens.shape
        T, D, HD, FL, RS = micro * rows, CB * 4, w_query.shape[1], w_gate.shape[1], w_query.shape[0]
        HL, NB = HD // BLK, T // BUF
        U, WAC, WBC = NB * HL, 4 * HD + BLK, HD + 3 * FL
        NCH, DR = WBC // HD, D // dp
        heads = w_beta.shape[1]
        cfg = dict(names=names, sizes=sizes, T=T, D=D, CB=CB, HL=HL, HD=HD, FL=FL, RS=RS)
        pack = jnp.concatenate(
            [w_query, w_key, w_value, w_house, jnp.pad(w_beta, ((0, 0), (0, BLK - heads))), w_out.T, w_gate, w_up,
             w_down.T], axis=1)
        gains = jnp.concatenate([jnp.broadcast_to(g, (8, CB)) for g in (norm_one, norm_two)], axis=0).astype(F32)
        sd = jax.ShapeDtypeStruct
        nch = 4 + NCH
        params = dict(has_side_effects=True, vmem_limit_bytes=62 << 20)
        unit = lambda t: sd((U, BUF, BLK), t)
        fwd = pl.pallas_call(
            functools.partial(forward_kernel, cfg),
            out_shape=(
                sd((T, CB), BF), sd((T, CB), F32), sd((8, CB), F32), unit(BF), unit(BF), unit(BF), unit(BF), unit(BF),
                unit(F32), sd((T, BLK), F32), sd((16, D), F32), sd((U, NRES, BLK, BLK), BF), sd((T, D), BF),
                sd((T, D), BF), sd((D, WAC), BF), sd((D, WBC), BF),
            ),
            in_specs=[SM, VM, ANY, ANY, ANY, ANY],
            out_specs=(VM,) * 11 + (ANY,) * 5,
            scratch_shapes=[
                pltpu.VMEM((D, WAC), BF), pltpu.VMEM((D, WBC), BF), pltpu.VMEM((T, D), BF), pltpu.VMEM((T, D), BF),
                pltpu.VMEM((T, D), BF), pltpu.VMEM((T, D), BF), pltpu.VMEM((T, D), BF), pltpu.VMEM((T, D), BF),
                pltpu.VMEM((T, HD), BF), pltpu.VMEM((T, FL), BF), pltpu.VMEM((T, FL), BF), pltpu.VMEM((T, FL), BF),
                pltpu.VMEM((2, NRES, BLK, BLK), BF),
                pltpu.VMEM((NB, 2, BUF, CB), BF), pltpu.VMEM((2, NB, 2, BUF, CB), BF),
                pltpu.VMEM((NB, 2, BUF, CB), BF), pltpu.VMEM((2, NB, 2, BUF, CB), BF),
                pltpu.VMEM((NB, 2, BUF, CB), F32),
                pltpu.VMEM((NB, BUF, CB), BF), pltpu.VMEM((NB, BUF, CB), BF),
                pltpu.VMEM((4, CB, max(FL, HD)), BF), pltpu.VMEM((T, CB), F32),
                DMA((5,)), DMA((3, 3)), DMA((3, 3)), DMA((nch, 2, wid)), DMA((nch, 2, wid)),
                DMA((nch, wid, max(dp - 1, 1))), DMA((nch, wid, max(dp - 1, 1))),
                DMA((3, NB, 2)), DMA((3, NB, 2)), DMA((3, NB, 2)), DMA((3, NB, 2)), DMA((2, NB, 2)), DMA((2, NB, 2)),
                DMA((3,)), DMA((2,)), DMA((4,)),
            ],
            compiler_params=pltpu.CompilerParams(collective_id=0, **params),
            name="forward",
        )
        (layer_out, hgrad, gain2, mgrad, qs, ks, vs, hs, hraw, beta, gf, res, n1, tokf, wa, g) = fwd(
            lengths.reshape(NB, lengths.shape[2]), keep.reshape(NB, 1, BUF), tokens.reshape(T, CB),
            cotangent.reshape(T, CB), gains, pack,
        )
        bwd = pl.pallas_call(
            functools.partial(backward_kernel, cfg),
            out_shape=(
                sd((RS, WAC), F32), sd((RS, WBC), F32), sd((T, CB), BF), sd((1, CB), F32), sd((1, CB), F32),
            ),
            in_specs=[ANY, ANY, VM, ANY] + [ANY] * 5 + [VM, ANY, ANY, ANY, VM, VM],
            out_specs=(VM,) * 5,
            scratch_shapes=[
                pltpu.VMEM((T, D), BF), pltpu.VMEM((T, D), BF), pltpu.VMEM((D, WAC), BF),
                *[pltpu.VMEM((U, BUF, BLK), BF)] * 4, pltpu.VMEM((U, BUF, BLK), F32), pltpu.VMEM((U, BUF, BLK), BF),
                pltpu.VMEM((2, NRES, BLK, BLK), BF), pltpu.VMEM((T, WAC), BF), pltpu.VMEM((T, BLK), F32),
                pltpu.VMEM((D, WAC), BF), pltpu.VMEM((NCH, dp - 1, DR, HD), BF), pltpu.VMEM((2, DR, HD), BF),
                pltpu.VMEM((NCH, wid - 1, RS, HD), BF), pltpu.VMEM((dp - 1, DR, WAC), BF),
                pltpu.VMEM((wid - 1, RS, WAC), BF),
                pltpu.VMEM((2, T, CB), BF), pltpu.VMEM((2, T, CB), BF), pltpu.VMEM((2, T, CB), F32),
                pltpu.VMEM((T, CB), BF), pltpu.VMEM((T, CB), BF),
                pltpu.VMEM((8, T), F32), pltpu.VMEM((3, 8, T), F32), pltpu.VMEM((T, BLK), F32),
                pltpu.VMEM((dp * wid, 16, CB), F32),
                DMA((9,)), DMA((2,)), DMA((2,)), DMA((NCH, dp - 1)), DMA((NCH, dp - 1)), DMA((NCH, wid - 1)),
                DMA((NCH, wid - 1)), DMA((4, dp - 1)), DMA((4, dp - 1)), DMA((4, wid - 1)), DMA((4, wid - 1)),
                DMA((2,)), DMA((2,)), DMA, DMA, DMA((3,)), DMA((3,)), DMA((dp * wid - 1,)), DMA((dp * wid - 1,)),
            ],
            compiler_params=pltpu.CompilerParams(collective_id=1, **params),
            name="backward",
        )
        oA, oF, tgrad, one, two = bwd(tokf, n1, gf, wa, qs, ks, vs, hs, hraw, beta, mgrad, res, g, hgrad, gain2)
        cut = lambda i: oA[:, i * HD : (i + 1) * HD]
        return (
            layer_out.reshape(tokens.shape), tgrad.reshape(tokens.shape), one, cut(0), cut(1), cut(2), cut(3),
            oA[:, 4 * HD : 4 * HD + heads], oF[:, :HD].T, two, oF[:, HD : HD + FL], oF[:, HD + FL : HD + 2 * FL],
            oF[:, HD + 2 * FL :].T,
        )

    rows = P(("dp", "wid"), "hid")
    cols = P("hid", ("dp", "wid"))
    wide = P(None, ("dp", "wid"), "hid")
    gain = P(None, "hid")
    return jax.shard_map(
        shards,
        mesh=mesh,
        in_specs=(
            wide, wide, P(None, ("dp", "wid"), None), P(None, ("dp", "wid")), gain, rows, rows, rows, rows, rows,
            cols, gain, rows, rows, cols,
        ),
        out_specs=(wide, wide, gain, rows, rows, rows, rows, rows, cols, gain, rows, rows, cols),
        check_vma=False,
    )
```

```python
import functools
import math

import jax
import jax.numpy as jnp
from jax import lax
from jax.experimental import pallas as pl
from jax.experimental.pallas import tpu as pltpu
from jax.sharding import PartitionSpec as P

BLK = 128
BUF = 384
EPSILON = 1e-06
F32 = jnp.float32
BF = jnp.bfloat16
MESH = pl.DeviceIdType.MESH
ANY = pl.BlockSpec(memory_space=pl.ANY)
VM = pl.BlockSpec(memory_space=pltpu.VMEM)
SM = pl.BlockSpec(memory_space=pltpu.SMEM)
DMA = pltpu.SemaphoreType.DMA
NRES = 30


def _dot(a,b,ca,cb): return lax.dot_general(a,b,(((ca,),(cb,)),((),())),preferred_element_type=F32)
def nn(a,b): return _dot(a.astype(BF),b.astype(BF),1,0)
def nt(a,b): return _dot(a.astype(BF),b.astype(BF),1,1)
def tn(a,b): return _dot(a.astype(BF),b.astype(BF),0,0)
def split(a):
    hi=a.astype(BF); return hi,(a-hi.astype(F32)).astype(BF)
def nn3(a,b):
    ah,al=split(a); bh,bl=split(b)
    return _dot(ah,bh,1,0)+(_dot(ah,bl,1,0)+_dot(al,bh,1,0))
INV=nn3
def iotas():
    return lax.broadcasted_iota(jnp.int32,(BLK,BLK),0), lax.broadcasted_iota(jnp.int32,(BLK,BLK),1)
def tri_inverse(inner, beta_col, row, col):
    diag=jnp.where(row==col, beta_col, 0.0)
    beta_lane=jnp.sum(diag,axis=0,keepdims=True)
    first=((row>>1)==(col>>1))&(row>col)
    x=diag-jnp.where(first, inner*beta_col*beta_lane, 0.0)
    lb=1
    while (1<<lb)<BLK:
        m=((row>>(lb+1))==(col>>(lb+1)))&((row>>lb)>(col>>lb))
        low=jnp.where(m,inner,0.0)
        x=x-INV(INV(x,low),x)
        lb+=1
    return x
def masks(a,c,e0,e1,keep_row,row,col):
    qp=row+BLK*a; kp=col+BLK*c
    segq=(qp>=e0).astype(jnp.int32)+(qp>=e1).astype(jnp.int32)
    segk=(kp>=e0).astype(jnp.int32)+(kp>=e1).astype(jnp.int32)
    ok=(segq==segk)
    if a==c: return ok&(row>=col)&((keep_row==1)|(row==col))
    return ok&(keep_row==1)
def fwd_unit(q,k,v,h,beta,keep,e0,e1):
    nb=len(q); row,col=iotas(); le=row>=col; st=row>col
    X,A1,L,W,R,Qm,Km=[],[],[],[],[],[],[]
    for a in range(nb):
        x=tri_inverse(nt(h[a],h[a]),beta[a],row,col).astype(BF)
        a1=jnp.where(le,nt(q[a],h[a]),0.0).astype(BF)
        w=jnp.where(st,nt(h[a],k[a]),0.0).astype(BF)
        l=nn(a1,x).astype(BF); r=nn(x,w).astype(BF)
        X.append(x);A1.append(a1);W.append(w);L.append(l);R.append(r)
        Qm.append((q[a].astype(F32)-nn(l,h[a])).astype(BF))
        Km.append((k[a].astype(F32)-tn(r,h[a])).astype(BF))
    scale=1.0/math.sqrt(BLK)
    S={}
    for a in range(nb):
        S[a,a]=nt(q[a],k[a])-nn(L[a],W[a])
    S[1,0]=nt(Qm[1],Km[0]); S[2,1]=nt(Qm[2],Km[1])
    u=nt(Qm[2],h[1]).astype(BF); ux=nn(u,X[1]).astype(BF)
    cq=(Qm[2].astype(F32)-nn(ux,h[1])).astype(BF)
    S[2,0]=nt(cq,Km[0])
    P={}; out=[]
    for a in range(nb):
        sc={c:jnp.where(masks(a,c,e0,e1,keep[c],row,col),S[a,c]*scale,-1e30) for c in range(a+1)}
        top=jnp.max(sc[0],axis=1,keepdims=True)
        for c in range(1,a+1): top=jnp.maximum(top,jnp.max(sc[c],axis=1,keepdims=True))
        ex={c:jnp.exp(sc[c]-top) for c in sc}
        tot=sum(jnp.sum(e,axis=1,keepdims=True) for e in ex.values())
        inv=1.0/tot
        o=0.0
        for c in sc:
            P[a,c]=(ex[c]*inv).astype(BF); o=o+nn(P[a,c],v[c])
        out.append(o)
    res=X+A1+L+W+R+Qm+Km+[u,ux,cq]+[P[0,0],P[1,0],P[1,1],P[2,0],P[2,1],P[2,2]]
    return out,res
def bwd_unit(q,k,v,h,do,res):
    nb=3; row,col=iotas(); le=row>=col; st=row>col
    X,A1,L,W,R,Qm,Km=[res[3*i:3*i+3] for i in range(7)]
    u,ux,cq=res[21:24]; pl_=res[24:30]
    P={(0,0):pl_[0],(1,0):pl_[1],(1,1):pl_[2],(2,0):pl_[3],(2,1):pl_[4],(2,2):pl_[5]}
    scale=1.0/math.sqrt(BLK)
    G={}; dv=[0.0]*nb
    for a in range(nb):
        dp={c:nt(do[a],v[c]) for c in range(a+1)}
        delta=sum(jnp.sum(P[a,c].astype(F32)*dp[c],axis=1,keepdims=True) for c in range(a+1))
        for c in range(a+1):
            G[a,c]=(P[a,c].astype(F32)*(dp[c]-delta)*scale).astype(BF)
            dv[c]=dv[c]+tn(P[a,c],do[a])
    dq=[nn(G[a,a],k[a]) for a in range(nb)]
    dk=[tn(G[a,a],q[a]) for a in range(nb)]
    dL=[-nt(G[a,a],W[a]) for a in range(nb)]
    dW=[-tn(L[a],G[a,a]) for a in range(nb)]
    dh=[0.0]*nb; dX=[0.0]*nb
    dcq=nn(G[2,0],Km[0]).astype(BF)
    dQm=[None, nn(G[1,0],Km[0]), nn(G[2,1],Km[1])+dcq.astype(F32)]
    dKm=[tn(G[1,0],Qm[1])+tn(G[2,0],cq), tn(G[2,1],Qm[2]), None]
    dux=(-nt(dcq,h[1])).astype(BF)
    dh[1]=dh[1]-tn(ux,dcq)
    du=nt(dux,X[1]).astype(BF)
    dX[1]=dX[1]+tn(u,dux)
    dQm[2]=dQm[2]+nn(du,h[1])
    dh[1]=dh[1]+tn(du,Qm[2])
    dbeta=[]
    for a in range(nb):
        if dQm[a] is not None:
            d_=dQm[a].astype(BF)
            dq[a]=dq[a]+d_.astype(F32); dL[a]=dL[a]-nt(d_,h[a]); dh[a]=dh[a]-tn(L[a],d_)
        if dKm[a] is not None:
            d_=dKm[a].astype(BF)
            dk[a]=dk[a]+d_.astype(F32); dR=(-nt(h[a],d_)).astype(BF); dh[a]=dh[a]-nn(R[a],d_)
            dX[a]=dX[a]+nt(dR,W[a]); dW[a]=dW[a]+tn(X[a],dR)
        dl=dL[a].astype(BF)
        dA=jnp.where(le,nt(dl,X[a]),0.0).astype(BF)
        dX[a]=dX[a]+tn(A1[a],dl)
        dw=jnp.where(st,dW[a],0.0).astype(BF)
        dh[a]=dh[a]+nn(dw,k[a]); dk[a]=dk[a]+tn(dw,h[a])
        dq[a]=dq[a]+nn(dA,h[a]); dh[a]=dh[a]+tn(dA,q[a])
        dM=nt(tn(X[a],dX[a]),X[a])
        dn=jnp.where(st,-dM,0.0).astype(BF)
        dh[a]=dh[a]+nn(dn,h[a])+tn(dn,h[a])
        dbeta.append(jnp.sum(jnp.where(row==col,dM,0.0),axis=1,keepdims=True))
    return dq,dk,dv,dh,dbeta


def spans(rows, step):
    return pl.ds(pl.multiple_of(rows, step), step)


class Place:
    def __init__(self, names, sizes):
        self.names, self.sizes = names, sizes
        self.d, self.h, self.w = (lax.axis_index(n) for n in ("dp", "hid", "wid"))
        self.dp, self.wid = sizes["dp"], sizes["wid"]
        self.c = lax.rem(self.h, 2)
        self.x = lax.div(self.h, 2)
        self.sib = self.at(h=self.h + 1 - 2 * self.c)
        self.xpeer = self.at(h=lax.rem(self.h + 2, 4))

    def at(self, d=None, h=None, w=None):
        where = {"dp": self.d if d is None else d, "hid": self.h if h is None else h, "wid": self.w if w is None else w}
        return tuple(where[n] for n in self.names)

    def greet(self, peers):
        barrier = pltpu.get_barrier_semaphore()
        for peer in peers:
            pl.semaphore_signal(barrier, inc=1, device_id=peer, device_id_type=MESH)
        pl.semaphore_wait(barrier, len(peers))

    def dp_peer(self, j):
        return self.at(d=lax.rem(self.d + j, self.dp))

    def wid_peer(self, k):
        return self.at(w=lax.rem(self.w + k, self.wid))

    def hid_peer(self, k):
        return self.at(h=lax.rem(self.h + k, 4))

    def group(self):
        return [
            self.at(d=lax.rem(self.d + i, self.dp), w=lax.rem(self.w + k, self.wid))
            for i in range(self.dp)
            for k in range(self.wid)
            if i + k > 0
        ]


def send(src, dst, sent, got, peer):
    return pltpu.make_async_remote_copy(
        src_ref=src, dst_ref=dst, send_sem=sent, recv_sem=got, device_id=peer, device_id_type=MESH
    )


class Gather:
    def __init__(self, me, rows, full, col, width, ch, sz, rz, sy, ry):
        self.me, self.rows, self.full, self.ch = me, rows, full, ch
        self.col, self.width = col, width
        self.sz, self.rz, self.sy, self.ry = sz, rz, sy, ry

    def piece(self, d, o):
        return self.full.at[
            pl.ds(pl.multiple_of((d * self.me.wid + o) * self.rows, 16), self.rows), pl.ds(self.col, self.width)
        ]

    def origin(self, way, hop):
        return lax.clamp(0, self.me.w - way * hop, self.me.wid - 1)

    def zcopy(self, way, hop, sem):
        me, side = self.me, (way + 1) // 2
        part = self.piece(me.d, self.origin(way, hop))
        return send(
            part, part, self.sz.at[self.ch, side, sem], self.rz.at[self.ch, side, sem],
            me.at(w=lax.clamp(0, me.w + way, me.wid - 1)),
        )

    def ycopy(self, d, o, j):
        part = self.piece(d, o)
        return send(part, part, self.sy.at[self.ch, o, j - 1], self.ry.at[self.ch, o, j - 1], self.me.dp_peer(j))

    def has_next(self, way):
        return self.me.w < self.me.wid - 1 if way == 1 else self.me.w > 0

    def has_piece(self, way, hop):
        return self.me.w - hop >= 0 if way == 1 else self.me.w + hop < self.me.wid

    def start_z(self):
        for way in (1, -1):

            @pl.when(self.has_next(way))
            def _():
                self.zcopy(way, 0, 0).start()

    def start_y(self):
        for j in range(1, self.me.dp):
            self.ycopy(self.me.d, self.me.w, j).start()

    def hop(self, hop):
        me = self.me
        for way in (1, -1):

            @pl.when(self.has_piece(way, hop))
            def _():
                self.zcopy(way, hop, hop - 1).wait_recv()

                @pl.when(self.has_next(way))
                def _():
                    self.zcopy(way, hop, hop).start()

                for j in range(1, me.dp):
                    self.ycopy(me.d, self.origin(way, hop), j).start()

    def finish(self):
        me = self.me
        for j in range(1, me.dp):
            for o in range(me.wid):
                self.ycopy(lax.rem(me.d + me.dp - j, me.dp), o, j).wait_recv()

    def drain(self):
        me = self.me
        for way in (1, -1):
            for hop in range(me.wid):

                @pl.when(self.has_piece(way, hop) & self.has_next(way))
                def _():
                    self.zcopy(way, hop, hop).wait_send()

        for j in range(1, me.dp):
            for o in range(me.wid):
                self.ycopy(me.d, o, j).wait_send()


def column(values, lane_index):
    lanes = lax.broadcasted_iota(jnp.int32, values.shape, 1)
    return jnp.sum(jnp.where(lanes == lane_index, values, 0.0), axis=1, keepdims=True)


def layer_kernel(
    cfg, lens, keep, tok, cot, gains, w_q, w_k, w_v, w_h, w_b, w_o, w_g, w_u, w_d,
    layer_out, tgrad, one, two, o_q, o_k, o_v, o_h, o_b, o_o, o_g, o_u, o_d, g_h, ry_h, z_h, res_h,
    W, tokf, cotf, n1, n2, hlow, ng, mix, act, gg, ug, qs, ks, vs, hs, hraw, mgrad, beta, dbeta, dB, gf, resb,
    s1, r1, s2, r2, acc, t2, q2, hidown, hgrad, stage, outv, rts, rtr, rt, gbuf,
    local, own, hx_s, hx_r, sz, rz, sy, ry, s1s, s1r, s2s, s2r, s3s, s3r, ress, stages,
    ys, yr, zs, zr, zo, ld, outs, rs_s, rs_r, gs_s, gs_r,
):
    me = Place(cfg["names"], cfg["sizes"])
    T, D, CB, HL, HD, FL, RS = (cfg[k] for k in ("T", "D", "CB", "HL", "HD", "FL", "RS"))
    FW = cfg["FW"]
    NF = 3 * FL // FW
    FB = 5 * HD
    BC = FB + 3 * FL
    GC, UC, DC, OC = FB, FB + FL, FB + 2 * FL, 4 * HD
    NB, U, DR = T // BUF, T // BUF * HL, RS * me.wid
    c = me.c
    own_cols = pl.ds(pl.multiple_of(me.h * CB, BLK), CB)
    own_rows = pl.ds(pl.multiple_of((me.d * me.wid + me.w) * RS, 16), RS)
    me.greet(me.group() + [me.hid_peer(k) for k in range(1, 4)])

    places = [(w_q, 0), (w_k, HD), (w_v, 2 * HD), (w_h, 3 * HD), (w_b, BC), (w_o, OC), (w_g, GC), (w_u, UC), (w_d, DC)]
    mine = [
        pltpu.make_async_copy(ref, W.at[own_rows, pl.ds(col, ref.shape[1])], own.at[i])
        for i, (ref, col) in enumerate(places)
    ]
    hid = []
    for i, (src, dst) in enumerate(((tok, tokf), (gains, gf), (cot, cotf))):
        here = pltpu.make_async_copy(src, dst.at[:, own_cols], local.at[i])
        away = [
            send(src, dst.at[:, own_cols], hx_s.at[i, k - 1], hx_r.at[i, k - 1], me.hid_peer(k)) for k in range(1, 4)
        ]
        hid.append([here] + away)
    for copy in mine[:6]:
        copy.start()
    for i in range(2):
        for copy in hid[i]:
            copy.start()
    for copy in mine[6:]:
        copy.start()
    sems = (sz, rz, sy, ry)
    first = [
        Gather(me, RS, W, col, ref.shape[1], i, *sems) for i, (ref, col) in enumerate(places[:6])
    ]

    def late(i):
        return Gather(me, RS, W, pl.multiple_of(FB + i * FW, BLK), FW, 6 + i, *sems)

    for i, g in enumerate(first):
        mine[i].wait()
        g.start_z()
        g.start_y()
    for copy in mine[6:]:
        copy.wait()

    def start_late(i, carry):
        late(i).start_z()
        late(i).start_y()
        return carry

    lax.fori_loop(0, NF, start_late, 0)
    for copy in hid[2]:
        copy.start()
    for i in range(2):
        for copy in hid[i]:
            copy.wait()
    RB = 32

    def rows_of(m):
        return pl.ds(pl.multiple_of(m * BUF, BLK), BUF)

    def norm(src, dst, gain, base):
        def body(i, carry):
            rows = spans(base + i * RB, RB)
            wide = src[rows, :].astype(F32)
            scale = lax.rsqrt(jnp.mean(wide * wide, axis=1, keepdims=True) + EPSILON)
            dst[rows, :] = (wide * scale * gf[gain : gain + 1, :]).astype(BF)
            return carry

        lax.fori_loop(0, BUF // RB, body, 0)

    for m in range(NB):
        norm(tokf, n1, 0, m * BUF)

    def project(a):
        for m in range(NB):
            rows = n1[m * BUF : (m + 1) * BUF, :]
            made = nn(rows, W[:, a * HD : (a + 1) * HD])
            for hd in range(HL):
                part = made[:, hd * BLK : (hd + 1) * BLK]
                u = m * HL + hd
                if a < 3:
                    (qs, ks, vs)[a][u] = part.astype(BF)
                else:
                    hraw[u] = part
                    hs[u] = (part * lax.rsqrt(jnp.sum(part * part, axis=1, keepdims=True) + EPSILON)).astype(BF)
            if a == 3:
                beta[m * BUF : (m + 1) * BUF, :] = 2.0 * jax.nn.sigmoid(nn(rows, W[:, BC:]))

    def tick(k):
        for hop in range(1, me.wid):
            if 0 <= k - hop + 1 < len(first):
                first[k - hop + 1].hop(hop)

    for k in range(len(first) + me.wid - 2):
        tick(k)
        if 2 <= k < 5:
            first[k - 2].finish()
            project(k - 2)
    first[3].finish()
    first[4].finish()
    project(3)

    def late_tick(k):
        for hop in range(1, me.wid):

            @pl.when((k >= hop - 1) & (k - hop + 1 < NF))
            def _():
                late(k - hop + 1).hop(hop)

    def attend(u, carry):
        m, hd = lax.div(u, HL), lax.rem(u, HL)
        slot = lax.rem(u, 2)
        e0 = lens[m, 0]
        e1 = e0 + lens[m, 1]
        parts = [slice(a * BLK, (a + 1) * BLK) for a in range(3)]
        strength = [column(beta[spans(m * BUF + a * BLK, BLK), :], hd) for a in range(3)]
        keys = [keep[m, :, p] for p in parts]
        late_tick(u)
        out, res = fwd_unit(
            [qs[u, p, :] for p in parts], [ks[u, p, :] for p in parts], [vs[u, p, :] for p in parts],
            [hs[u, p, :] for p in parts], strength, keys, e0, e1,
        )
        for a in range(3):
            mix[spans(m * BUF + a * BLK, BLK), pl.ds(pl.multiple_of(hd * BLK, BLK), BLK)] = out[a].astype(BF)

        @pl.when(u >= 2)
        def _():
            pltpu.make_async_copy(resb.at[slot], res_h.at[u], ress.at[slot]).wait()

        for i, value in enumerate(res):
            resb[slot, i] = value
        pltpu.make_async_copy(resb.at[slot], res_h.at[u], ress.at[slot]).start()
        return carry

    lax.fori_loop(0, U, attend, 0)
    for slot in range(2):
        pltpu.make_async_copy(resb.at[slot], res_h.at[0], ress.at[slot]).wait()

    def block(b):
        return pl.ds(pl.multiple_of(b * CB, BLK), CB)

    def hop1(tag, m, j):
        return send(s1.at[m, j], r1.at[tag % 3 // 2, m, j], s1s.at[tag, m, j], s1r.at[tag, m, j], me.sib)

    def hop2(tag, m, j):
        return send(s2.at[m, j], r2.at[tag, m, j], s2s.at[tag, m, j], s2r.at[tag, m, j], me.xpeer)

    def first_hop(tag, m, partial):
        for j in range(2):
            s1[m, j] = partial((1 - c) + 2 * j).astype(BF)
            hop1(tag, m, j).start()
        for j in range(2):
            acc[m, j] = partial(c + 2 * j)

    def second_hop(tag, m):
        for j in range(2):
            hop1(tag, m, j).wait()
            s2[m, j] = (acc[m, j] + r1[tag // 2, m, j].astype(F32)).astype(BF)
            hop2(tag, m, j).start()

    def total(tag, m, j):
        return s2[m, j].astype(F32) + r2[tag, m, j].astype(F32)

    def third(tag, full, m, j, core):
        part = full.at[rows_of(m), block(core + 2 * j)]
        return send(part, part, s3s.at[tag, m, j], s3r.at[tag, m, j], me.sib)

    def wait_third(tag, full, m):
        for j in range(2):
            third(tag, full, m, j, 1 - c).wait_recv()
            third(tag, full, m, j, c).wait_send()

    def branch(m):
        return lambda b: nt(mix[rows_of(m), :], W[block(b), OC : OC + HD])

    first[5].finish()
    for m in range(NB):
        first_hop(0, m, branch(m))

    def more(k, carry):
        late_tick(k)
        return carry

    lax.fori_loop(U, NF + me.wid - 2, more, 0)
    for m in range(NB):
        second_hop(0, m)

    def residual(m):
        for j in range(2):
            hop2(0, m, j).wait()
            b = c + 2 * j
            hidden = tokf[rows_of(m), block(b)].astype(F32) + total(0, m, j)
            hlow[rows_of(m), block(b)] = hidden.astype(BF)
            third(0, hlow, m, j, c).start()
        hidown[rows_of(m), :] = tokf[rows_of(m), own_cols].astype(F32) + (
            s2[m, me.x].astype(F32) + r2[0, m, me.x].astype(F32)
        )

    for m in range(NB):
        residual(m)
    for m in range(NB):
        wait_third(0, hlow, m)
        norm(hlow, n2, 8, m * BUF)
    for copy in hid[2]:
        copy.wait()

    def finish_late(i, carry):
        late(i).finish()
        return carry

    NT = 256
    ND = 2 * FL // FW
    lax.fori_loop(0, ND, finish_late, 0)

    def ffn(m):
        def body(n, carry):
            at = pl.multiple_of(n * NT, NT)
            gate = nn(n2[rows_of(m), :], W[:, pl.ds(pl.multiple_of(GC + at, BLK), NT)])
            up = nn(n2[rows_of(m), :], W[:, pl.ds(pl.multiple_of(UC + at, BLK), NT)])
            sig = jax.nn.sigmoid(gate)
            silu = gate * sig
            cols = pl.ds(at, NT)
            act[rows_of(m), cols] = (silu * up).astype(BF)
            gg[rows_of(m), cols] = (up * sig * (1.0 + gate * (1.0 - sig))).astype(BF)
            ug[rows_of(m), cols] = silu.astype(BF)
            return carry

        lax.fori_loop(0, FL // NT, body, 0)

    def ffn_back(m):
        def body(n, carry):
            at = pl.multiple_of(n * NT, NT)
            cols = pl.ds(at, NT)
            back = nn(cotf[rows_of(m), :], W[:, pl.ds(pl.multiple_of(DC + at, BLK), NT)])
            gg[rows_of(m), cols] = (back * gg[rows_of(m), cols].astype(F32)).astype(BF)
            ug[rows_of(m), cols] = (back * ug[rows_of(m), cols].astype(F32)).astype(BF)
            return carry

        lax.fori_loop(0, FL // NT, body, 0)

    def dp_rows(j):
        return pl.ds(pl.multiple_of(lax.rem(me.d + j, me.dp) * DR, 16), DR)

    def staged(side, i, col, width):
        return pltpu.make_async_copy(
            stage.at[side, i, :, pl.ds(0, width)],
            g_h.at[pl.ds(pl.multiple_of(i * CB, BLK), CB), pl.ds(col, width)],
            stages.at[side, i],
        )

    def rs_y(ch, col, width, j):
        return send(
            g_h.at[dp_rows(j), pl.ds(col, width)], ry_h.at[j - 1, :, pl.ds(col, width)],
            ys.at[ch, j - 1], yr.at[ch, j - 1], me.dp_peer(j),
        )

    pending = []
    made_terms = [0]

    def flush():
        side, ch, col, width = pending.pop()
        for i in range(D // CB):
            staged(side, i, col, width).wait()
        for j in range(1, me.dp):
            rs_y(ch, col, width, j).start()

    def weight_term(ch, left, right, at, col, width):
        side = made_terms[0] % 2
        made_terms[0] += 1

        def body(i, carry):
            stage[side, i, :, pl.ds(0, width)] = tn(
                left[:, pl.ds(pl.multiple_of(i * CB, BLK), CB)], right[:, at : at + width]
            ).astype(BF)
            staged(side, i, col, width).start()
            return carry

        lax.fori_loop(0, D // CB, body, 0)
        if pending:
            flush()
        pending.append((side, ch, col, width))

    def ffn_terms(left, right, col):
        for n in range(FL // FW):
            weight_term(6 + (col - FB) // FW + n, left, right, n * FW, col + n * FW, FW)

    for m in range(NB):
        ffn(m)
    ffn_terms(cotf, act, DC)
    flush()
    lax.fori_loop(ND, NF, finish_late, 0)

    def normed_back(m):
        return lambda b: nt(gg[rows_of(m), :], W[block(b), GC : GC + FL]) + nt(
            ug[rows_of(m), :], W[block(b), UC : UC + FL]
        )

    def down(m):
        return lambda b: nt(act[rows_of(m), :], W[block(b), DC : DC + FL])

    ffn_back(0)
    first_hop(1, 0, normed_back(0))
    ffn_back(1)
    second_hop(1, 0)
    for m in range(1, NB):
        first_hop(1, m, normed_back(m))
        if m + 1 < NB:
            ffn_back(m + 1)
        second_hop(1, m)
    for g in first:
        g.drain()

    def drain_late(i, carry):
        late(i).drain()
        return carry

    lax.fori_loop(0, NF, drain_late, 0)
    ffn_terms(n2, gg, GC)
    ffn_terms(n2, ug, UC)
    flush()

    def hop2_out(m):
        return send(t2.at[m], q2.at[m], s2s.at[2, m, 0], s2r.at[2, m, 0], me.xpeer)

    for m in range(NB):
        first_hop(2, m, down(m))
    other = 1 - me.x
    for m in range(NB):
        for j in range(2):
            hop1(2, m, j).wait()
        t2[m] = (acc[m, other] + r1[1, m, other].astype(F32)).astype(BF)
        hop2_out(m).start()

    gm = W.at[0:DR, FB : FB + FW]
    peer_term = W.at[DR : 2 * DR, FB : FB + FW]
    loaded = W.at[DR : 2 * DR, FB + FW : FB + 2 * FW]

    def to_wid(slot):
        return W.at[0:DR, pl.ds(pl.multiple_of(FB + FW + slot * FW, BLK), FW)]

    def wid_rows(k):
        return pl.ds(pl.multiple_of(lax.rem(me.w + k, me.wid) * RS, 16), RS)

    def rs_z(ch, col, width, slot, k):
        return send(
            to_wid(slot).at[wid_rows(k), pl.ds(0, width)], z_h.at[k, :, pl.ds(col, width)],
            zs.at[ch, k - 1], zr.at[ch, k - 1], me.wid_peer(k),
        )

    def rs_own(ch, col, width, slot):
        return pltpu.make_async_copy(
            to_wid(slot).at[wid_rows(0), pl.ds(0, width)], z_h.at[0, :, pl.ds(col, width)], zo.at[ch]
        )

    def rs_free(ch, col, width, slot):
        for k in range(1, me.wid):
            rs_z(ch, col, width, slot, k).wait_send()

    def rs_stage(ch, col, width, slot):
        here = pltpu.make_async_copy(g_h.at[dp_rows(0), pl.ds(col, width)], gm.at[:, pl.ds(0, width)], ld.at[0])
        here.start()
        for j in range(1, me.dp):
            rs_y(ch, col, width, j).wait_recv()
            there = pltpu.make_async_copy(
                ry_h.at[j - 1, :, pl.ds(col, width)], peer_term.at[:, pl.ds(0, width)], ld.at[1]
            )
            there.start()
            if j == 1:
                here.wait()
            there.wait()
            for k in range(me.wid):
                rows = wid_rows(k)
                so_far = gm if j == 1 else to_wid(slot)
                to_wid(slot)[rows, 0:width] = (
                    so_far[rows, 0:width].astype(F32) + peer_term[rows, 0:width].astype(F32)
                ).astype(BF)
                if j == me.dp - 1:
                    if k > 0:
                        rs_z(ch, col, width, slot, k).start()
                    else:
                        rs_own(ch, col, width, slot).start()
        rs_own(ch, col, width, slot).wait()

    def rs_late(i):
        f = lax.rem(i + ND, NF)
        return 6 + f, pl.multiple_of(FB + f * FW, BLK), FW

    def rs_sum(ch, col, width, out, at, side, busy):
        for k in range(1, me.wid):
            rs_z(ch, col, width, 0, k).wait_recv()
        loads = [
            pltpu.make_async_copy(
                z_h.at[k, :, pl.ds(col, width)], loaded.at[pl.ds(k * RS, RS), pl.ds(0, width)], ld.at[2 + k]
            )
            for k in range(me.wid)
        ]
        for copy in loads:
            copy.start()
        if busy is not None:
            busy.wait()
        for copy in loads:
            copy.wait()
        done = loaded[0:RS, 0:width].astype(F32)
        for k in range(1, me.wid):
            done = done + loaded[k * RS : (k + 1) * RS, 0:width].astype(F32)
        outv[side, :, 0:width] = done
        copy = pltpu.make_async_copy(outv.at[side, :, pl.ds(0, width)], out.at[:, pl.ds(at, width)], outs.at[side])
        copy.start()
        return copy

    def spread_back(m):
        for j in range(2):
            hop2(1, m, j).wait()
            ng[rows_of(m), block(c + 2 * j)] = total(1, m, j).astype(BF)
            third(1, ng, m, j, c).start()

    def branch_back(m):
        def body(i, carry):
            rows = spans(m * BUF + i * RB, RB)
            low = hlow[rows, :].astype(F32)
            scale = lax.rsqrt(jnp.mean(low * low, axis=1, keepdims=True) + EPSILON)
            scaled = ng[rows, :].astype(F32) * gf[8:9, :]
            row_total = jnp.sum(low * scaled, axis=1, keepdims=True)
            cube = scale * scale * scale * row_total / D
            low_own = hlow[rows, own_cols].astype(F32)
            ng_own = ng[rows, own_cols].astype(F32)
            hgrad[rows, :] = (
                cotf[rows, own_cols].astype(F32) + scale * gf[8:9, own_cols] * ng_own - low_own * cube
            )
            gbuf[slot_here, 8:16, :] += jnp.broadcast_to(
                jnp.sum(low_own * scale * ng_own, axis=0, keepdims=True), (8, CB)
            )
            ng[rows, :] = (cotf[rows, :].astype(F32) + scale * scaled - low * cube).astype(BF)
            return carry

        lax.fori_loop(0, BUF // RB, body, 0)
        made = nn(ng[rows_of(m), :], W[:, OC : OC + HD])
        for hd in range(HL):
            mgrad[m * HL + hd] = made[:, hd * BLK : (hd + 1) * BLK].astype(BF)

    slot_here = me.d * me.wid + me.w
    gbuf[slot_here] = jnp.zeros((16, CB), F32)
    dbeta[...] = jnp.zeros_like(dbeta)
    dA = n2

    def fetch_res(u):
        slot = lax.rem(u, 2)
        return pltpu.make_async_copy(res_h.at[u], resb.at[slot], ress.at[slot])

    fetch_res(0).start()

    def attend_back(u, carry):
        m, hd = lax.div(u, HL), lax.rem(u, HL)
        slot = lax.rem(u, 2)
        parts = [slice(a * BLK, (a + 1) * BLK) for a in range(3)]

        @pl.when(hd == 0)
        def _():
            spread_back(m)
            wait_third(1, ng, m)
            branch_back(m)

        fetch_res(u).wait()

        @pl.when(u + 1 < U)
        def _():
            fetch_res(u + 1).start()

        dq, dk, dv, dh, db = bwd_unit(
            [qs[u, p, :] for p in parts], [ks[u, p, :] for p in parts], [vs[u, p, :] for p in parts],
            [hs[u, p, :] for p in parts], [mgrad[u, p, :] for p in parts], [resb[slot, i] for i in range(NRES)],
        )
        for a in range(3):
            rows = spans(m * BUF + a * BLK, BLK)
            for n, value in enumerate((dq[a], dk[a], dv[a])):
                dA[rows, pl.ds(pl.multiple_of(n * HD + hd * BLK, BLK), BLK)] = value.astype(BF)
            raw = hraw[u, parts[a], :]
            scale = lax.rsqrt(jnp.sum(raw * raw, axis=1, keepdims=True) + EPSILON)
            along = jnp.sum(raw * dh[a], axis=1, keepdims=True)
            dA[rows, pl.ds(pl.multiple_of(3 * HD + hd * BLK, BLK), BLK)] = (
                scale * dh[a] - raw * (scale * scale * scale * along)
            ).astype(BF)
            strength = column(beta[rows, :], hd)
            pull = db[a] * (1.0 / jnp.maximum(strength, 1e-30) - 0.5)
            lanes = lax.broadcasted_iota(jnp.int32, (BLK, BLK), 1)
            dbeta[rows, :] += jnp.where(lanes == hd, pull, 0.0)

        @pl.when((u >= 1) & (u <= NF))
        def _():
            i = u - 1
            slot = lax.rem(i, 4)

            @pl.when(i >= 4)
            def _():
                rs_free(*rs_late(i - 4), slot)

            rs_stage(*rs_late(i), slot)

        return carry

    lax.fori_loop(0, U, attend_back, 0)
    dB[...] = dbeta[...].astype(BF)
    statics = {5: (5, OC, HD), 0: (0, 0, HD), 1: (1, HD, HD), 2: (2, 2 * HD, HD), 3: (3, 3 * HD, HD), 4: (4, BC, BLK)}
    weight_term(5, ng, mix, 0, OC, HD)
    for a in range(4):
        weight_term(a, n1, dA, a * HD, a * HD, HD)
    weight_term(4, n1, dB, 0, BC, BLK)
    flush()

    rt[...] = jnp.zeros_like(rt)

    def first_back(m):
        def partial(b):
            made = nt(dA[rows_of(m), :], W[block(b), 0 : 4 * HD]) + nt(dB[rows_of(m), :], W[block(b), BC:])
            along = jnp.sum(made * tokf[rows_of(m), block(b)].astype(F32) * gf[0:1, block(b)], axis=1, keepdims=True)
            rt[rows_of(m), :] += jnp.broadcast_to(along, (BUF, BLK))
            return made

        return partial

    for m in range(NB):
        hop2_out(m).wait()
        layer_out[rows_of(m), :] = (
            hidown[rows_of(m), :] + (acc[m, me.x] + r1[1, m, me.x].astype(F32) + q2[m].astype(F32))
        ).astype(BF)
    for m in range(NB):
        first_hop(3, m, first_back(m))
    for i in range(T // BLK):
        rts[:, i * BLK : (i + 1) * BLK] = rt[i * BLK : (i + 1) * BLK, :].T[0:8, :]
    rt_copies = [send(rts, rtr.at[k - 1], rs_s.at[k - 1], rs_r.at[k - 1], me.hid_peer(k)) for k in range(1, 4)]
    for copy in rt_copies:
        copy.start()

    def hop2_in(m):
        return send(t2.at[m], r2.at[0, m, 0], s2s.at[3, m, 0], s2r.at[3, m, 0], me.xpeer)

    for m in range(NB):
        for j in range(2):
            hop1(3, m, j).wait()
        t2[m] = (acc[m, other] + r1[0, m, other].astype(F32)).astype(BF)
        hop2_in(m).start()

    done = min(max(U - 1, 0), NF)
    order = [(6 + (i + ND) % NF, FB + (i + ND) % NF * FW, FW) for i in range(NF)]
    order += [statics[k] for k in (5, 0, 1, 2, 3, 4)]

    def target(ch, col):
        if ch < 6:
            return (o_q, o_k, o_v, o_h, o_b, o_o)[ch], 0
        return (o_g, o_u, o_d)[(col - FB) // FL], (col - FB) % FL

    writing = [None, None]
    summed = [0]
    freed = [max(done - 4, 0)]

    def take(n):
        if n >= 4 and freed[0] == n - 4:
            rs_free(*order[n - 4], (n - 4) % 4)
            freed[0] += 1
        rs_stage(*order[n], n % 4)

    def give():
        n = summed[0]
        side = n % 2
        ch, col, width = order[n]
        out, at = target(ch, col)
        writing[side] = rs_sum(ch, col, width, out, at, side, writing[side])
        summed[0] += 1

    for n in range(done, NF + 1):
        take(n)
    give()
    give()
    for m in range(NB):
        hop2_in(m).wait()
    for copy in rt_copies:
        copy.wait()

    def token_rows(i, carry):
        rows = spans(i * BLK, BLK)
        m = lax.div(i, BUF // BLK)
        part = spans(lax.rem(i, BUF // BLK) * BLK, BLK)
        lane = rts[0:1, rows] + rtr[0, 0:1, rows] + rtr[1, 0:1, rows] + rtr[2, 0:1, rows]
        row_total = jnp.broadcast_to(lane, (BLK, BLK)).T[:, 0:1]
        wide = tokf[rows, :].astype(F32)
        scale = lax.rsqrt(jnp.mean(wide * wide, axis=1, keepdims=True) + EPSILON)
        made = acc[m, me.x, part, :] + r1[0, m, me.x, part, :].astype(F32) + r2[0, m, 0, part, :].astype(F32)
        own_tok = tokf[rows, own_cols].astype(F32)
        back = scale * gf[0:1, own_cols] * made - own_tok * (scale * scale * scale * row_total / D)
        tgrad[rows, :] = (hgrad[rows, :] + back).astype(BF)
        gbuf[slot_here, 0:8, :] += jnp.broadcast_to(jnp.sum(own_tok * scale * made, axis=0, keepdims=True), (8, CB))
        return carry

    lax.fori_loop(0, T // BLK, token_rows, 0)
    gain_copies = []
    for n, peer in enumerate(me.group()):
        copy = send(gbuf.at[slot_here], gbuf.at[slot_here], gs_s.at[n], gs_r.at[n], peer)
        copy.start()
        gain_copies.append(copy)
    for n in range(NF + 1, len(order)):
        take(n)
        give()
    for copy in gain_copies:
        copy.wait()
    both = gbuf[0]
    for n in range(1, me.dp * me.wid):
        both = both + gbuf[n]
    one[...] = both[0:1, :]
    two[...] = both[8:9, :]
    while summed[0] < len(order):
        give()
    for n in range(freed[0], len(order)):
        rs_free(*order[n], n % 4)
    for ch, col, width in order:
        for j in range(1, me.dp):
            rs_y(ch, col, width, j).wait_send()
    for copy in writing:
        copy.wait()


def solution(mesh):
    names = tuple(mesh.axis_names)
    sizes = {n: mesh.shape[n] for n in names}
    dp, wid = sizes["dp"], sizes["wid"]
    assert sizes["hid"] == 4

    def shards(
        tokens, cotangent, lengths, keep, norm_one, w_query, w_key, w_value, w_house, w_beta, w_out, norm_two,
        w_gate, w_up, w_down,
    ):
        micro, rows, CB = tokens.shape
        T, D, HD, FL, RS = micro * rows, CB * 4, w_query.shape[1], w_gate.shape[1], w_query.shape[0]
        HL, NB, FW = HD // BLK, T // BUF, 512
        U, NF, DR = NB * HL, 3 * FL // FW, D // dp
        CT = 5 * HD + 3 * FL + BLK
        heads = w_beta.shape[1]
        cfg = dict(names=names, sizes=sizes, T=T, D=D, CB=CB, HL=HL, HD=HD, FL=FL, RS=RS, FW=FW)
        gains = jnp.concatenate([jnp.broadcast_to(g, (8, CB)) for g in (norm_one, norm_two)], axis=0).astype(F32)
        sd = jax.ShapeDtypeStruct
        nch = 6 + NF
        vm = pltpu.VMEM
        unit = lambda t: vm((U, BUF, BLK), t)
        pair = vm((NB, 2, BUF, CB), BF)
        outs = pl.pallas_call(
            functools.partial(layer_kernel, cfg),
            out_shape=(
                sd((T, CB), BF), sd((T, CB), BF), sd((1, CB), F32), sd((1, CB), F32),
                *[sd((RS, HD), F32)] * 4, sd((RS, BLK), F32), sd((RS, HD), F32), *[sd((RS, FL), F32)] * 3,
                sd((D, CT), BF), sd((dp - 1, DR, CT), BF), sd((wid, RS, CT), BF), sd((U, NRES, BLK, BLK), BF),
            ),
            in_specs=[SM, VM] + [ANY] * 12,
            out_specs=(VM,) * 4 + (ANY,) * 13,
            scratch_shapes=[
                vm((D, CT), BF), *[vm((T, D), BF)] * 6, vm((T, HD), BF), *[vm((T, FL), BF)] * 3,
                *[unit(BF)] * 4, unit(F32), unit(BF), vm((T, BLK), F32), vm((T, BLK), F32), vm((T, BLK), BF),
                vm((16, D), F32), vm((2, NRES, BLK, BLK), BF),
                pair, vm((2, NB, 2, BUF, CB), BF), pair, vm((2, NB, 2, BUF, CB), BF), vm((NB, 2, BUF, CB), F32),
                vm((NB, BUF, CB), BF), vm((NB, BUF, CB), BF), vm((T, CB), F32), vm((T, CB), F32),
                vm((2, 4, CB, FW), BF), vm((2, RS, FW), F32),
                vm((8, T), F32), vm((3, 8, T), F32), vm((T, BLK), F32), vm((dp * wid, 16, CB), F32),
                DMA((3,)), DMA((9,)), DMA((3, 3)), DMA((3, 3)), DMA((nch, 2, wid)), DMA((nch, 2, wid)),
                DMA((nch, wid, dp - 1)), DMA((nch, wid, dp - 1)),
                *[DMA((4, NB, 2))] * 4, *[DMA((2, NB, 2))] * 2, DMA((2,)), DMA((2, 4)),
                DMA((nch, dp - 1)), DMA((nch, dp - 1)), DMA((nch, wid - 1)), DMA((nch, wid - 1)), DMA((nch,)),
                DMA((2 + wid,)), DMA((2,)), DMA((3,)), DMA((3,)), DMA((dp * wid - 1,)), DMA((dp * wid - 1,)),
            ],
            compiler_params=pltpu.CompilerParams(
                collective_id=0, has_side_effects=True, vmem_limit_bytes=cfg.get("limit", 63 << 20)
            ),
            name="layer",
        )(
            lengths.reshape(NB, lengths.shape[2]), keep.reshape(NB, 1, BUF), tokens.reshape(T, CB),
            cotangent.reshape(T, CB), gains, w_query, w_key, w_value, w_house,
            jnp.pad(w_beta, ((0, 0), (0, BLK - heads))), w_out.T, w_gate, w_up, w_down.T,
        )
        layer_out, tgrad, one, two, gq, gk, gv, gh, gb, go, g_gate, g_up, g_down = outs[:13]
        return (
            layer_out.reshape(tokens.shape), tgrad.reshape(tokens.shape), one, gq, gk, gv, gh, gb[:, :heads],
            go.T, two, g_gate, g_up, g_down.T,
        )

    rows = P(("dp", "wid"), "hid")
    cols = P("hid", ("dp", "wid"))
    wide = P(None, ("dp", "wid"), "hid")
    gain = P(None, "hid")
    return jax.shard_map(
        shards,
        mesh=mesh,
        in_specs=(
            wide, wide, P(None, ("dp", "wid"), None), P(None, ("dp", "wid")), gain, rows, rows, rows, rows, rows,
            cols, gain, rows, rows, cols,
        ),
        out_specs=(wide, wide, gain, rows, rows, rows, rows, rows, cols, gain, rows, rows, cols),
        check_vma=False,
    )
```

```python
import functools
import math

import jax
import jax.numpy as jnp
from jax import lax
from jax.experimental import pallas as pl
from jax.experimental.pallas import tpu as pltpu
from jax.sharding import PartitionSpec as P

BLK = 128
BUF = 384
EPSILON = 1e-06
F32 = jnp.float32
BF = jnp.bfloat16
MESH = pl.DeviceIdType.MESH
ANY = pl.BlockSpec(memory_space=pl.ANY)
VM = pl.BlockSpec(memory_space=pltpu.VMEM)
SM = pl.BlockSpec(memory_space=pltpu.SMEM)
DMA = pltpu.SemaphoreType.DMA
NRES = 27


def _dot(a,b,ca,cb): return lax.dot_general(a,b,(((ca,),(cb,)),((),())),preferred_element_type=F32)
def nn(a,b): return _dot(a.astype(BF),b.astype(BF),1,0)
def nt(a,b): return _dot(a.astype(BF),b.astype(BF),1,1)
def tn(a,b): return _dot(a.astype(BF),b.astype(BF),0,0)
def split(a):
    hi=a.astype(BF); return hi,(a-hi.astype(F32)).astype(BF)
def nn3(a,b):
    ah,al=split(a); bh,bl=split(b)
    return _dot(ah,bh,1,0)+(_dot(ah,bl,1,0)+_dot(al,bh,1,0))
INV=nn3
def iotas():
    return lax.broadcasted_iota(jnp.int32,(BLK,BLK),0), lax.broadcasted_iota(jnp.int32,(BLK,BLK),1)
def tri_inverse(inners, betas, row, col, between):
    first=((row>>1)==(col>>1))&(row>col)
    xs=[]
    for inner,beta_col in zip(inners,betas):
        diag=jnp.where(row==col, beta_col, 0.0)
        beta_lane=jnp.sum(diag,axis=0,keepdims=True)
        xs.append(diag-jnp.where(first, inner*beta_col*beta_lane, 0.0))
    lb=1
    while (1<<lb)<BLK:
        m=((row>>(lb+1))==(col>>(lb+1)))&((row>>lb)>(col>>lb))
        half=[INV(x,jnp.where(m,inner,0.0)) for x,inner in zip(xs,inners)]
        xs=[x-INV(y,x) for x,y in zip(xs,half)]
        between(lb)
        lb+=1
    return xs
def masks(a,c,e0,e1,keep_row,row,col):
    qp=row+BLK*a; kp=col+BLK*c
    segq=(qp>=e0).astype(jnp.int32)+(qp>=e1).astype(jnp.int32)
    segk=(kp>=e0).astype(jnp.int32)+(kp>=e1).astype(jnp.int32)
    ok=(segq==segk)
    if a==c: return ok&(row>=col)&((keep_row==1)|(row==col))
    return ok&(keep_row==1)
def fwd_unit(q,k,v,h,X,keep,e0,e1):
    nb=len(q); row,col=iotas(); le=row>=col; st=row>col
    A1,L,W,R,Qm,Km=[],[],[],[],[],[]
    for a in range(nb):
        x=X[a]
        a1=jnp.where(le,nt(q[a],h[a]),0.0).astype(BF)
        w=jnp.where(st,nt(h[a],k[a]),0.0).astype(BF)
        l=nn(a1,x).astype(BF); r=nn(x,w).astype(BF)
        A1.append(a1);W.append(w);L.append(l);R.append(r)
        Qm.append((q[a].astype(F32)-nn(l,h[a])).astype(BF))
        Km.append((k[a].astype(F32)-tn(r,h[a])).astype(BF))
    scale=1.0/math.sqrt(BLK)
    S={}
    for a in range(nb):
        S[a,a]=nt(q[a],k[a])-nn(L[a],W[a])
    S[1,0]=nt(Qm[1],Km[0]); S[2,1]=nt(Qm[2],Km[1])
    u=nt(Qm[2],h[1]).astype(BF); ux=nn(u,X[1]).astype(BF)
    cq=(Qm[2].astype(F32)-nn(ux,h[1])).astype(BF)
    S[2,0]=nt(cq,Km[0])
    P={}; out=[]
    for a in range(nb):
        sc={c:jnp.where(masks(a,c,e0,e1,keep[c],row,col),S[a,c]*scale,-1e30) for c in range(a+1)}
        top=jnp.max(sc[0],axis=1,keepdims=True)
        for c in range(1,a+1): top=jnp.maximum(top,jnp.max(sc[c],axis=1,keepdims=True))
        ex={c:jnp.exp(sc[c]-top) for c in sc}
        tot=sum(jnp.sum(e,axis=1,keepdims=True) for e in ex.values())
        inv=1.0/tot
        o=0.0
        for c in sc:
            P[a,c]=(ex[c]*inv).astype(BF); o=o+nn(P[a,c],v[c])
        out.append(o)
    res=A1+L+W+R+Qm+Km+[u,ux,cq]+[P[0,0],P[1,0],P[1,1],P[2,0],P[2,1],P[2,2]]
    return out,res
def bwd_unit(q,k,v,h,do,X,res):
    nb=3; row,col=iotas(); le=row>=col; st=row>col
    A1,L,W,R,Qm,Km=[res[3*i:3*i+3] for i in range(6)]
    u,ux,cq=res[18:21]; pl_=res[21:27]
    P={(0,0):pl_[0],(1,0):pl_[1],(1,1):pl_[2],(2,0):pl_[3],(2,1):pl_[4],(2,2):pl_[5]}
    scale=1.0/math.sqrt(BLK)
    G={}; dv=[0.0]*nb
    for a in range(nb):
        dp={c:nt(do[a],v[c]) for c in range(a+1)}
        delta=sum(jnp.sum(P[a,c].astype(F32)*dp[c],axis=1,keepdims=True) for c in range(a+1))
        for c in range(a+1):
            G[a,c]=(P[a,c].astype(F32)*(dp[c]-delta)*scale).astype(BF)
            dv[c]=dv[c]+tn(P[a,c],do[a])
    dq=[nn(G[a,a],k[a]) for a in range(nb)]
    dk=[tn(G[a,a],q[a]) for a in range(nb)]
    dL=[-nt(G[a,a],W[a]) for a in range(nb)]
    dW=[-tn(L[a],G[a,a]) for a in range(nb)]
    dh=[0.0]*nb; dX=[0.0]*nb
    dcq=nn(G[2,0],Km[0]).astype(BF)
    dQm=[None, nn(G[1,0],Km[0]), nn(G[2,1],Km[1])+dcq.astype(F32)]
    dKm=[tn(G[1,0],Qm[1])+tn(G[2,0],cq), tn(G[2,1],Qm[2]), None]
    dux=(-nt(dcq,h[1])).astype(BF)
    dh[1]=dh[1]-tn(ux,dcq)
    du=nt(dux,X[1]).astype(BF)
    dX[1]=dX[1]+tn(u,dux)
    dQm[2]=dQm[2]+nn(du,h[1])
    dh[1]=dh[1]+tn(du,Qm[2])
    dbeta=[]
    for a in range(nb):
        if dQm[a] is not None:
            d_=dQm[a].astype(BF)
            dq[a]=dq[a]+d_.astype(F32); dL[a]=dL[a]-nt(d_,h[a]); dh[a]=dh[a]-tn(L[a],d_)
        if dKm[a] is not None:
            d_=dKm[a].astype(BF)
            dk[a]=dk[a]+d_.astype(F32); dR=(-nt(h[a],d_)).astype(BF); dh[a]=dh[a]-nn(R[a],d_)
            dX[a]=dX[a]+nt(dR,W[a]); dW[a]=dW[a]+tn(X[a],dR)
        dl=dL[a].astype(BF)
        dA=jnp.where(le,nt(dl,X[a]),0.0).astype(BF)
        dX[a]=dX[a]+tn(A1[a],dl)
        dw=jnp.where(st,dW[a],0.0).astype(BF)
        dh[a]=dh[a]+nn(dw,k[a]); dk[a]=dk[a]+tn(dw,h[a])
        dq[a]=dq[a]+nn(dA,h[a]); dh[a]=dh[a]+tn(dA,q[a])
        dM=nt(tn(X[a],dX[a]),X[a])
        dn=jnp.where(st,-dM,0.0).astype(BF)
        dh[a]=dh[a]+nn(dn,h[a])+tn(dn,h[a])
        dbeta.append(jnp.sum(jnp.where(row==col,dM,0.0),axis=1,keepdims=True))
    return dq,dk,dv,dh,dbeta


def spans(rows, step):
    return pl.ds(pl.multiple_of(rows, step), step)


class Place:
    def __init__(self, names, sizes):
        self.names, self.sizes = names, sizes
        self.d, self.h, self.w = (lax.axis_index(n) for n in ("dp", "hid", "wid"))
        self.dp, self.wid = sizes["dp"], sizes["wid"]
        self.c = lax.rem(self.h, 2)
        self.x = lax.div(self.h, 2)
        self.sib = self.at(h=self.h + 1 - 2 * self.c)
        self.xpeer = self.at(h=lax.rem(self.h + 2, 4))

    def at(self, d=None, h=None, w=None):
        where = {"dp": self.d if d is None else d, "hid": self.h if h is None else h, "wid": self.w if w is None else w}
        return tuple(where[n] for n in self.names)

    def greet(self, peers):
        barrier = pltpu.get_barrier_semaphore()
        for peer in peers:
            pl.semaphore_signal(barrier, inc=1, device_id=peer, device_id_type=MESH)
        pl.semaphore_wait(barrier, len(peers))

    def dp_peer(self, j):
        return self.at(d=lax.rem(self.d + j, self.dp))

    def wid_peer(self, k):
        return self.at(w=lax.rem(self.w + k, self.wid))

    def hid_peer(self, k):
        return self.at(h=lax.rem(self.h + k, 4))

    def group(self):
        return [
            self.at(d=lax.rem(self.d + i, self.dp), w=lax.rem(self.w + k, self.wid))
            for i in range(self.dp)
            for k in range(self.wid)
            if i + k > 0
        ]


def send(src, dst, sent, got, peer):
    return pltpu.make_async_remote_copy(
        src_ref=src, dst_ref=dst, send_sem=sent, recv_sem=got, device_id=peer, device_id_type=MESH
    )


class Gather:
    def __init__(self, me, rows, full, col, width, ch, sz, rz, sy, ry):
        self.me, self.rows, self.full, self.ch = me, rows, full, ch
        self.col, self.width = col, width
        self.sz, self.rz, self.sy, self.ry = sz, rz, sy, ry

    def piece(self, d, o):
        return self.full.at[
            pl.ds(pl.multiple_of((d * self.me.wid + o) * self.rows, 16), self.rows), pl.ds(self.col, self.width)
        ]

    def origin(self, way, hop):
        return lax.clamp(0, self.me.w - way * hop, self.me.wid - 1)

    def zcopy(self, way, hop, sem):
        me, side = self.me, (way + 1) // 2
        part = self.piece(me.d, self.origin(way, hop))
        return send(
            part, part, self.sz.at[self.ch, side, sem], self.rz.at[self.ch, side, sem],
            me.at(w=lax.clamp(0, me.w + way, me.wid - 1)),
        )

    def ycopy(self, d, o, j):
        part = self.piece(d, o)
        return send(part, part, self.sy.at[self.ch, o, j - 1], self.ry.at[self.ch, o, j - 1], self.me.dp_peer(j))

    def has_next(self, way):
        return self.me.w < self.me.wid - 1 if way == 1 else self.me.w > 0

    def has_piece(self, way, hop):
        return self.me.w - hop >= 0 if way == 1 else self.me.w + hop < self.me.wid

    def start_z(self):
        for way in (1, -1):

            @pl.when(self.has_next(way))
            def _():
                self.zcopy(way, 0, 0).start()

    def start_y(self):
        for j in range(1, self.me.dp):
            self.ycopy(self.me.d, self.me.w, j).start()

    def hop(self, hop):
        me = self.me
        for way in (1, -1):

            @pl.when(self.has_piece(way, hop))
            def _():
                self.zcopy(way, hop, hop - 1).wait_recv()

                @pl.when(self.has_next(way))
                def _():
                    self.zcopy(way, hop, hop).start()

                for j in range(1, me.dp):
                    self.ycopy(me.d, self.origin(way, hop), j).start()

    def finish(self):
        me = self.me
        for j in range(1, me.dp):
            for o in range(me.wid):
                self.ycopy(lax.rem(me.d + me.dp - j, me.dp), o, j).wait_recv()

    def drain(self):
        me = self.me
        for way in (1, -1):
            for hop in range(me.wid):

                @pl.when(self.has_piece(way, hop) & self.has_next(way))
                def _():
                    self.zcopy(way, hop, hop).wait_send()

        for j in range(1, me.dp):
            for o in range(me.wid):
                self.ycopy(me.d, o, j).wait_send()


def column(values, lane_index):
    lanes = lax.broadcasted_iota(jnp.int32, values.shape, 1)
    return jnp.sum(jnp.where(lanes == lane_index, values, 0.0), axis=1, keepdims=True)


def layer_kernel(
    cfg, lens, keep, tok, cot, gains, w_q, w_k, w_v, w_h, w_b, w_o, w_g, w_u, w_d,
    layer_out, tgrad, gsum, g_h, ry_h, z_h, res_h,
    W, tokf, cotf, n1, n2, hlow, ng, mix, act, gg, ug, qs, ks, vs, hs, hraw, mgrad, xs, beta, dbeta, dB, gf, resb,
    s1, r1, s2, r2, acc, t2, q2, hidown, hgrad, stage, rts, rtr, rt, gbuf,
    local, own, hx_s, hx_r, sz, rz, sy, ry, s1s, s1r, s2s, s2r, s3s, s3r, ress, stages,
    ys, yr, zs, zr, zo, ld, rs_s, rs_r, gs_s, gs_r,
):
    me = Place(cfg["names"], cfg["sizes"])
    T, D, CB, HL, HD, FL, RS = (cfg[k] for k in ("T", "D", "CB", "HL", "HD", "FL", "RS"))
    FW = cfg["FW"]
    NF = 3 * FL // FW
    FB = 5 * HD
    BC = FB + 3 * FL
    GC, UC, DC, OC = FB, FB + FL, FB + 2 * FL, 4 * HD
    NB, U, DR = T // BUF, T // BUF * HL, RS * me.wid
    c = me.c
    own_cols = pl.ds(pl.multiple_of(me.h * CB, BLK), CB)
    own_rows = pl.ds(pl.multiple_of((me.d * me.wid + me.w) * RS, 16), RS)
    me.greet(me.group() + [me.hid_peer(k) for k in range(1, 4)])

    places = [(w_h, 3 * HD), (w_b, BC), (w_q, 0), (w_k, HD), (w_v, 2 * HD), (w_o, OC), (w_g, GC), (w_u, UC), (w_d, DC)]
    mine = [
        pltpu.make_async_copy(ref, W.at[own_rows, pl.ds(col, ref.shape[1])], own.at[i])
        for i, (ref, col) in enumerate(places)
    ]
    hid = []
    for i, (src, dst) in enumerate(((tok, tokf), (gains, gf), (cot, cotf))):
        here = pltpu.make_async_copy(src, dst.at[:, own_cols], local.at[i])
        away = [
            send(src, dst.at[:, own_cols], hx_s.at[i, k - 1], hx_r.at[i, k - 1], me.hid_peer(k)) for k in range(1, 4)
        ]
        hid.append([here] + away)
    for copy in mine[:6]:
        copy.start()
    for i in range(2):
        for copy in hid[i]:
            copy.start()
    for copy in mine[6:]:
        copy.start()
    sems = (sz, rz, sy, ry)
    first = [
        Gather(me, RS, W, col, ref.shape[1], i, *sems) for i, (ref, col) in enumerate(places[:6])
    ]

    def late(i):
        return Gather(me, RS, W, pl.multiple_of(FB + i * FW, BLK), FW, 6 + i, *sems)

    NG = len(first) + NF

    def chunk(n):
        return first[n] if n < len(first) else late(n - len(first))

    def begin(n):
        if n < NG:
            if n < len(first):
                mine[n].wait()
            elif n == len(first):
                for copy in mine[6:]:
                    copy.wait()
            chunk(n).start_z()
            chunk(n).start_y()

    events = [
        (k - hop + 1, hop) for k in range(NG + me.wid - 2) for hop in range(1, me.wid) if 0 <= k - hop + 1 < NG
    ]

    def advance(count):
        for _ in range(min(count, len(events))):
            n, hop = events.pop(0)
            chunk(n).hop(hop)

    for n in range(NG):
        begin(n)
    for copy in hid[2]:
        copy.start()
    for i in range(2):
        for copy in hid[i]:
            copy.wait()
    RB = 32

    def rows_of(m):
        return pl.ds(pl.multiple_of(m * BUF, BLK), BUF)

    def norm(src, dst, gain, base):
        def body(i, carry):
            rows = spans(base + i * RB, RB)
            wide = src[rows, :].astype(F32)
            scale = lax.rsqrt(jnp.mean(wide * wide, axis=1, keepdims=True) + EPSILON)
            dst[rows, :] = (wide * scale * gf[gain : gain + 1, :]).astype(BF)
            return carry

        lax.fori_loop(0, BUF // RB, body, 0)

    for m in range(NB):
        norm(tokf, n1, 0, m * BUF)

    def project(a):
        for m in range(NB):
            rows = n1[m * BUF : (m + 1) * BUF, :]
            made = nn(rows, W[:, a * HD : (a + 1) * HD])
            for hd in range(HL):
                part = made[:, hd * BLK : (hd + 1) * BLK]
                u = m * HL + hd
                if a < 3:
                    (qs, ks, vs)[a][u] = part.astype(BF)
                else:
                    hraw[u] = part
                    hs[u] = (part * lax.rsqrt(jnp.sum(part * part, axis=1, keepdims=True) + EPSILON)).astype(BF)
            if a == 3:
                beta[m * BUF : (m + 1) * BUF, :] = 2.0 * jax.nn.sigmoid(nn(rows, W[:, BC:]))

    advance(9)
    first[0].finish()
    first[1].finish()
    project(3)

    def invert(hd, carry):
        row, col = iotas()
        blocks = [(m, a) for m in range(NB) for a in range(3)]
        parts = [hs[m * HL + hd, a * BLK : (a + 1) * BLK, :] for m, a in blocks]
        strengths = [column(beta[m * BUF + a * BLK : m * BUF + (a + 1) * BLK, :], hd) for m, a in blocks]

        def between(level):
            for i in range(HL):
                later = slots[i].get(level, [])
                if later:

                    @pl.when(hd == i)
                    def _():
                        for n, hop in later:
                            chunk(n).hop(hop)

        made = tri_inverse([nt(part, part) for part in parts], strengths, row, col, between)
        for (m, a), x in zip(blocks, made):
            xs[m * HL + hd, a] = x.astype(BF)
        return carry

    advance(2)
    slots = [{level: [events.pop(0)] for level in (2, 4, 6) if events} for _ in range(HL)]
    lax.fori_loop(0, HL, invert, 0)
    for a in range(3):
        first[2 + a].finish()
        project(a)
        advance(2)

    def attend(u, carry):
        m, hd = lax.div(u, HL), lax.rem(u, HL)
        slot = lax.rem(u, 2)
        e0 = lens[m, 0]
        e1 = e0 + lens[m, 1]
        parts = [slice(a * BLK, (a + 1) * BLK) for a in range(3)]
        keys = [keep[m, :, p] for p in parts]
        out, res = fwd_unit(
            [qs[u, p, :] for p in parts], [ks[u, p, :] for p in parts], [vs[u, p, :] for p in parts],
            [hs[u, p, :] for p in parts], [xs[u, a] for a in range(3)], keys, e0, e1,
        )
        for a in range(3):
            mix[spans(m * BUF + a * BLK, BLK), pl.ds(pl.multiple_of(hd * BLK, BLK), BLK)] = out[a].astype(BF)

        @pl.when(u >= 2)
        def _():
            pltpu.make_async_copy(resb.at[slot], res_h.at[u], ress.at[slot]).wait()

        for i, value in enumerate(res):
            resb[slot, i] = value
        pltpu.make_async_copy(resb.at[slot], res_h.at[u], ress.at[slot]).start()
        for m in range(NB):

            @pl.when(u == (m + 1) * HL - 1)
            def _():
                if m == 0:
                    first[5].finish()
                first_hop(0, m, branch(m))

            @pl.when(u == (m + 1) * HL)
            def _():
                second_hop(0, m)

        for i, (n, hop) in enumerate(during):

            @pl.when(u == i)
            def _():
                chunk(n).hop(hop)

        return carry

    def block(b):
        return pl.ds(pl.multiple_of(b * CB, BLK), CB)

    def hop1(tag, m, j):
        return send(s1.at[m, j], r1.at[tag % 3 // 2, m, j], s1s.at[tag, m, j], s1r.at[tag, m, j], me.sib)

    def hop2(tag, m, j):
        return send(s2.at[m, j], r2.at[tag, m, j], s2s.at[tag, m, j], s2r.at[tag, m, j], me.xpeer)

    def first_hop(tag, m, partial):
        for j in range(2):
            s1[m, j] = partial((1 - c) + 2 * j).astype(BF)
            hop1(tag, m, j).start()
        for j in range(2):
            acc[m, j] = partial(c + 2 * j)

    def second_hop(tag, m):
        for j in range(2):
            hop1(tag, m, j).wait()
            s2[m, j] = (acc[m, j] + r1[tag // 2, m, j].astype(F32)).astype(BF)
            hop2(tag, m, j).start()

    def total(tag, m, j):
        return s2[m, j].astype(F32) + r2[tag, m, j].astype(F32)

    def third(tag, full, m, j, core):
        part = full.at[rows_of(m), block(core + 2 * j)]
        return send(part, part, s3s.at[tag, m, j], s3r.at[tag, m, j], me.sib)

    def wait_third(tag, full, m):
        for j in range(2):
            third(tag, full, m, j, 1 - c).wait_recv()
            third(tag, full, m, j, c).wait_send()

    def branch(m):
        return lambda b: nt(mix[rows_of(m), :], W[block(b), OC : OC + HD])

    during = [events.pop(0) for _ in range(min(U, len(events)))]
    lax.fori_loop(0, U, attend, 0)
    for slot in range(2):
        pltpu.make_async_copy(resb.at[slot], res_h.at[0], ress.at[slot]).wait()
    second_hop(0, NB - 1)

    def residual(m):
        for j in range(2):
            hop2(0, m, j).wait()
            b = c + 2 * j
            hidden = tokf[rows_of(m), block(b)].astype(F32) + total(0, m, j)
            hlow[rows_of(m), block(b)] = hidden.astype(BF)
            third(0, hlow, m, j, c).start()
        hidown[rows_of(m), :] = tokf[rows_of(m), own_cols].astype(F32) + (
            s2[m, me.x].astype(F32) + r2[0, m, me.x].astype(F32)
        )

    for m in range(NB):
        residual(m)
        advance(2)
        wait_third(0, hlow, m)
        norm(hlow, n2, 8, m * BUF)
    advance(len(events))
    for copy in hid[2]:
        copy.wait()

    def finish_late(i, carry):
        late(i).finish()
        return carry

    NT = 256
    ND = 2 * FL // FW
    lax.fori_loop(0, ND, finish_late, 0)

    def ffn(m):
        def body(n, carry):
            at = pl.multiple_of(n * NT, NT)
            gate = nn(n2[rows_of(m), :], W[:, pl.ds(pl.multiple_of(GC + at, BLK), NT)])
            up = nn(n2[rows_of(m), :], W[:, pl.ds(pl.multiple_of(UC + at, BLK), NT)])
            sig = jax.nn.sigmoid(gate)
            silu = gate * sig
            cols = pl.ds(at, NT)
            act[rows_of(m), cols] = (silu * up).astype(BF)
            gg[rows_of(m), cols] = (up * sig * (1.0 + gate * (1.0 - sig))).astype(BF)
            ug[rows_of(m), cols] = silu.astype(BF)
            return carry

        lax.fori_loop(0, FL // NT, body, 0)

    def ffn_back(m):
        def body(n, carry):
            at = pl.multiple_of(n * NT, NT)
            cols = pl.ds(at, NT)
            back = nn(cotf[rows_of(m), :], W[:, pl.ds(pl.multiple_of(DC + at, BLK), NT)])
            gg[rows_of(m), cols] = (back * gg[rows_of(m), cols].astype(F32)).astype(BF)
            ug[rows_of(m), cols] = (back * ug[rows_of(m), cols].astype(F32)).astype(BF)
            return carry

        lax.fori_loop(0, FL // NT, body, 0)

    def dp_rows(j):
        return pl.ds(pl.multiple_of(lax.rem(me.d + j, me.dp) * DR, 16), DR)

    def staged(side, i, col, width):
        return pltpu.make_async_copy(
            stage.at[side, i, :, pl.ds(0, width)],
            g_h.at[pl.ds(pl.multiple_of(i * CB, BLK), CB), pl.ds(col, width)],
            stages.at[side, i],
        )

    def rs_y(ch, col, width, j):
        return send(
            g_h.at[dp_rows(j), pl.ds(col, width)], ry_h.at[j - 1, :, pl.ds(col, width)],
            ys.at[ch, j - 1], yr.at[ch, j - 1], me.dp_peer(j),
        )

    pending = []
    made_terms = [0]

    def flush():
        side, ch, col, width = pending.pop()
        for i in range(D // CB):
            staged(side, i, col, width).wait()
        for j in range(1, me.dp):
            rs_y(ch, col, width, j).start()

    def weight_term(ch, left, right, at, col, width):
        side = made_terms[0] % 2
        made_terms[0] += 1

        def body(i, carry):
            stage[side, i, :, pl.ds(0, width)] = tn(
                left[:, pl.ds(pl.multiple_of(i * CB, BLK), CB)], right[:, at : at + width]
            ).astype(BF)
            staged(side, i, col, width).start()
            return carry

        lax.fori_loop(0, D // CB, body, 0)
        if pending:
            flush()
        pending.append((side, ch, col, width))

    def ffn_terms(left, right, col):
        for n in range(FL // FW):
            weight_term(6 + (col - FB) // FW + n, left, right, n * FW, col + n * FW, FW)

    for m in range(NB):
        ffn(m)
    ffn_terms(cotf, act, DC)
    flush()
    lax.fori_loop(ND, NF, finish_late, 0)

    def normed_back(m):
        return lambda b: nt(gg[rows_of(m), :], W[block(b), GC : GC + FL]) + nt(
            ug[rows_of(m), :], W[block(b), UC : UC + FL]
        )

    def down(m):
        return lambda b: nt(act[rows_of(m), :], W[block(b), DC : DC + FL])

    ffn_back(0)
    first_hop(1, 0, normed_back(0))
    ffn_back(1)
    second_hop(1, 0)
    for m in range(1, NB):
        first_hop(1, m, normed_back(m))
        if m + 1 < NB:
            ffn_back(m + 1)
        second_hop(1, m)
    for g in first:
        g.drain()

    def drain_late(i, carry):
        late(i).drain()
        return carry

    lax.fori_loop(0, NF, drain_late, 0)
    ffn_terms(n2, gg, GC)
    ffn_terms(n2, ug, UC)
    flush()

    def hop2_out(m):
        return send(t2.at[m], q2.at[m], s2s.at[2, m, 0], s2r.at[2, m, 0], me.xpeer)

    for m in range(NB):
        first_hop(2, m, down(m))
    other = 1 - me.x
    for m in range(NB):
        for j in range(2):
            hop1(2, m, j).wait()
        t2[m] = (acc[m, other] + r1[1, m, other].astype(F32)).astype(BF)
        hop2_out(m).start()

    gm = W.at[0:DR, FB : FB + FW]
    peer_term = W.at[DR : 2 * DR, FB : FB + FW]
    loaded = W.at[DR : 2 * DR, FB + FW : FB + 2 * FW]

    def to_wid(slot):
        return W.at[0:DR, pl.ds(pl.multiple_of(FB + FW + slot * FW, BLK), FW)]

    def wid_rows(k):
        return pl.ds(pl.multiple_of(lax.rem(me.w + k, me.wid) * RS, 16), RS)

    def rs_z(ch, col, width, slot, k):
        return send(
            to_wid(slot).at[wid_rows(k), pl.ds(0, width)], z_h.at[k, :, pl.ds(col, width)],
            zs.at[ch, k - 1], zr.at[ch, k - 1], me.wid_peer(k),
        )

    def rs_own(ch, col, width, slot):
        return pltpu.make_async_copy(
            to_wid(slot).at[wid_rows(0), pl.ds(0, width)], z_h.at[0, :, pl.ds(col, width)], zo.at[ch]
        )

    def rs_free(ch, col, width, slot):
        for k in range(1, me.wid):
            rs_z(ch, col, width, slot, k).wait_send()

    def rs_stage(ch, col, width, slot):
        here = pltpu.make_async_copy(g_h.at[dp_rows(0), pl.ds(col, width)], gm.at[:, pl.ds(0, width)], ld.at[0])
        here.start()
        for j in range(1, me.dp):
            rs_y(ch, col, width, j).wait_recv()
            there = pltpu.make_async_copy(
                ry_h.at[j - 1, :, pl.ds(col, width)], peer_term.at[:, pl.ds(0, width)], ld.at[1]
            )
            there.start()
            if j == 1:
                here.wait()
            there.wait()
            for k in range(me.wid):
                rows = wid_rows(k)
                so_far = gm if j == 1 else to_wid(slot)
                to_wid(slot)[rows, 0:width] = (
                    so_far[rows, 0:width].astype(F32) + peer_term[rows, 0:width].astype(F32)
                ).astype(BF)
                if j == me.dp - 1:
                    if k > 0:
                        rs_z(ch, col, width, slot, k).start()
                    else:
                        rs_own(ch, col, width, slot).start()
        rs_own(ch, col, width, slot).wait()

    places_of = [(3 * HD, HD), (BC, BLK), (0, HD), (HD, HD), (2 * HD, HD), (OC, HD)]
    order = [(6 + (i + ND) % NF, FB + (i + ND) % NF * FW, FW) for i in range(NF)]
    order += [(k, *places_of[k]) for k in (5, 2, 3, 4, 0, 1)]
    taken = [0]

    def take():
        n = taken[0]
        taken[0] += 1
        if n >= 4:
            rs_free(*order[n - 4], n % 4)
        rs_stage(*order[n], n % 4)

    def spread_back(m):
        for j in range(2):
            hop2(1, m, j).wait()
            ng[rows_of(m), block(c + 2 * j)] = total(1, m, j).astype(BF)
            third(1, ng, m, j, c).start()

    def branch_back(m):
        def body(i, carry):
            rows = spans(m * BUF + i * RB, RB)
            low = hlow[rows, :].astype(F32)
            scale = lax.rsqrt(jnp.mean(low * low, axis=1, keepdims=True) + EPSILON)
            scaled = ng[rows, :].astype(F32) * gf[8:9, :]
            row_total = jnp.sum(low * scaled, axis=1, keepdims=True)
            cube = scale * scale * scale * row_total / D
            low_own = hlow[rows, own_cols].astype(F32)
            ng_own = ng[rows, own_cols].astype(F32)
            hgrad[rows, :] = (
                cotf[rows, own_cols].astype(F32) + scale * gf[8:9, own_cols] * ng_own - low_own * cube
            )
            gbuf[slot_here, 8:16, :] += jnp.broadcast_to(
                jnp.sum(low_own * scale * ng_own, axis=0, keepdims=True), (8, CB)
            )
            ng[rows, :] = (cotf[rows, :].astype(F32) + scale * scaled - low * cube).astype(BF)
            return carry

        lax.fori_loop(0, BUF // RB, body, 0)
        made = nn(ng[rows_of(m), :], W[:, OC : OC + HD])
        for hd in range(HL):
            mgrad[m * HL + hd] = made[:, hd * BLK : (hd + 1) * BLK].astype(BF)

    slot_here = me.d * me.wid + me.w
    gbuf[slot_here] = jnp.zeros((16, CB), F32)
    dbeta[...] = jnp.zeros_like(dbeta)
    dA = n2

    def fetch_res(u):
        slot = lax.rem(u, 2)
        return pltpu.make_async_copy(res_h.at[u], resb.at[slot], ress.at[slot])

    fetch_res(0).start()

    def attend_back(u, carry):
        m, hd = lax.div(u, HL), lax.rem(u, HL)
        slot = lax.rem(u, 2)
        parts = [slice(a * BLK, (a + 1) * BLK) for a in range(3)]

        fetch_res(u).wait()

        @pl.when(u + 1 < U)
        def _():
            fetch_res(u + 1).start()

        dq, dk, dv, dh, db = bwd_unit(
            [qs[u, p, :] for p in parts], [ks[u, p, :] for p in parts], [vs[u, p, :] for p in parts],
            [hs[u, p, :] for p in parts], [mgrad[u, p, :] for p in parts], [xs[u, a] for a in range(3)],
            [resb[slot, i] for i in range(NRES)],
        )
        for a in range(3):
            rows = spans(m * BUF + a * BLK, BLK)
            for n, value in enumerate((dq[a], dk[a], dv[a])):
                dA[rows, pl.ds(pl.multiple_of(n * HD + hd * BLK, BLK), BLK)] = value.astype(BF)
            raw = hraw[u, parts[a], :]
            scale = lax.rsqrt(jnp.sum(raw * raw, axis=1, keepdims=True) + EPSILON)
            along = jnp.sum(raw * dh[a], axis=1, keepdims=True)
            dA[rows, pl.ds(pl.multiple_of(3 * HD + hd * BLK, BLK), BLK)] = (
                scale * dh[a] - raw * (scale * scale * scale * along)
            ).astype(BF)
            strength = column(beta[rows, :], hd)
            pull = db[a] * (1.0 / jnp.maximum(strength, 1e-30) - 0.5)
            lanes = lax.broadcasted_iota(jnp.int32, (BLK, BLK), 1)
            dbeta[rows, :] += jnp.where(lanes == hd, pull, 0.0)

        return carry

    take()
    for m in range(NB):
        spread_back(m)
        wait_third(1, ng, m)
        branch_back(m)
        if m == 0:
            take()
    lax.fori_loop(0, U, attend_back, 0)
    dB[...] = dbeta[...].astype(BF)
    weight_term(5, ng, mix, 0, OC, HD)
    take()
    for a in range(3):
        weight_term(2 + a, n1, dA, a * HD, a * HD, HD)
    weight_term(0, n1, dA, 3 * HD, 3 * HD, HD)
    weight_term(1, n1, dB, 0, BC, BLK)
    flush()

    rt[...] = jnp.zeros_like(rt)

    def first_back(m):
        def partial(b):
            made = nt(dA[rows_of(m), :], W[block(b), 0 : 4 * HD]) + nt(dB[rows_of(m), :], W[block(b), BC:])
            along = jnp.sum(made * tokf[rows_of(m), block(b)].astype(F32) * gf[0:1, block(b)], axis=1, keepdims=True)
            rt[rows_of(m), :] += jnp.broadcast_to(along, (BUF, BLK))
            return made

        return partial

    for m in range(NB):
        hop2_out(m).wait()
        layer_out[rows_of(m), :] = (
            hidown[rows_of(m), :] + (acc[m, me.x] + r1[1, m, me.x].astype(F32) + q2[m].astype(F32))
        ).astype(BF)
    for m in range(NB):
        first_hop(3, m, first_back(m))
    for i in range(T // BLK):
        rts[:, i * BLK : (i + 1) * BLK] = rt[i * BLK : (i + 1) * BLK, :].T[0:8, :]
    rt_copies = [send(rts, rtr.at[k - 1], rs_s.at[k - 1], rs_r.at[k - 1], me.hid_peer(k)) for k in range(1, 4)]
    for copy in rt_copies:
        copy.start()

    def hop2_in(m):
        return send(t2.at[m], r2.at[0, m, 0], s2s.at[3, m, 0], s2r.at[3, m, 0], me.xpeer)

    for m in range(NB):
        for j in range(2):
            hop1(3, m, j).wait()
        t2[m] = (acc[m, other] + r1[0, m, other].astype(F32)).astype(BF)
        hop2_in(m).start()

    take()
    for m in range(NB):
        hop2_in(m).wait()
    for copy in rt_copies:
        copy.wait()

    def token_rows(i, carry):
        rows = spans(i * BLK, BLK)
        m = lax.div(i, BUF // BLK)
        part = spans(lax.rem(i, BUF // BLK) * BLK, BLK)
        lane = rts[0:1, rows] + rtr[0, 0:1, rows] + rtr[1, 0:1, rows] + rtr[2, 0:1, rows]
        row_total = jnp.broadcast_to(lane, (BLK, BLK)).T[:, 0:1]
        wide = tokf[rows, :].astype(F32)
        scale = lax.rsqrt(jnp.mean(wide * wide, axis=1, keepdims=True) + EPSILON)
        made = acc[m, me.x, part, :] + r1[0, m, me.x, part, :].astype(F32) + r2[0, m, 0, part, :].astype(F32)
        own_tok = tokf[rows, own_cols].astype(F32)
        back = scale * gf[0:1, own_cols] * made - own_tok * (scale * scale * scale * row_total / D)
        tgrad[rows, :] = (hgrad[rows, :] + back).astype(BF)
        gbuf[slot_here, 0:8, :] += jnp.broadcast_to(jnp.sum(own_tok * scale * made, axis=0, keepdims=True), (8, CB))
        return carry

    lax.fori_loop(0, T // BLK, token_rows, 0)
    gain_copies = []
    for n, peer in enumerate(me.group()):
        copy = send(gbuf.at[slot_here], gbuf.at[slot_here], gs_s.at[n], gs_r.at[n], peer)
        copy.start()
        gain_copies.append(copy)
    while taken[0] < len(order):
        take()
    for copy in gain_copies:
        copy.wait()
    both = gbuf[0]
    for n in range(1, me.dp * me.wid):
        both = both + gbuf[n]
    gsum[...] = both
    for ch, col, width in order:
        for k in range(1, me.wid):
            rs_z(ch, col, width, 0, k).wait_recv()
    for n in range(len(order) - 4, len(order)):
        rs_free(*order[n], n % 4)
    for ch, col, width in order:
        for j in range(1, me.dp):
            rs_y(ch, col, width, j).wait_send()


def final_kernel(
    cfg, z_h, layer_in, tgrad_in, gsum,
    layer_out, tgrad, one, two, o_q, o_k, o_v, o_h, o_b, o_o, o_g, o_u, o_d,
    zbuf, total, gb, loads, stores, through,
):
    HD, FL, RS, wid = cfg["HD"], cfg["FL"], cfg["RS"], cfg["sizes"]["wid"]
    FB = 5 * HD
    targets = [(o_g, FB, FL), (o_u, FB + FL, FL), (o_d, FB + 2 * FL, FL), (o_q, 0, HD), (o_k, HD, HD), (o_v, 2 * HD, HD)]
    targets += [(o_h, 3 * HD, HD), (o_o, 4 * HD, HD), (None, FB + 3 * FL, BLK)]
    passed = [
        pltpu.make_async_copy(layer_in, layer_out, through.at[0]),
        pltpu.make_async_copy(tgrad_in, tgrad, through.at[1]),
        pltpu.make_async_copy(gsum, gb, through.at[2]),
    ]
    copies = [
        pltpu.make_async_copy(z_h.at[:, :, pl.ds(col, w)], zbuf.at[:, :, pl.ds(col, w)], loads.at[i])
        for i, (_, col, w) in enumerate(targets)
    ]
    for copy in copies + passed:
        copy.start()
    written = []
    for i, (out, col, w) in enumerate(targets):
        copies[i].wait()
        value = zbuf[0, :, col : col + w].astype(F32)
        for k in range(1, wid):
            value = value + zbuf[k, :, col : col + w].astype(F32)
        if out is None:
            o_b[...] = value[:, 0 : o_b.shape[1]]
        else:
            total[:, col : col + w] = value
            copy = pltpu.make_async_copy(total.at[:, pl.ds(col, w)], out, stores.at[i])
            copy.start()
            written.append(copy)
    passed[2].wait()
    one[...] = gb[0:1, :]
    two[...] = gb[8:9, :]
    for copy in passed[:2] + written:
        copy.wait()


def solution(mesh):
    names = tuple(mesh.axis_names)
    sizes = {n: mesh.shape[n] for n in names}
    dp, wid = sizes["dp"], sizes["wid"]
    assert sizes["hid"] == 4

    def shards(
        tokens, cotangent, lengths, keep, norm_one, w_query, w_key, w_value, w_house, w_beta, w_out, norm_two,
        w_gate, w_up, w_down,
    ):
        micro, rows, CB = tokens.shape
        T, D, HD, FL, RS = micro * rows, CB * 4, w_query.shape[1], w_gate.shape[1], w_query.shape[0]
        HL, NB, FW = HD // BLK, T // BUF, 512
        U, NF, DR = NB * HL, 3 * FL // FW, D // dp
        CT = 5 * HD + 3 * FL + BLK
        heads = w_beta.shape[1]
        cfg = dict(names=names, sizes=sizes, T=T, D=D, CB=CB, HL=HL, HD=HD, FL=FL, RS=RS, FW=FW)
        gains = jnp.concatenate([jnp.broadcast_to(g, (8, CB)) for g in (norm_one, norm_two)], axis=0).astype(F32)
        sd = jax.ShapeDtypeStruct
        nch = 6 + NF
        vm = pltpu.VMEM
        unit = lambda t: vm((U, BUF, BLK), t)
        pair = vm((NB, 2, BUF, CB), BF)
        outs = pl.pallas_call(
            functools.partial(layer_kernel, cfg),
            out_shape=(
                sd((T, CB), BF), sd((T, CB), BF), sd((16, CB), F32),
                sd((D, CT), BF), sd((dp - 1, DR, CT), BF), sd((wid, RS, CT), BF), sd((U, NRES, BLK, BLK), BF),
            ),
            in_specs=[SM, VM] + [ANY] * 12,
            out_specs=(VM,) * 3 + (ANY,) * 4,
            scratch_shapes=[
                vm((D, CT), BF), *[vm((T, D), BF)] * 6, vm((T, HD), BF), *[vm((T, FL), BF)] * 3,
                *[unit(BF)] * 4, unit(F32), unit(BF), vm((U, 3, BLK, BLK), BF), vm((T, BLK), F32), vm((T, BLK), F32), vm((T, BLK), BF),
                vm((16, D), F32), vm((2, NRES, BLK, BLK), BF),
                pair, vm((2, NB, 2, BUF, CB), BF), pair, vm((2, NB, 2, BUF, CB), BF), vm((NB, 2, BUF, CB), F32),
                vm((NB, BUF, CB), BF), vm((NB, BUF, CB), BF), vm((T, CB), F32), vm((T, CB), F32),
                vm((2, 4, CB, FW), BF),
                vm((8, T), F32), vm((3, 8, T), F32), vm((T, BLK), F32), vm((dp * wid, 16, CB), F32),
                DMA((3,)), DMA((9,)), DMA((3, 3)), DMA((3, 3)), DMA((nch, 2, wid)), DMA((nch, 2, wid)),
                DMA((nch, wid, dp - 1)), DMA((nch, wid, dp - 1)),
                *[DMA((4, NB, 2))] * 4, *[DMA((2, NB, 2))] * 2, DMA((2,)), DMA((2, 4)),
                DMA((nch, dp - 1)), DMA((nch, dp - 1)), DMA((nch, wid - 1)), DMA((nch, wid - 1)), DMA((nch,)),
                DMA((2,)), DMA((3,)), DMA((3,)), DMA((dp * wid - 1,)), DMA((dp * wid - 1,)),
            ],
            compiler_params=pltpu.CompilerParams(
                collective_id=0, has_side_effects=True, vmem_limit_bytes=cfg.get("limit", 63 << 20)
            ),
            name="layer",
        )(
            lengths.reshape(NB, lengths.shape[2]), keep.reshape(NB, 1, BUF), tokens.reshape(T, CB),
            cotangent.reshape(T, CB), gains, w_query, w_key, w_value, w_house,
            jnp.pad(w_beta, ((0, 0), (0, BLK - heads))), w_out.T, w_gate, w_up, w_down.T,
        )
        done = pl.pallas_call(
            functools.partial(final_kernel, cfg),
            out_shape=(
                sd((T, CB), BF), sd((T, CB), BF), sd((1, CB), F32), sd((1, CB), F32),
                *[sd((RS, HD), F32)] * 4, sd((RS, heads), F32), sd((RS, HD), F32), *[sd((RS, FL), F32)] * 3,
            ),
            in_specs=[ANY] * 4,
            out_specs=(ANY, ANY, VM, VM) + (ANY,) * 4 + (VM,) + (ANY,) * 4,
            scratch_shapes=[
                vm((wid, RS, CT), BF), vm((RS, CT), F32), vm((16, CB), F32), DMA((9,)), DMA((9,)), DMA((3,)),
            ],
            compiler_params=pltpu.CompilerParams(vmem_limit_bytes=32 << 20),
            name="final",
        )(outs[5], outs[0], outs[1], outs[2])
        layer_out, tgrad, one, two, gq, gk, gv, gh, gb, go, g_gate, g_up, g_down = done
        return (
            layer_out.reshape(tokens.shape), tgrad.reshape(tokens.shape), one, gq, gk, gv, gh, gb, go.T, two,
            g_gate, g_up, g_down.T,
        )

    rows = P(("dp", "wid"), "hid")
    cols = P("hid", ("dp", "wid"))
    wide = P(None, ("dp", "wid"), "hid")
    gain = P(None, "hid")
    return jax.shard_map(
        shards,
        mesh=mesh,
        in_specs=(
            wide, wide, P(None, ("dp", "wid"), None), P(None, ("dp", "wid")), gain, rows, rows, rows, rows, rows,
            cols, gain, rows, rows, cols,
        ),
        out_specs=(wide, wide, gain, rows, rows, rows, rows, rows, cols, gain, rows, rows, cols),
        check_vma=False,
    )
```

```python
import functools
import math

import jax
import jax.numpy as jnp
from jax import lax
from jax.experimental import pallas as pl
from jax.experimental.pallas import tpu as pltpu
from jax.sharding import PartitionSpec as P

BLK = 128
BUF = 384
EPSILON = 1e-06
F32 = jnp.float32
BF = jnp.bfloat16
MESH = pl.DeviceIdType.MESH
ANY = pl.BlockSpec(memory_space=pl.ANY)
VM = pl.BlockSpec(memory_space=pltpu.VMEM)
SM = pl.BlockSpec(memory_space=pltpu.SMEM)
DMA = pltpu.SemaphoreType.DMA
NRES = 27


def _dot(a,b,ca,cb): return lax.dot_general(a,b,(((ca,),(cb,)),((),())),preferred_element_type=F32)
def nn(a,b): return _dot(a.astype(BF),b.astype(BF),1,0)
def nt(a,b): return _dot(a.astype(BF),b.astype(BF),1,1)
def tn(a,b): return _dot(a.astype(BF),b.astype(BF),0,0)
def split(a):
    hi=a.astype(BF); return hi,(a-hi.astype(F32)).astype(BF)
def nn3(a,b):
    ah,al=split(a); bh,bl=split(b)
    return _dot(ah,bh,1,0)+(_dot(ah,bl,1,0)+_dot(al,bh,1,0))
INV=nn3
def iotas():
    return lax.broadcasted_iota(jnp.int32,(BLK,BLK),0), lax.broadcasted_iota(jnp.int32,(BLK,BLK),1)
def tri_inverse(inners, betas, row, col, between):
    first=((row>>1)==(col>>1))&(row>col)
    xs=[]
    for inner,beta_col in zip(inners,betas):
        diag=jnp.where(row==col, beta_col, 0.0)
        beta_lane=jnp.sum(diag,axis=0,keepdims=True)
        xs.append(diag-jnp.where(first, inner*beta_col*beta_lane, 0.0))
    lb=1
    while (1<<lb)<BLK:
        m=((row>>(lb+1))==(col>>(lb+1)))&((row>>lb)>(col>>lb))
        half=[INV(x,jnp.where(m,inner,0.0)) for x,inner in zip(xs,inners)]
        xs=[x-INV(y,x) for x,y in zip(xs,half)]
        between(lb)
        lb+=1
    return xs
def masks(a,c,e0,e1,keep_row,row,col):
    qp=row+BLK*a; kp=col+BLK*c
    segq=(qp>=e0).astype(jnp.int32)+(qp>=e1).astype(jnp.int32)
    segk=(kp>=e0).astype(jnp.int32)+(kp>=e1).astype(jnp.int32)
    ok=(segq==segk)
    if a==c: return ok&(row>=col)&((keep_row==1)|(row==col))
    return ok&(keep_row==1)
def fwd_unit(q,k,v,h,X,keep,e0,e1):
    nb=len(q); row,col=iotas(); le=row>=col; st=row>col
    A1,L,W,R,Qm,Km=[],[],[],[],[],[]
    for a in range(nb):
        x=X[a]
        a1=jnp.where(le,nt(q[a],h[a]),0.0).astype(BF)
        w=jnp.where(st,nt(h[a],k[a]),0.0).astype(BF)
        l=nn(a1,x).astype(BF); r=nn(x,w).astype(BF)
        A1.append(a1);W.append(w);L.append(l);R.append(r)
        Qm.append((q[a].astype(F32)-nn(l,h[a])).astype(BF))
        Km.append((k[a].astype(F32)-tn(r,h[a])).astype(BF))
    scale=1.0/math.sqrt(BLK)
    S={}
    for a in range(nb):
        S[a,a]=nt(q[a],k[a])-nn(L[a],W[a])
    S[1,0]=nt(Qm[1],Km[0]); S[2,1]=nt(Qm[2],Km[1])
    u=nt(Qm[2],h[1]).astype(BF); ux=nn(u,X[1]).astype(BF)
    cq=(Qm[2].astype(F32)-nn(ux,h[1])).astype(BF)
    S[2,0]=nt(cq,Km[0])
    P={}; out=[]
    for a in range(nb):
        sc={c:jnp.where(masks(a,c,e0,e1,keep[c],row,col),S[a,c]*scale,-1e30) for c in range(a+1)}
        top=jnp.max(sc[0],axis=1,keepdims=True)
        for c in range(1,a+1): top=jnp.maximum(top,jnp.max(sc[c],axis=1,keepdims=True))
        ex={c:jnp.exp(sc[c]-top) for c in sc}
        tot=sum(jnp.sum(e,axis=1,keepdims=True) for e in ex.values())
        inv=1.0/tot
        o=0.0
        for c in sc:
            P[a,c]=(ex[c]*inv).astype(BF); o=o+nn(P[a,c],v[c])
        out.append(o)
    res=A1+L+W+R+Qm+Km+[u,ux,cq]+[P[0,0],P[1,0],P[1,1],P[2,0],P[2,1],P[2,2]]
    return out,res
def bwd_unit(q,k,v,h,do,X,res):
    nb=3; row,col=iotas(); le=row>=col; st=row>col
    A1,L,W,R,Qm,Km=[res[3*i:3*i+3] for i in range(6)]
    u,ux,cq=res[18:21]; pl_=res[21:27]
    P={(0,0):pl_[0],(1,0):pl_[1],(1,1):pl_[2],(2,0):pl_[3],(2,1):pl_[4],(2,2):pl_[5]}
    scale=1.0/math.sqrt(BLK)
    G={}; dv=[0.0]*nb
    for a in range(nb):
        dp={c:nt(do[a],v[c]) for c in range(a+1)}
        delta=sum(jnp.sum(P[a,c].astype(F32)*dp[c],axis=1,keepdims=True) for c in range(a+1))
        for c in range(a+1):
            G[a,c]=(P[a,c].astype(F32)*(dp[c]-delta)*scale).astype(BF)
            dv[c]=dv[c]+tn(P[a,c],do[a])
    dq=[nn(G[a,a],k[a]) for a in range(nb)]
    dk=[tn(G[a,a],q[a]) for a in range(nb)]
    dL=[-nt(G[a,a],W[a]) for a in range(nb)]
    dW=[-tn(L[a],G[a,a]) for a in range(nb)]
    dh=[0.0]*nb; dX=[0.0]*nb
    dcq=nn(G[2,0],Km[0]).astype(BF)
    dQm=[None, nn(G[1,0],Km[0]), nn(G[2,1],Km[1])+dcq.astype(F32)]
    dKm=[tn(G[1,0],Qm[1])+tn(G[2,0],cq), tn(G[2,1],Qm[2]), None]
    dux=(-nt(dcq,h[1])).astype(BF)
    dh[1]=dh[1]-tn(ux,dcq)
    du=nt(dux,X[1]).astype(BF)
    dX[1]=dX[1]+tn(u,dux)
    dQm[2]=dQm[2]+nn(du,h[1])
    dh[1]=dh[1]+tn(du,Qm[2])
    dbeta=[]
    for a in range(nb):
        if dQm[a] is not None:
            d_=dQm[a].astype(BF)
            dq[a]=dq[a]+d_.astype(F32); dL[a]=dL[a]-nt(d_,h[a]); dh[a]=dh[a]-tn(L[a],d_)
        if dKm[a] is not None:
            d_=dKm[a].astype(BF)
            dk[a]=dk[a]+d_.astype(F32); dR=(-nt(h[a],d_)).astype(BF); dh[a]=dh[a]-nn(R[a],d_)
            dX[a]=dX[a]+nt(dR,W[a]); dW[a]=dW[a]+tn(X[a],dR)
        dl=dL[a].astype(BF)
        dA=jnp.where(le,nt(dl,X[a]),0.0).astype(BF)
        dX[a]=dX[a]+tn(A1[a],dl)
        dw=jnp.where(st,dW[a],0.0).astype(BF)
        dh[a]=dh[a]+nn(dw,k[a]); dk[a]=dk[a]+tn(dw,h[a])
        dq[a]=dq[a]+nn(dA,h[a]); dh[a]=dh[a]+tn(dA,q[a])
        dM=nt(tn(X[a],dX[a]),X[a])
        dn=jnp.where(st,-dM,0.0).astype(BF)
        dh[a]=dh[a]+nn(dn,h[a])+tn(dn,h[a])
        dbeta.append(jnp.sum(jnp.where(row==col,dM,0.0),axis=1,keepdims=True))
    return dq,dk,dv,dh,dbeta


def spans(rows, step):
    return pl.ds(pl.multiple_of(rows, step), step)


class Place:
    def __init__(self, names, sizes):
        self.names, self.sizes = names, sizes
        self.d, self.h, self.w = (lax.axis_index(n) for n in ("dp", "hid", "wid"))
        self.dp, self.wid = sizes["dp"], sizes["wid"]
        self.c = lax.rem(self.h, 2)
        self.x = lax.div(self.h, 2)
        self.sib = self.at(h=self.h + 1 - 2 * self.c)
        self.xpeer = self.at(h=lax.rem(self.h + 2, 4))

    def at(self, d=None, h=None, w=None):
        where = {"dp": self.d if d is None else d, "hid": self.h if h is None else h, "wid": self.w if w is None else w}
        return tuple(where[n] for n in self.names)

    def greet(self, peers):
        barrier = pltpu.get_barrier_semaphore()
        for peer in peers:
            pl.semaphore_signal(barrier, inc=1, device_id=peer, device_id_type=MESH)
        pl.semaphore_wait(barrier, len(peers))

    def dp_peer(self, j):
        return self.at(d=lax.rem(self.d + j, self.dp))

    def wid_peer(self, k):
        return self.at(w=lax.rem(self.w + k, self.wid))

    def hid_peer(self, k):
        return self.at(h=lax.rem(self.h + k, 4))

    def group(self):
        return [
            self.at(d=lax.rem(self.d + i, self.dp), w=lax.rem(self.w + k, self.wid))
            for i in range(self.dp)
            for k in range(self.wid)
            if i + k > 0
        ]


def send(src, dst, sent, got, peer):
    return pltpu.make_async_remote_copy(
        src_ref=src, dst_ref=dst, send_sem=sent, recv_sem=got, device_id=peer, device_id_type=MESH
    )


class Gather:
    def __init__(self, me, rows, full, col, width, ch, sz, rz, sy, ry):
        self.me, self.rows, self.full, self.ch = me, rows, full, ch
        self.col, self.width = col, width
        self.sz, self.rz, self.sy, self.ry = sz, rz, sy, ry

    def piece(self, d, o):
        return self.full.at[
            pl.ds(pl.multiple_of((d * self.me.wid + o) * self.rows, 16), self.rows), pl.ds(self.col, self.width)
        ]

    def origin(self, way, hop):
        return lax.clamp(0, self.me.w - way * hop, self.me.wid - 1)

    def zcopy(self, way, hop, sem):
        me, side = self.me, (way + 1) // 2
        part = self.piece(me.d, self.origin(way, hop))
        return send(
            part, part, self.sz.at[self.ch, side, sem], self.rz.at[self.ch, side, sem],
            me.at(w=lax.clamp(0, me.w + way, me.wid - 1)),
        )

    def ycopy(self, d, o, j):
        part = self.piece(d, o)
        return send(part, part, self.sy.at[self.ch, o, j - 1], self.ry.at[self.ch, o, j - 1], self.me.dp_peer(j))

    def has_next(self, way):
        return self.me.w < self.me.wid - 1 if way == 1 else self.me.w > 0

    def has_piece(self, way, hop):
        return self.me.w - hop >= 0 if way == 1 else self.me.w + hop < self.me.wid

    def start_z(self):
        for way in (1, -1):

            @pl.when(self.has_next(way))
            def _():
                self.zcopy(way, 0, 0).start()

    def start_y(self):
        for j in range(1, self.me.dp):
            self.ycopy(self.me.d, self.me.w, j).start()

    def hop(self, hop):
        me = self.me
        for way in (1, -1):

            @pl.when(self.has_piece(way, hop))
            def _():
                self.zcopy(way, hop, hop - 1).wait_recv()

                @pl.when(self.has_next(way))
                def _():
                    self.zcopy(way, hop, hop).start()

                for j in range(1, me.dp):
                    self.ycopy(me.d, self.origin(way, hop), j).start()

    def finish(self):
        me = self.me
        for j in range(1, me.dp):
            for o in range(me.wid):
                self.ycopy(lax.rem(me.d + me.dp - j, me.dp), o, j).wait_recv()

    def drain_z(self):
        me = self.me
        for way in (1, -1):
            for hop in range(me.wid):

                @pl.when(self.has_piece(way, hop) & self.has_next(way))
                def _():
                    self.zcopy(way, hop, hop).wait_send()

    def drain(self):
        self.drain_z()
        for j in range(1, self.me.dp):
            for o in range(self.me.wid):
                self.ycopy(self.me.d, o, j).wait_send()


class Line(Gather):
    def __init__(self, d, *args):
        super().__init__(*args)
        self.group = d

    def zcopy(self, way, hop, sem):
        me, side = self.me, (way + 1) // 2
        part = self.piece(self.group, self.origin(way, hop))
        return send(
            part, part, self.sz.at[self.ch, side, sem], self.rz.at[self.ch, side, sem],
            me.at(w=lax.clamp(0, me.w + way, me.wid - 1)),
        )

    def hop(self, hop):
        for way in (1, -1):

            @pl.when(self.has_piece(way, hop))
            def _():
                self.zcopy(way, hop, hop - 1).wait_recv()

                @pl.when(self.has_next(way))
                def _():
                    self.zcopy(way, hop, hop).start()


class Across(Gather):
    def __init__(self, extra, *args):
        super().__init__(*args)
        me, rows, full, col, width, ch = args[:6]
        self.lines = [
            Line(lax.rem(me.d + me.dp - j, me.dp), me, rows, full, col, width, ch if j == 0 else extra + j - 1, *args[6:])
            for j in range(me.dp)
        ]

    def start_z(self):
        self.lines[0].start_z()

    def hop(self, hop):
        me = self.me
        if hop == 0:
            for j in range(1, me.dp):
                self.ycopy(lax.rem(me.d + me.dp - j, me.dp), me.w, j).wait_recv()
                self.lines[j].start_z()
        else:
            for line in self.lines:
                line.hop(hop)

    def finish(self):
        pass

    def drain(self):
        for line in self.lines:
            line.drain_z()
        for j in range(1, self.me.dp):
            self.ycopy(self.me.d, self.me.w, j).wait_send()


def column(values, lane_index):
    lanes = lax.broadcasted_iota(jnp.int32, values.shape, 1)
    return jnp.sum(jnp.where(lanes == lane_index, values, 0.0), axis=1, keepdims=True)


def layer_kernel(
    cfg, lens, keep, tok, cot, gains, w_q, w_k, w_v, w_h, w_b, w_o, w_g, w_u, w_d,
    layer_out, tgrad, gsum, g_h, ry_h, z_h, res_h,
    W, tokf, cotf, n1, n2, hlow, ng, mix, act, gg, ug, qs, ks, vs, hs, hraw, mgrad, xs, beta, dbeta, dB, gf, resb,
    s1, r1, s2, r2, acc, t2, q2, hidown, hgrad, stage, rts, rtr, rt, gbuf,
    local, own, hx_s, hx_r, sz, rz, sy, ry, s1s, s1r, s2s, s2r, s3s, s3r, ress, stages,
    ys, yr, zs, zr, zo, ld, rs_s, rs_r, gs_s, gs_r,
):
    me = Place(cfg["names"], cfg["sizes"])
    T, D, CB, HL, HD, FL, RS = (cfg[k] for k in ("T", "D", "CB", "HL", "HD", "FL", "RS"))
    FW = cfg["FW"]
    NF = 3 * FL // FW
    FB = 5 * HD
    BC = FB + 3 * FL
    GC, UC, DC, OC = FB, FB + FL, FB + 2 * FL, 4 * HD
    NB, U, DR = T // BUF, T // BUF * HL, RS * me.wid
    c = me.c
    own_cols = pl.ds(pl.multiple_of(me.h * CB, BLK), CB)
    own_rows = pl.ds(pl.multiple_of((me.d * me.wid + me.w) * RS, 16), RS)
    me.greet(me.group() + [me.hid_peer(k) for k in range(1, 4)])

    places = [(w_h, 3 * HD), (w_b, BC), (w_q, 0), (w_k, HD), (w_v, 2 * HD), (w_o, OC), (w_g, GC), (w_u, UC), (w_d, DC)]
    mine = [
        pltpu.make_async_copy(ref, W.at[own_rows, pl.ds(col, ref.shape[1])], own.at[i])
        for i, (ref, col) in enumerate(places)
    ]
    hid = []
    for i, (src, dst) in enumerate(((tok, tokf), (gains, gf), (cot, cotf))):
        here = pltpu.make_async_copy(src, dst.at[:, own_cols], local.at[i])
        away = [
            send(src, dst.at[:, own_cols], hx_s.at[i, k - 1], hx_r.at[i, k - 1], me.hid_peer(k)) for k in range(1, 4)
        ]
        hid.append([here] + away)
    for copy in mine[:6]:
        copy.start()
    for i in range(2):
        for copy in hid[i]:
            copy.start()
    for copy in mine[6:]:
        copy.start()
    sems = (sz, rz, sy, ry)
    first = [
        Gather(me, RS, W, col, ref.shape[1], i, *sems) for i, (ref, col) in enumerate(places[:6])
    ]

    def late(i):
        args = (me, RS, W, FB + i * FW, FW, 6 + i, *sems)
        if i in cfg["across"]:
            return Across(6 + NF + cfg["across"].index(i) * (me.dp - 1), *args)
        return Gather(*args)

    NG = len(first) + NF

    def chunk(n):
        return first[n] if n < len(first) else late(n - len(first))

    def begin(n):
        if n < NG:
            if n < len(first):
                mine[n].wait()
            elif n == len(first):
                for copy in mine[6:]:
                    copy.wait()
            chunk(n).start_z()
            chunk(n).start_y()

    events = [
        (k - hop + 1, hop) for k in range(NG + me.wid - 2) for hop in range(1, me.wid) if 0 <= k - hop + 1 < NG
    ]
    for i in cfg["across"]:
        events.insert(events.index((6 + i, 1)), (6 + i, 0))

    def advance(count):
        for _ in range(min(count, len(events))):
            n, hop = events.pop(0)
            chunk(n).hop(hop)

    for n in range(NG):
        begin(n)
    for copy in hid[2]:
        copy.start()
    for i in range(2):
        for copy in hid[i]:
            copy.wait()
    RB = 32

    def rows_of(m):
        return pl.ds(pl.multiple_of(m * BUF, BLK), BUF)

    def norm(src, dst, gain, base):
        def body(i, carry):
            rows = spans(base + i * RB, RB)
            wide = src[rows, :].astype(F32)
            scale = lax.rsqrt(jnp.mean(wide * wide, axis=1, keepdims=True) + EPSILON)
            dst[rows, :] = (wide * scale * gf[gain : gain + 1, :]).astype(BF)
            return carry

        lax.fori_loop(0, BUF // RB, body, 0)

    for m in range(NB):
        norm(tokf, n1, 0, m * BUF)

    def project(a):
        for m in range(NB):
            rows = n1[m * BUF : (m + 1) * BUF, :]
            made = nn(rows, W[:, a * HD : (a + 1) * HD])
            for hd in range(HL):
                part = made[:, hd * BLK : (hd + 1) * BLK]
                u = m * HL + hd
                if a < 3:
                    (qs, ks, vs)[a][u] = part.astype(BF)
                else:
                    hraw[u] = part
                    hs[u] = (part * lax.rsqrt(jnp.sum(part * part, axis=1, keepdims=True) + EPSILON)).astype(BF)
            if a == 3:
                beta[m * BUF : (m + 1) * BUF, :] = 2.0 * jax.nn.sigmoid(nn(rows, W[:, BC:]))

    advance(9)
    first[0].finish()
    first[1].finish()
    project(3)

    def invert(hd, carry):
        row, col = iotas()
        blocks = [(m, a) for m in range(NB) for a in range(3)]
        parts = [hs[m * HL + hd, a * BLK : (a + 1) * BLK, :] for m, a in blocks]
        strengths = [column(beta[m * BUF + a * BLK : m * BUF + (a + 1) * BLK, :], hd) for m, a in blocks]

        def between(level):
            for i in range(HL):
                later = slots[i].get(level, [])
                if later:

                    @pl.when(hd == i)
                    def _():
                        for n, hop in later:
                            chunk(n).hop(hop)

        made = tri_inverse([nt(part, part) for part in parts], strengths, row, col, between)
        for (m, a), x in zip(blocks, made):
            xs[m * HL + hd, a] = x.astype(BF)
        return carry

    advance(2)
    slots = [{level: [events.pop(0)] for level in (2, 4, 6) if events} for _ in range(HL)]
    lax.fori_loop(0, HL, invert, 0)
    for a in range(3):
        first[2 + a].finish()
        project(a)
        advance(2)

    def attend(u, carry):
        m, hd = lax.div(u, HL), lax.rem(u, HL)
        slot = lax.rem(u, 2)
        e0 = lens[m, 0]
        e1 = e0 + lens[m, 1]
        parts = [slice(a * BLK, (a + 1) * BLK) for a in range(3)]
        keys = [keep[m, :, p] for p in parts]
        out, res = fwd_unit(
            [qs[u, p, :] for p in parts], [ks[u, p, :] for p in parts], [vs[u, p, :] for p in parts],
            [hs[u, p, :] for p in parts], [xs[u, a] for a in range(3)], keys, e0, e1,
        )
        for a in range(3):
            mix[spans(m * BUF + a * BLK, BLK), pl.ds(pl.multiple_of(hd * BLK, BLK), BLK)] = out[a].astype(BF)

        @pl.when(u >= 2)
        def _():
            pltpu.make_async_copy(resb.at[slot], res_h.at[u], ress.at[slot]).wait()

        for i, value in enumerate(res):
            resb[slot, i] = value
        pltpu.make_async_copy(resb.at[slot], res_h.at[u], ress.at[slot]).start()
        for m in range(NB):

            @pl.when(u == (m + 1) * HL - 1)
            def _():
                if m == 0:
                    first[5].finish()
                first_hop(0, m, branch(m))

            @pl.when(u == (m + 1) * HL)
            def _():
                second_hop(0, m)

        for i, (n, hop) in enumerate(during):

            @pl.when(u == i)
            def _():
                chunk(n).hop(hop)

        return carry

    def block(b):
        return pl.ds(pl.multiple_of(b * CB, BLK), CB)

    def hop1(tag, m, j):
        return send(s1.at[m, j], r1.at[tag % 3 // 2, m, j], s1s.at[tag, m, j], s1r.at[tag, m, j], me.sib)

    def hop2(tag, m, j):
        return send(s2.at[m, j], r2.at[tag, m, j], s2s.at[tag, m, j], s2r.at[tag, m, j], me.xpeer)

    def first_hop(tag, m, partial):
        for j in range(2):
            s1[m, j] = partial((1 - c) + 2 * j).astype(BF)
            hop1(tag, m, j).start()
        for j in range(2):
            acc[m, j] = partial(c + 2 * j)

    def second_hop(tag, m):
        for j in range(2):
            hop1(tag, m, j).wait()
            s2[m, j] = (acc[m, j] + r1[tag // 2, m, j].astype(F32)).astype(BF)
            hop2(tag, m, j).start()

    def total(tag, m, j):
        return s2[m, j].astype(F32) + r2[tag, m, j].astype(F32)

    def third(tag, full, m, j, core):
        part = full.at[rows_of(m), block(core + 2 * j)]
        return send(part, part, s3s.at[tag, m, j], s3r.at[tag, m, j], me.sib)

    def wait_third(tag, full, m):
        for j in range(2):
            third(tag, full, m, j, 1 - c).wait_recv()
            third(tag, full, m, j, c).wait_send()

    def branch(m):
        return lambda b: nt(mix[rows_of(m), :], W[block(b), OC : OC + HD])

    during = [events.pop(0) for _ in range(min(U, len(events)))]
    lax.fori_loop(0, U, attend, 0)
    for slot in range(2):
        pltpu.make_async_copy(resb.at[slot], res_h.at[0], ress.at[slot]).wait()
    second_hop(0, NB - 1)

    def residual(m):
        for j in range(2):
            hop2(0, m, j).wait()
            b = c + 2 * j
            hidden = tokf[rows_of(m), block(b)].astype(F32) + total(0, m, j)
            hlow[rows_of(m), block(b)] = hidden.astype(BF)
            third(0, hlow, m, j, c).start()
        hidown[rows_of(m), :] = tokf[rows_of(m), own_cols].astype(F32) + (
            s2[m, me.x].astype(F32) + r2[0, m, me.x].astype(F32)
        )

    for m in range(NB):
        residual(m)
        advance(2)
        wait_third(0, hlow, m)
        norm(hlow, n2, 8, m * BUF)
    advance(len(events))
    for copy in hid[2]:
        copy.wait()

    NT = 256
    ND = 2 * FL // FW
    for i in range(ND):
        late(i).finish()

    def ffn(m):
        def body(n, carry):
            at = pl.multiple_of(n * NT, NT)
            gate = nn(n2[rows_of(m), :], W[:, pl.ds(pl.multiple_of(GC + at, BLK), NT)])
            up = nn(n2[rows_of(m), :], W[:, pl.ds(pl.multiple_of(UC + at, BLK), NT)])
            sig = jax.nn.sigmoid(gate)
            silu = gate * sig
            cols = pl.ds(at, NT)
            act[rows_of(m), cols] = (silu * up).astype(BF)
            gg[rows_of(m), cols] = (up * sig * (1.0 + gate * (1.0 - sig))).astype(BF)
            ug[rows_of(m), cols] = silu.astype(BF)
            return carry

        lax.fori_loop(0, FL // NT, body, 0)

    def ffn_back(m):
        def body(n, carry):
            at = pl.multiple_of(n * NT, NT)
            cols = pl.ds(at, NT)
            back = nn(cotf[rows_of(m), :], W[:, pl.ds(pl.multiple_of(DC + at, BLK), NT)])
            gg[rows_of(m), cols] = (back * gg[rows_of(m), cols].astype(F32)).astype(BF)
            ug[rows_of(m), cols] = (back * ug[rows_of(m), cols].astype(F32)).astype(BF)
            return carry

        lax.fori_loop(0, FL // NT, body, 0)

    def dp_rows(j):
        return pl.ds(pl.multiple_of(lax.rem(me.d + j, me.dp) * DR, 16), DR)

    def staged(side, i, col, width):
        return pltpu.make_async_copy(
            stage.at[side, i, :, pl.ds(0, width)],
            g_h.at[pl.ds(pl.multiple_of(i * CB, BLK), CB), pl.ds(col, width)],
            stages.at[side, i],
        )

    def rs_y(ch, col, width, j):
        return send(
            g_h.at[dp_rows(j), pl.ds(col, width)], ry_h.at[j - 1, :, pl.ds(col, width)],
            ys.at[ch, j - 1], yr.at[ch, j - 1], me.dp_peer(j),
        )

    pending = []
    made_terms = [0]

    def flush():
        side, ch, col, width = pending.pop()
        for i in range(D // CB):
            staged(side, i, col, width).wait()
        for j in range(1, me.dp):
            rs_y(ch, col, width, j).start()

    def weight_term(ch, left, right, at, col, width):
        side = made_terms[0] % 2
        made_terms[0] += 1

        def body(i, carry):
            stage[side, i, :, pl.ds(0, width)] = tn(
                left[:, pl.ds(pl.multiple_of(i * CB, BLK), CB)], right[:, at : at + width]
            ).astype(BF)
            staged(side, i, col, width).start()
            return carry

        lax.fori_loop(0, D // CB, body, 0)
        if pending:
            flush()
        pending.append((side, ch, col, width))

    def ffn_terms(left, right, col):
        for n in range(FL // FW):
            weight_term(6 + (col - FB) // FW + n, left, right, n * FW, col + n * FW, FW)

    for m in range(NB):
        ffn(m)
    ffn_terms(cotf, act, DC)
    flush()
    for i in range(ND, NF):
        late(i).finish()

    def normed_back(m):
        return lambda b: nt(gg[rows_of(m), :], W[block(b), GC : GC + FL]) + nt(
            ug[rows_of(m), :], W[block(b), UC : UC + FL]
        )

    def down(m):
        return lambda b: nt(act[rows_of(m), :], W[block(b), DC : DC + FL])

    ffn_back(0)
    first_hop(1, 0, normed_back(0))
    ffn_back(1)
    second_hop(1, 0)
    for m in range(1, NB):
        first_hop(1, m, normed_back(m))
        if m + 1 < NB:
            ffn_back(m + 1)
        second_hop(1, m)
    for g in first:
        g.drain()

    for i in range(NF):
        late(i).drain()
    ffn_terms(n2, gg, GC)
    ffn_terms(n2, ug, UC)
    flush()

    def hop2_out(m):
        return send(t2.at[m], q2.at[m], s2s.at[2, m, 0], s2r.at[2, m, 0], me.xpeer)

    for m in range(NB):
        first_hop(2, m, down(m))
    other = 1 - me.x
    for m in range(NB):
        for j in range(2):
            hop1(2, m, j).wait()
        t2[m] = (acc[m, other] + r1[1, m, other].astype(F32)).astype(BF)
        hop2_out(m).start()

    gm = W.at[0:DR, FB : FB + FW]
    peer_term = W.at[DR : 2 * DR, FB : FB + FW]
    loaded = W.at[DR : 2 * DR, FB + FW : FB + 2 * FW]

    def to_wid(slot):
        return W.at[0:DR, pl.ds(pl.multiple_of(FB + FW + slot * FW, BLK), FW)]

    def wid_rows(k):
        return pl.ds(pl.multiple_of(lax.rem(me.w + k, me.wid) * RS, 16), RS)

    def rs_z(ch, col, width, slot, k):
        return send(
            to_wid(slot).at[wid_rows(k), pl.ds(0, width)], z_h.at[k, :, pl.ds(col, width)],
            zs.at[ch, k - 1], zr.at[ch, k - 1], me.wid_peer(k),
        )

    def rs_own(ch, col, width, slot):
        return pltpu.make_async_copy(
            to_wid(slot).at[wid_rows(0), pl.ds(0, width)], z_h.at[0, :, pl.ds(col, width)], zo.at[ch]
        )

    def rs_free(ch, col, width, slot):
        for k in range(1, me.wid):
            rs_z(ch, col, width, slot, k).wait_send()

    def rs_stage(ch, col, width, slot):
        here = pltpu.make_async_copy(g_h.at[dp_rows(0), pl.ds(col, width)], gm.at[:, pl.ds(0, width)], ld.at[0])
        here.start()
        for j in range(1, me.dp):
            rs_y(ch, col, width, j).wait_recv()
            there = pltpu.make_async_copy(
                ry_h.at[j - 1, :, pl.ds(col, width)], peer_term.at[:, pl.ds(0, width)], ld.at[1]
            )
            there.start()
            if j == 1:
                here.wait()
            there.wait()
            for k in range(me.wid):
                rows = wid_rows(k)
                so_far = gm if j == 1 else to_wid(slot)
                to_wid(slot)[rows, 0:width] = (
                    so_far[rows, 0:width].astype(F32) + peer_term[rows, 0:width].astype(F32)
                ).astype(BF)
                if j == me.dp - 1:
                    if k > 0:
                        rs_z(ch, col, width, slot, k).start()
                    else:
                        rs_own(ch, col, width, slot).start()
        rs_own(ch, col, width, slot).wait()

    places_of = [(3 * HD, HD), (BC, BLK), (0, HD), (HD, HD), (2 * HD, HD), (OC, HD)]
    order = [(6 + (i + ND) % NF, FB + (i + ND) % NF * FW, FW) for i in range(NF)]
    order += [(k, *places_of[k]) for k in (5, 2, 3, 4, 0, 1)]
    taken = [0]

    def take():
        n = taken[0]
        taken[0] += 1
        if n >= 4:
            rs_free(*order[n - 4], n % 4)
        rs_stage(*order[n], n % 4)

    def spread_back(m):
        for j in range(2):
            hop2(1, m, j).wait()
            ng[rows_of(m), block(c + 2 * j)] = total(1, m, j).astype(BF)
            third(1, ng, m, j, c).start()

    def branch_back(m):
        def body(i, carry):
            rows = spans(m * BUF + i * RB, RB)
            low = hlow[rows, :].astype(F32)
            scale = lax.rsqrt(jnp.mean(low * low, axis=1, keepdims=True) + EPSILON)
            scaled = ng[rows, :].astype(F32) * gf[8:9, :]
            row_total = jnp.sum(low * scaled, axis=1, keepdims=True)
            cube = scale * scale * scale * row_total / D
            low_own = hlow[rows, own_cols].astype(F32)
            ng_own = ng[rows, own_cols].astype(F32)
            hgrad[rows, :] = (
                cotf[rows, own_cols].astype(F32) + scale * gf[8:9, own_cols] * ng_own - low_own * cube
            )
            gbuf[slot_here, 8:16, :] += jnp.broadcast_to(
                jnp.sum(low_own * scale * ng_own, axis=0, keepdims=True), (8, CB)
            )
            ng[rows, :] = (cotf[rows, :].astype(F32) + scale * scaled - low * cube).astype(BF)
            return carry

        lax.fori_loop(0, BUF // RB, body, 0)
        made = nn(ng[rows_of(m), :], W[:, OC : OC + HD])
        for hd in range(HL):
            mgrad[m * HL + hd] = made[:, hd * BLK : (hd + 1) * BLK].astype(BF)

    slot_here = me.d * me.wid + me.w
    gbuf[slot_here] = jnp.zeros((16, CB), F32)
    dbeta[...] = jnp.zeros_like(dbeta)
    dA = n2

    def fetch_res(u):
        slot = lax.rem(u, 2)
        return pltpu.make_async_copy(res_h.at[u], resb.at[slot], ress.at[slot])

    fetch_res(0).start()

    def attend_back(u, carry):
        m, hd = lax.div(u, HL), lax.rem(u, HL)
        slot = lax.rem(u, 2)
        parts = [slice(a * BLK, (a + 1) * BLK) for a in range(3)]

        fetch_res(u).wait()

        @pl.when(u + 1 < U)
        def _():
            fetch_res(u + 1).start()

        dq, dk, dv, dh, db = bwd_unit(
            [qs[u, p, :] for p in parts], [ks[u, p, :] for p in parts], [vs[u, p, :] for p in parts],
            [hs[u, p, :] for p in parts], [mgrad[u, p, :] for p in parts], [xs[u, a] for a in range(3)],
            [resb[slot, i] for i in range(NRES)],
        )
        for a in range(3):
            rows = spans(m * BUF + a * BLK, BLK)
            for n, value in enumerate((dq[a], dk[a], dv[a])):
                dA[rows, pl.ds(pl.multiple_of(n * HD + hd * BLK, BLK), BLK)] = value.astype(BF)
            raw = hraw[u, parts[a], :]
            scale = lax.rsqrt(jnp.sum(raw * raw, axis=1, keepdims=True) + EPSILON)
            along = jnp.sum(raw * dh[a], axis=1, keepdims=True)
            dA[rows, pl.ds(pl.multiple_of(3 * HD + hd * BLK, BLK), BLK)] = (
                scale * dh[a] - raw * (scale * scale * scale * along)
            ).astype(BF)
            strength = column(beta[rows, :], hd)
            pull = db[a] * (1.0 / jnp.maximum(strength, 1e-30) - 0.5)
            lanes = lax.broadcasted_iota(jnp.int32, (BLK, BLK), 1)
            dbeta[rows, :] += jnp.where(lanes == hd, pull, 0.0)

        return carry

    take()
    for m in range(NB):
        spread_back(m)
        wait_third(1, ng, m)
        branch_back(m)
        if m == 0:
            take()
    lax.fori_loop(0, U, attend_back, 0)
    dB[...] = dbeta[...].astype(BF)
    weight_term(5, ng, mix, 0, OC, HD)
    take()
    for a in range(3):
        weight_term(2 + a, n1, dA, a * HD, a * HD, HD)
    weight_term(0, n1, dA, 3 * HD, 3 * HD, HD)
    weight_term(1, n1, dB, 0, BC, BLK)
    flush()

    rt[...] = jnp.zeros_like(rt)

    def first_back(m):
        def partial(b):
            made = nt(dA[rows_of(m), :], W[block(b), 0 : 4 * HD]) + nt(dB[rows_of(m), :], W[block(b), BC:])
            along = jnp.sum(made * tokf[rows_of(m), block(b)].astype(F32) * gf[0:1, block(b)], axis=1, keepdims=True)
            rt[rows_of(m), :] += jnp.broadcast_to(along, (BUF, BLK))
            return made

        return partial

    for m in range(NB):
        hop2_out(m).wait()
        layer_out[rows_of(m), :] = (
            hidown[rows_of(m), :] + (acc[m, me.x] + r1[1, m, me.x].astype(F32) + q2[m].astype(F32))
        ).astype(BF)
    for m in range(NB):
        first_hop(3, m, first_back(m))
    for i in range(T // BLK):
        rts[:, i * BLK : (i + 1) * BLK] = rt[i * BLK : (i + 1) * BLK, :].T[0:8, :]
    rt_copies = [send(rts, rtr.at[k - 1], rs_s.at[k - 1], rs_r.at[k - 1], me.hid_peer(k)) for k in range(1, 4)]
    for copy in rt_copies:
        copy.start()

    def hop2_in(m):
        return send(t2.at[m], r2.at[0, m, 0], s2s.at[3, m, 0], s2r.at[3, m, 0], me.xpeer)

    for m in range(NB):
        for j in range(2):
            hop1(3, m, j).wait()
        t2[m] = (acc[m, other] + r1[0, m, other].astype(F32)).astype(BF)
        hop2_in(m).start()

    take()
    for m in range(NB):
        hop2_in(m).wait()
    for copy in rt_copies:
        copy.wait()

    def token_rows(i, carry):
        rows = spans(i * BLK, BLK)
        m = lax.div(i, BUF // BLK)
        part = spans(lax.rem(i, BUF // BLK) * BLK, BLK)
        lane = rts[0:1, rows] + rtr[0, 0:1, rows] + rtr[1, 0:1, rows] + rtr[2, 0:1, rows]
        row_total = jnp.broadcast_to(lane, (BLK, BLK)).T[:, 0:1]
        wide = tokf[rows, :].astype(F32)
        scale = lax.rsqrt(jnp.mean(wide * wide, axis=1, keepdims=True) + EPSILON)
        made = acc[m, me.x, part, :] + r1[0, m, me.x, part, :].astype(F32) + r2[0, m, 0, part, :].astype(F32)
        own_tok = tokf[rows, own_cols].astype(F32)
        back = scale * gf[0:1, own_cols] * made - own_tok * (scale * scale * scale * row_total / D)
        tgrad[rows, :] = (hgrad[rows, :] + back).astype(BF)
        gbuf[slot_here, 0:8, :] += jnp.broadcast_to(jnp.sum(own_tok * scale * made, axis=0, keepdims=True), (8, CB))
        return carry

    lax.fori_loop(0, T // BLK, token_rows, 0)
    gain_copies = []
    for n, peer in enumerate(me.group()):
        copy = send(gbuf.at[slot_here], gbuf.at[slot_here], gs_s.at[n], gs_r.at[n], peer)
        copy.start()
        gain_copies.append(copy)
    while taken[0] < len(order):
        take()
    for copy in gain_copies:
        copy.wait()
    both = gbuf[0]
    for n in range(1, me.dp * me.wid):
        both = both + gbuf[n]
    gsum[...] = both
    for ch, col, width in order:
        for k in range(1, me.wid):
            rs_z(ch, col, width, 0, k).wait_recv()
    for n in range(len(order) - 4, len(order)):
        rs_free(*order[n], n % 4)
    for ch, col, width in order:
        for j in range(1, me.dp):
            rs_y(ch, col, width, j).wait_send()


def final_kernel(
    cfg, z_h, layer_in, tgrad_in, gsum,
    layer_out, tgrad, one, two, o_q, o_k, o_v, o_h, o_b, o_o, o_g, o_u, o_d,
    zbuf, total, gb, loads, stores, through,
):
    HD, FL, RS, wid = cfg["HD"], cfg["FL"], cfg["RS"], cfg["sizes"]["wid"]
    FB = 5 * HD
    targets = [(o_g, FB, FL), (o_u, FB + FL, FL), (o_d, FB + 2 * FL, FL), (o_q, 0, HD), (o_k, HD, HD), (o_v, 2 * HD, HD)]
    targets += [(o_h, 3 * HD, HD), (o_o, 4 * HD, HD), (None, FB + 3 * FL, BLK)]
    passed = [
        pltpu.make_async_copy(layer_in, layer_out, through.at[0]),
        pltpu.make_async_copy(tgrad_in, tgrad, through.at[1]),
        pltpu.make_async_copy(gsum, gb, through.at[2]),
    ]
    copies = [
        pltpu.make_async_copy(z_h.at[:, :, pl.ds(col, w)], zbuf.at[:, :, pl.ds(col, w)], loads.at[i])
        for i, (_, col, w) in enumerate(targets)
    ]
    for copy in copies + passed:
        copy.start()
    written = []
    for i, (out, col, w) in enumerate(targets):
        copies[i].wait()
        value = zbuf[0, :, col : col + w].astype(F32)
        for k in range(1, wid):
            value = value + zbuf[k, :, col : col + w].astype(F32)
        if out is None:
            o_b[...] = value[:, 0 : o_b.shape[1]]
        else:
            total[:, col : col + w] = value
            copy = pltpu.make_async_copy(total.at[:, pl.ds(col, w)], out, stores.at[i])
            copy.start()
            written.append(copy)
    passed[2].wait()
    one[...] = gb[0:1, :]
    two[...] = gb[8:9, :]
    for copy in passed[:2] + written:
        copy.wait()


def solution(mesh):
    names = tuple(mesh.axis_names)
    sizes = {n: mesh.shape[n] for n in names}
    dp, wid = sizes["dp"], sizes["wid"]
    assert sizes["hid"] == 4

    def shards(
        tokens, cotangent, lengths, keep, norm_one, w_query, w_key, w_value, w_house, w_beta, w_out, norm_two,
        w_gate, w_up, w_down,
    ):
        micro, rows, CB = tokens.shape
        T, D, HD, FL, RS = micro * rows, CB * 4, w_query.shape[1], w_gate.shape[1], w_query.shape[0]
        HL, NB, FW = HD // BLK, T // BUF, 512
        U, NF, DR = NB * HL, 3 * FL // FW, D // dp
        CT = 5 * HD + 3 * FL + BLK
        heads = w_beta.shape[1]
        cfg = dict(names=names, sizes=sizes, T=T, D=D, CB=CB, HL=HL, HD=HD, FL=FL, RS=RS, FW=FW, across=[4, 5])
        gains = jnp.concatenate([jnp.broadcast_to(g, (8, CB)) for g in (norm_one, norm_two)], axis=0).astype(F32)
        sd = jax.ShapeDtypeStruct
        nch = 6 + NF
        vm = pltpu.VMEM
        unit = lambda t: vm((U, BUF, BLK), t)
        pair = vm((NB, 2, BUF, CB), BF)
        outs = pl.pallas_call(
            functools.partial(layer_kernel, cfg),
            out_shape=(
                sd((T, CB), BF), sd((T, CB), BF), sd((16, CB), F32),
                sd((D, CT), BF), sd((dp - 1, DR, CT), BF), sd((wid, RS, CT), BF), sd((U, NRES, BLK, BLK), BF),
            ),
            in_specs=[SM, VM] + [ANY] * 12,
            out_specs=(VM,) * 3 + (ANY,) * 4,
            scratch_shapes=[
                vm((D, CT), BF), *[vm((T, D), BF)] * 6, vm((T, HD), BF), *[vm((T, FL), BF)] * 3,
                *[unit(BF)] * 4, unit(F32), unit(BF), vm((U, 3, BLK, BLK), BF), vm((T, BLK), F32), vm((T, BLK), F32), vm((T, BLK), BF),
                vm((16, D), F32), vm((2, NRES, BLK, BLK), BF),
                pair, vm((2, NB, 2, BUF, CB), BF), pair, vm((2, NB, 2, BUF, CB), BF), vm((NB, 2, BUF, CB), F32),
                vm((NB, BUF, CB), BF), vm((NB, BUF, CB), BF), vm((T, CB), F32), vm((T, CB), F32),
                vm((2, 4, CB, FW), BF),
                vm((8, T), F32), vm((3, 8, T), F32), vm((T, BLK), F32), vm((dp * wid, 16, CB), F32),
                DMA((3,)), DMA((9,)), DMA((3, 3)), DMA((3, 3)), *[DMA((nch + len(cfg["across"]) * (dp - 1), 2, wid))] * 2,
                DMA((nch, wid, dp - 1)), DMA((nch, wid, dp - 1)),
                *[DMA((4, NB, 2))] * 4, *[DMA((2, NB, 2))] * 2, DMA((2,)), DMA((2, 4)),
                DMA((nch, dp - 1)), DMA((nch, dp - 1)), DMA((nch, wid - 1)), DMA((nch, wid - 1)), DMA((nch,)),
                DMA((2,)), DMA((3,)), DMA((3,)), DMA((dp * wid - 1,)), DMA((dp * wid - 1,)),
            ],
            compiler_params=pltpu.CompilerParams(
                collective_id=0, has_side_effects=True, vmem_limit_bytes=cfg.get("limit", 63 << 20)
            ),
            name="layer",
        )(
            lengths.reshape(NB, lengths.shape[2]), keep.reshape(NB, 1, BUF), tokens.reshape(T, CB),
            cotangent.reshape(T, CB), gains, w_query, w_key, w_value, w_house,
            jnp.pad(w_beta, ((0, 0), (0, BLK - heads))), w_out.T, w_gate, w_up, w_down.T,
        )
        done = pl.pallas_call(
            functools.partial(final_kernel, cfg),
            out_shape=(
                sd((T, CB), BF), sd((T, CB), BF), sd((1, CB), F32), sd((1, CB), F32),
                *[sd((RS, HD), F32)] * 4, sd((RS, heads), F32), sd((RS, HD), F32), *[sd((RS, FL), F32)] * 3,
            ),
            in_specs=[ANY] * 4,
            out_specs=(ANY, ANY, VM, VM) + (ANY,) * 4 + (VM,) + (ANY,) * 4,
            scratch_shapes=[
                vm((wid, RS, CT), BF), vm((RS, CT), F32), vm((16, CB), F32), DMA((9,)), DMA((9,)), DMA((3,)),
            ],
            compiler_params=pltpu.CompilerParams(vmem_limit_bytes=32 << 20),
            name="final",
        )(outs[5], outs[0], outs[1], outs[2])
        layer_out, tgrad, one, two, gq, gk, gv, gh, gb, go, g_gate, g_up, g_down = done
        return (
            layer_out.reshape(tokens.shape), tgrad.reshape(tokens.shape), one, gq, gk, gv, gh, gb, go.T, two,
            g_gate, g_up, g_down.T,
        )

    rows = P(("dp", "wid"), "hid")
    cols = P("hid", ("dp", "wid"))
    wide = P(None, ("dp", "wid"), "hid")
    gain = P(None, "hid")
    return jax.shard_map(
        shards,
        mesh=mesh,
        in_specs=(
            wide, wide, P(None, ("dp", "wid"), None), P(None, ("dp", "wid")), gain, rows, rows, rows, rows, rows,
            cols, gain, rows, rows, cols,
        ),
        out_specs=(wide, wide, gain, rows, rows, rows, rows, rows, cols, gain, rows, rows, cols),
        check_vma=False,
    )
```

```python
import functools
import math

import jax
import jax.numpy as jnp
from jax import lax
from jax.experimental import pallas as pl
from jax.experimental.pallas import tpu as pltpu
from jax.sharding import PartitionSpec as P

BLK = 128
BUF = 384
EPSILON = 1e-06
F32 = jnp.float32
BF = jnp.bfloat16
MESH = pl.DeviceIdType.MESH
ANY = pl.BlockSpec(memory_space=pl.ANY)
VM = pl.BlockSpec(memory_space=pltpu.VMEM)
SM = pl.BlockSpec(memory_space=pltpu.SMEM)
DMA = pltpu.SemaphoreType.DMA
NRES = 27


def _dot(a,b,ca,cb): return lax.dot_general(a,b,(((ca,),(cb,)),((),())),preferred_element_type=F32)
def nn(a,b): return _dot(a.astype(BF),b.astype(BF),1,0)
def nt(a,b): return _dot(a.astype(BF),b.astype(BF),1,1)
def tn(a,b): return _dot(a.astype(BF),b.astype(BF),0,0)
def split(a):
    hi=a.astype(BF); return hi,(a-hi.astype(F32)).astype(BF)
def nn3(a,b):
    ah,al=split(a); bh,bl=split(b)
    return _dot(ah,bh,1,0)+(_dot(ah,bl,1,0)+_dot(al,bh,1,0))
INV=nn3
def iotas():
    return lax.broadcasted_iota(jnp.int32,(BLK,BLK),0), lax.broadcasted_iota(jnp.int32,(BLK,BLK),1)
def tri_inverse(inners, betas, row, col, between):
    first=((row>>1)==(col>>1))&(row>col)
    xs=[]
    for inner,beta_col in zip(inners,betas):
        diag=jnp.where(row==col, beta_col, 0.0)
        beta_lane=jnp.sum(diag,axis=0,keepdims=True)
        xs.append(diag-jnp.where(first, inner*beta_col*beta_lane, 0.0))
    lb=1
    while (1<<lb)<BLK:
        m=((row>>(lb+1))==(col>>(lb+1)))&((row>>lb)>(col>>lb))
        half=[INV(x,jnp.where(m,inner,0.0)) for x,inner in zip(xs,inners)]
        xs=[x-INV(y,x) for x,y in zip(xs,half)]
        between(lb)
        lb+=1
    return xs
def masks(a,c,e0,e1,keep_row,row,col):
    qp=row+BLK*a; kp=col+BLK*c
    segq=(qp>=e0).astype(jnp.int32)+(qp>=e1).astype(jnp.int32)
    segk=(kp>=e0).astype(jnp.int32)+(kp>=e1).astype(jnp.int32)
    ok=(segq==segk)
    if a==c: return ok&(row>=col)&((keep_row==1)|(row==col))
    return ok&(keep_row==1)
def fwd_unit(q,k,v,h,X,keep,e0,e1):
    nb=len(q); row,col=iotas(); le=row>=col; st=row>col
    A1,L,W,R,Qm,Km=[],[],[],[],[],[]
    for a in range(nb):
        x=X[a]
        a1=jnp.where(le,nt(q[a],h[a]),0.0).astype(BF)
        w=jnp.where(st,nt(h[a],k[a]),0.0).astype(BF)
        l=nn(a1,x).astype(BF); r=nn(x,w).astype(BF)
        A1.append(a1);W.append(w);L.append(l);R.append(r)
        Qm.append((q[a].astype(F32)-nn(l,h[a])).astype(BF))
        Km.append((k[a].astype(F32)-tn(r,h[a])).astype(BF))
    scale=1.0/math.sqrt(BLK)
    S={}
    for a in range(nb):
        S[a,a]=nt(q[a],k[a])-nn(L[a],W[a])
    S[1,0]=nt(Qm[1],Km[0]); S[2,1]=nt(Qm[2],Km[1])
    u=nt(Qm[2],h[1]).astype(BF); ux=nn(u,X[1]).astype(BF)
    cq=(Qm[2].astype(F32)-nn(ux,h[1])).astype(BF)
    S[2,0]=nt(cq,Km[0])
    P={}; out=[]
    for a in range(nb):
        sc={c:jnp.where(masks(a,c,e0,e1,keep[c],row,col),S[a,c]*scale,-1e30) for c in range(a+1)}
        top=jnp.max(sc[0],axis=1,keepdims=True)
        for c in range(1,a+1): top=jnp.maximum(top,jnp.max(sc[c],axis=1,keepdims=True))
        ex={c:jnp.exp(sc[c]-top) for c in sc}
        tot=sum(jnp.sum(e,axis=1,keepdims=True) for e in ex.values())
        inv=1.0/tot
        o=0.0
        for c in sc:
            P[a,c]=(ex[c]*inv).astype(BF); o=o+nn(P[a,c],v[c])
        out.append(o)
    res=A1+L+W+R+Qm+Km+[u,ux,cq]+[P[0,0],P[1,0],P[1,1],P[2,0],P[2,1],P[2,2]]
    return out,res
def bwd_unit(q,k,v,h,do,X,res):
    nb=3; row,col=iotas(); le=row>=col; st=row>col
    A1,L,W,R,Qm,Km=[res[3*i:3*i+3] for i in range(6)]
    u,ux,cq=res[18:21]; pl_=res[21:27]
    P={(0,0):pl_[0],(1,0):pl_[1],(1,1):pl_[2],(2,0):pl_[3],(2,1):pl_[4],(2,2):pl_[5]}
    scale=1.0/math.sqrt(BLK)
    G={}; dv=[0.0]*nb
    for a in range(nb):
        dp={c:nt(do[a],v[c]) for c in range(a+1)}
        delta=sum(jnp.sum(P[a,c].astype(F32)*dp[c],axis=1,keepdims=True) for c in range(a+1))
        for c in range(a+1):
            G[a,c]=(P[a,c].astype(F32)*(dp[c]-delta)*scale).astype(BF)
            dv[c]=dv[c]+tn(P[a,c],do[a])
    dq=[nn(G[a,a],k[a]) for a in range(nb)]
    dk=[tn(G[a,a],q[a]) for a in range(nb)]
    dL=[-nt(G[a,a],W[a]) for a in range(nb)]
    dW=[-tn(L[a],G[a,a]) for a in range(nb)]
    dh=[0.0]*nb; dX=[0.0]*nb
    dcq=nn(G[2,0],Km[0]).astype(BF)
    dQm=[None, nn(G[1,0],Km[0]), nn(G[2,1],Km[1])+dcq.astype(F32)]
    dKm=[tn(G[1,0],Qm[1])+tn(G[2,0],cq), tn(G[2,1],Qm[2]), None]
    dux=(-nt(dcq,h[1])).astype(BF)
    dh[1]=dh[1]-tn(ux,dcq)
    du=nt(dux,X[1]).astype(BF)
    dX[1]=dX[1]+tn(u,dux)
    dQm[2]=dQm[2]+nn(du,h[1])
    dh[1]=dh[1]+tn(du,Qm[2])
    dbeta=[]
    for a in range(nb):
        if dQm[a] is not None:
            d_=dQm[a].astype(BF)
            dq[a]=dq[a]+d_.astype(F32); dL[a]=dL[a]-nt(d_,h[a]); dh[a]=dh[a]-tn(L[a],d_)
        if dKm[a] is not None:
            d_=dKm[a].astype(BF)
            dk[a]=dk[a]+d_.astype(F32); dR=(-nt(h[a],d_)).astype(BF); dh[a]=dh[a]-nn(R[a],d_)
            dX[a]=dX[a]+nt(dR,W[a]); dW[a]=dW[a]+tn(X[a],dR)
        dl=dL[a].astype(BF)
        dA=jnp.where(le,nt(dl,X[a]),0.0).astype(BF)
        dX[a]=dX[a]+tn(A1[a],dl)
        dw=jnp.where(st,dW[a],0.0).astype(BF)
        dh[a]=dh[a]+nn(dw,k[a]); dk[a]=dk[a]+tn(dw,h[a])
        dq[a]=dq[a]+nn(dA,h[a]); dh[a]=dh[a]+tn(dA,q[a])
        dM=nt(tn(X[a],dX[a]),X[a])
        dn=jnp.where(st,-dM,0.0).astype(BF)
        dh[a]=dh[a]+nn(dn,h[a])+tn(dn,h[a])
        dbeta.append(jnp.sum(jnp.where(row==col,dM,0.0),axis=1,keepdims=True))
    return dq,dk,dv,dh,dbeta


def spans(rows, step):
    return pl.ds(pl.multiple_of(rows, step), step)


class Place:
    def __init__(self, names, sizes):
        self.names, self.sizes = names, sizes
        self.d, self.h, self.w = (lax.axis_index(n) for n in ("dp", "hid", "wid"))
        self.dp, self.wid = sizes["dp"], sizes["wid"]
        self.c = lax.rem(self.h, 2)
        self.x = lax.div(self.h, 2)
        self.sib = self.at(h=self.h + 1 - 2 * self.c)
        self.xpeer = self.at(h=lax.rem(self.h + 2, 4))

    def at(self, d=None, h=None, w=None):
        where = {"dp": self.d if d is None else d, "hid": self.h if h is None else h, "wid": self.w if w is None else w}
        return tuple(where[n] for n in self.names)

    def greet(self, peers):
        barrier = pltpu.get_barrier_semaphore()
        for peer in peers:
            pl.semaphore_signal(barrier, inc=1, device_id=peer, device_id_type=MESH)
        pl.semaphore_wait(barrier, len(peers))

    def dp_peer(self, j):
        return self.at(d=lax.rem(self.d + j, self.dp))

    def wid_peer(self, k):
        return self.at(w=lax.rem(self.w + k, self.wid))

    def hid_peer(self, k):
        return self.at(h=lax.rem(self.h + k, 4))

    def group(self):
        return [
            self.at(d=lax.rem(self.d + i, self.dp), w=lax.rem(self.w + k, self.wid))
            for i in range(self.dp)
            for k in range(self.wid)
            if i + k > 0
        ]


def send(src, dst, sent, got, peer):
    return pltpu.make_async_remote_copy(
        src_ref=src, dst_ref=dst, send_sem=sent, recv_sem=got, device_id=peer, device_id_type=MESH
    )


class Gather:
    def __init__(self, me, rows, full, col, width, ch, sz, rz, sy, ry):
        self.me, self.rows, self.full, self.ch = me, rows, full, ch
        self.col, self.width = col, width
        self.sz, self.rz, self.sy, self.ry = sz, rz, sy, ry

    def piece(self, d, o):
        return self.full.at[
            pl.ds(pl.multiple_of((d * self.me.wid + o) * self.rows, 16), self.rows), pl.ds(self.col, self.width)
        ]

    def origin(self, way, hop):
        return lax.clamp(0, self.me.w - way * hop, self.me.wid - 1)

    def zcopy(self, way, hop, sem):
        me, side = self.me, (way + 1) // 2
        part = self.piece(me.d, self.origin(way, hop))
        return send(
            part, part, self.sz.at[self.ch, side, sem], self.rz.at[self.ch, side, sem],
            me.at(w=lax.clamp(0, me.w + way, me.wid - 1)),
        )

    def ycopy(self, d, o, j):
        part = self.piece(d, o)
        return send(part, part, self.sy.at[self.ch, o, j - 1], self.ry.at[self.ch, o, j - 1], self.me.dp_peer(j))

    def has_next(self, way):
        return self.me.w < self.me.wid - 1 if way == 1 else self.me.w > 0

    def has_piece(self, way, hop):
        return self.me.w - hop >= 0 if way == 1 else self.me.w + hop < self.me.wid

    def start_z(self):
        for way in (1, -1):

            @pl.when(self.has_next(way))
            def _():
                self.zcopy(way, 0, 0).start()

    def start_y(self):
        for j in range(1, self.me.dp):
            self.ycopy(self.me.d, self.me.w, j).start()

    def hop(self, hop):
        me = self.me
        for way in (1, -1):

            @pl.when(self.has_piece(way, hop))
            def _():
                self.zcopy(way, hop, hop - 1).wait_recv()

                @pl.when(self.has_next(way))
                def _():
                    self.zcopy(way, hop, hop).start()

                for j in range(1, me.dp):
                    self.ycopy(me.d, self.origin(way, hop), j).start()

    def finish(self):
        me = self.me
        for j in range(1, me.dp):
            for o in range(me.wid):
                self.ycopy(lax.rem(me.d + me.dp - j, me.dp), o, j).wait_recv()

    def drain_z(self):
        me = self.me
        for way in (1, -1):
            for hop in range(me.wid):

                @pl.when(self.has_piece(way, hop) & self.has_next(way))
                def _():
                    self.zcopy(way, hop, hop).wait_send()

    def drain(self):
        self.drain_z()
        for j in range(1, self.me.dp):
            for o in range(self.me.wid):
                self.ycopy(self.me.d, o, j).wait_send()


class Line(Gather):
    def __init__(self, d, *args):
        super().__init__(*args)
        self.group = d

    def zcopy(self, way, hop, sem):
        me, side = self.me, (way + 1) // 2
        part = self.piece(self.group, self.origin(way, hop))
        return send(
            part, part, self.sz.at[self.ch, side, sem], self.rz.at[self.ch, side, sem],
            me.at(w=lax.clamp(0, me.w + way, me.wid - 1)),
        )

    def hop(self, hop):
        for way in (1, -1):

            @pl.when(self.has_piece(way, hop))
            def _():
                self.zcopy(way, hop, hop - 1).wait_recv()

                @pl.when(self.has_next(way))
                def _():
                    self.zcopy(way, hop, hop).start()


class Across(Gather):
    def __init__(self, extra, *args):
        super().__init__(*args)
        me, rows, full, col, width, ch = args[:6]
        self.lines = [
            Line(lax.rem(me.d + me.dp - j, me.dp), me, rows, full, col, width, ch if j == 0 else extra + j - 1, *args[6:])
            for j in range(me.dp)
        ]

    def start_z(self):
        self.lines[0].start_z()

    def hop(self, hop):
        me = self.me
        if hop == 0:
            for j in range(1, me.dp):
                self.ycopy(lax.rem(me.d + me.dp - j, me.dp), me.w, j).wait_recv()
                self.lines[j].start_z()
        else:
            for line in self.lines:
                line.hop(hop)

    def finish(self):
        pass

    def drain(self):
        for line in self.lines:
            line.drain_z()
        for j in range(1, self.me.dp):
            self.ycopy(self.me.d, self.me.w, j).wait_send()


def column(values, lane_index):
    lanes = lax.broadcasted_iota(jnp.int32, values.shape, 1)
    return jnp.sum(jnp.where(lanes == lane_index, values, 0.0), axis=1, keepdims=True)


def layer_kernel(
    cfg, lens, keep, tok, cot, gains, w_q, w_k, w_v, w_h, w_b, w_o, w_g, w_u, w_d,
    layer_out, tgrad, gsum, g_h, ry_h, z_h, zt_h, res_h,
    W, tokf, cotf, n1, n2, hlow, ng, mix, act, gg, ug, qs, ks, vs, hs, hraw, mgrad, xs, beta, dbeta, dB, gf, resb,
    s1, r1, s2, r2, acc, t2, q2, hidown, hgrad, stage, rts, rtr, rt, gbuf,
    local, own, hx_s, hx_r, sz, rz, sy, ry, s1s, s1r, s2s, s2r, s3s, s3r, ress, stages,
    ys, yr, zs, zr, zo, ld, rs_s, rs_r, gs_s, gs_r,
):
    me = Place(cfg["names"], cfg["sizes"])
    T, D, CB, HL, HD, FL, RS = (cfg[k] for k in ("T", "D", "CB", "HL", "HD", "FL", "RS"))
    FW = cfg["FW"]
    NF = 3 * FL // FW
    FB = 5 * HD
    BC = FB + 3 * FL
    GC, UC, DC, OC = FB, FB + FL, FB + 2 * FL, 4 * HD
    NB, U, DR = T // BUF, T // BUF * HL, RS * me.wid
    c = me.c
    own_cols = pl.ds(pl.multiple_of(me.h * CB, BLK), CB)
    own_rows = pl.ds(pl.multiple_of((me.d * me.wid + me.w) * RS, 16), RS)
    me.greet(me.group() + [me.hid_peer(k) for k in range(1, 4)])

    places = [(w_h, 3 * HD), (w_b, BC), (w_q, 0), (w_k, HD), (w_v, 2 * HD), (w_o, OC), (w_g, GC), (w_u, UC), (w_d, DC)]
    mine = [
        pltpu.make_async_copy(ref, W.at[own_rows, pl.ds(col, ref.shape[1])], own.at[i])
        for i, (ref, col) in enumerate(places)
    ]
    hid = []
    for i, (src, dst) in enumerate(((tok, tokf), (gains, gf), (cot, cotf))):
        here = pltpu.make_async_copy(src, dst.at[:, own_cols], local.at[i])
        away = [
            send(src, dst.at[:, own_cols], hx_s.at[i, k - 1], hx_r.at[i, k - 1], me.hid_peer(k)) for k in range(1, 4)
        ]
        hid.append([here] + away)
    for copy in mine[:6]:
        copy.start()
    for i in range(2):
        for copy in hid[i]:
            copy.start()
    for copy in mine[6:]:
        copy.start()
    sems = (sz, rz, sy, ry)
    first = [
        Gather(me, RS, W, col, ref.shape[1], i, *sems) for i, (ref, col) in enumerate(places[:6])
    ]

    def late(i):
        args = (me, RS, W, FB + i * FW, FW, 6 + i, *sems)
        if i in cfg["across"]:
            return Across(6 + NF + cfg["across"].index(i) * (me.dp - 1), *args)
        return Gather(*args)

    NG = len(first) + NF

    def chunk(n):
        return first[n] if n < len(first) else late(n - len(first))

    def begin(n):
        if n < NG:
            if n < len(first):
                mine[n].wait()
            elif n == len(first):
                for copy in mine[6:]:
                    copy.wait()
            chunk(n).start_z()
            chunk(n).start_y()

    events = [
        (k - hop + 1, hop) for k in range(NG + me.wid - 2) for hop in range(1, me.wid) if 0 <= k - hop + 1 < NG
    ]
    for i in cfg["across"]:
        events.insert(events.index((6 + i, 1)), (6 + i, 0))

    def advance(count):
        for _ in range(min(count, len(events))):
            n, hop = events.pop(0)
            chunk(n).hop(hop)

    for n in range(NG):
        begin(n)
    for copy in hid[2]:
        copy.start()
    for i in range(2):
        for copy in hid[i]:
            copy.wait()
    RB = 32

    def rows_of(m):
        return pl.ds(pl.multiple_of(m * BUF, BLK), BUF)

    def norm(src, dst, gain, base):
        def body(i, carry):
            rows = spans(base + i * RB, RB)
            wide = src[rows, :].astype(F32)
            scale = lax.rsqrt(jnp.mean(wide * wide, axis=1, keepdims=True) + EPSILON)
            dst[rows, :] = (wide * scale * gf[gain : gain + 1, :]).astype(BF)
            return carry

        lax.fori_loop(0, BUF // RB, body, 0)

    for m in range(NB):
        norm(tokf, n1, 0, m * BUF)

    def project(a):
        for m in range(NB):
            rows = n1[m * BUF : (m + 1) * BUF, :]
            made = nn(rows, W[:, a * HD : (a + 1) * HD])
            for hd in range(HL):
                part = made[:, hd * BLK : (hd + 1) * BLK]
                u = m * HL + hd
                if a < 3:
                    (qs, ks, vs)[a][u] = part.astype(BF)
                else:
                    hraw[u] = part
                    hs[u] = (part * lax.rsqrt(jnp.sum(part * part, axis=1, keepdims=True) + EPSILON)).astype(BF)
            if a == 3:
                beta[m * BUF : (m + 1) * BUF, :] = 2.0 * jax.nn.sigmoid(nn(rows, W[:, BC:]))

    advance(9)
    first[0].finish()
    first[1].finish()
    project(3)

    def invert(hd, carry):
        row, col = iotas()
        blocks = [(m, a) for m in range(NB) for a in range(3)]
        parts = [hs[m * HL + hd, a * BLK : (a + 1) * BLK, :] for m, a in blocks]
        strengths = [column(beta[m * BUF + a * BLK : m * BUF + (a + 1) * BLK, :], hd) for m, a in blocks]

        def between(level):
            for i in range(HL):
                later = slots[i].get(level, [])
                if later:

                    @pl.when(hd == i)
                    def _():
                        for n, hop in later:
                            chunk(n).hop(hop)

        made = tri_inverse([nt(part, part) for part in parts], strengths, row, col, between)
        for (m, a), x in zip(blocks, made):
            xs[m * HL + hd, a] = x.astype(BF)
        return carry

    advance(2)
    slots = [{level: [events.pop(0)] for level in (2, 4, 6) if events} for _ in range(HL)]
    lax.fori_loop(0, HL, invert, 0)
    for a in range(3):
        first[2 + a].finish()
        project(a)
        advance(2)

    def attend(u, carry):
        m, hd = lax.div(u, HL), lax.rem(u, HL)
        slot = lax.rem(u, 2)
        e0 = lens[m, 0]
        e1 = e0 + lens[m, 1]
        parts = [slice(a * BLK, (a + 1) * BLK) for a in range(3)]
        keys = [keep[m, :, p] for p in parts]
        out, res = fwd_unit(
            [qs[u, p, :] for p in parts], [ks[u, p, :] for p in parts], [vs[u, p, :] for p in parts],
            [hs[u, p, :] for p in parts], [xs[u, a] for a in range(3)], keys, e0, e1,
        )
        for a in range(3):
            mix[spans(m * BUF + a * BLK, BLK), pl.ds(pl.multiple_of(hd * BLK, BLK), BLK)] = out[a].astype(BF)

        @pl.when(u >= 2)
        def _():
            pltpu.make_async_copy(resb.at[slot], res_h.at[u], ress.at[slot]).wait()

        for i, value in enumerate(res):
            resb[slot, i] = value
        pltpu.make_async_copy(resb.at[slot], res_h.at[u], ress.at[slot]).start()
        for m in range(NB):

            @pl.when(u == (m + 1) * HL - 1)
            def _():
                if m == 0:
                    first[5].finish()
                first_hop(0, m, branch(m))

            @pl.when(u == (m + 1) * HL)
            def _():
                second_hop(0, m)

        for i, (n, hop) in enumerate(during):

            @pl.when(u == i)
            def _():
                chunk(n).hop(hop)

        return carry

    def block(b):
        return pl.ds(pl.multiple_of(b * CB, BLK), CB)

    def hop1(tag, m, j):
        return send(s1.at[m, j], r1.at[tag % 3 // 2, m, j], s1s.at[tag, m, j], s1r.at[tag, m, j], me.sib)

    def hop2(tag, m, j):
        return send(s2.at[m, j], r2.at[tag, m, j], s2s.at[tag, m, j], s2r.at[tag, m, j], me.xpeer)

    def first_hop(tag, m, partial):
        for j in range(2):
            s1[m, j] = partial((1 - c) + 2 * j).astype(BF)
            hop1(tag, m, j).start()
        for j in range(2):
            acc[m, j] = partial(c + 2 * j)

    def second_hop(tag, m):
        for j in range(2):
            hop1(tag, m, j).wait()
            s2[m, j] = (acc[m, j] + r1[tag // 2, m, j].astype(F32)).astype(BF)
            hop2(tag, m, j).start()

    def total(tag, m, j):
        return s2[m, j].astype(F32) + r2[tag, m, j].astype(F32)

    def third(tag, full, m, j, core):
        part = full.at[rows_of(m), block(core + 2 * j)]
        return send(part, part, s3s.at[tag, m, j], s3r.at[tag, m, j], me.sib)

    def wait_third(tag, full, m):
        for j in range(2):
            third(tag, full, m, j, 1 - c).wait_recv()
            third(tag, full, m, j, c).wait_send()

    def branch(m):
        return lambda b: nt(mix[rows_of(m), :], W[block(b), OC : OC + HD])

    during = [events.pop(0) for _ in range(min(U, len(events)))]
    lax.fori_loop(0, U, attend, 0)
    for slot in range(2):
        pltpu.make_async_copy(resb.at[slot], res_h.at[0], ress.at[slot]).wait()
    second_hop(0, NB - 1)

    def residual(m):
        for j in range(2):
            hop2(0, m, j).wait()
            b = c + 2 * j
            hidden = tokf[rows_of(m), block(b)].astype(F32) + total(0, m, j)
            hlow[rows_of(m), block(b)] = hidden.astype(BF)
            third(0, hlow, m, j, c).start()
        hidown[rows_of(m), :] = tokf[rows_of(m), own_cols].astype(F32) + (
            s2[m, me.x].astype(F32) + r2[0, m, me.x].astype(F32)
        )

    for m in range(NB):
        residual(m)
        advance(2)
        wait_third(0, hlow, m)
        norm(hlow, n2, 8, m * BUF)
    advance(max([i + 1 for i, (n, _) in enumerate(events) if n < 6 + 2 * FL // FW], default=0))
    for copy in hid[2]:
        copy.wait()

    NT = 256
    ND = 2 * FL // FW
    for i in range(ND):
        late(i).finish()

    def ffn(m):
        def body(n, carry):
            at = pl.multiple_of(n * NT, NT)
            gate = nn(n2[rows_of(m), :], W[:, pl.ds(pl.multiple_of(GC + at, BLK), NT)])
            up = nn(n2[rows_of(m), :], W[:, pl.ds(pl.multiple_of(UC + at, BLK), NT)])
            sig = jax.nn.sigmoid(gate)
            silu = gate * sig
            cols = pl.ds(at, NT)
            act[rows_of(m), cols] = (silu * up).astype(BF)
            gg[rows_of(m), cols] = (up * sig * (1.0 + gate * (1.0 - sig))).astype(BF)
            ug[rows_of(m), cols] = silu.astype(BF)
            return carry

        lax.fori_loop(0, FL // NT, body, 0)

    def ffn_back(m):
        def body(n, carry):
            at = pl.multiple_of(n * NT, NT)
            cols = pl.ds(at, NT)
            back = nn(cotf[rows_of(m), :], W[:, pl.ds(pl.multiple_of(DC + at, BLK), NT)])
            gg[rows_of(m), cols] = (back * gg[rows_of(m), cols].astype(F32)).astype(BF)
            ug[rows_of(m), cols] = (back * ug[rows_of(m), cols].astype(F32)).astype(BF)
            return carry

        lax.fori_loop(0, FL // NT, body, 0)

    def dp_rows(j):
        return pl.ds(pl.multiple_of(lax.rem(me.d + j, me.dp) * DR, 16), DR)

    def staged(side, i, col, width):
        return pltpu.make_async_copy(
            stage.at[side, i, :, pl.ds(0, width)],
            g_h.at[pl.ds(pl.multiple_of(i * CB, BLK), CB), pl.ds(col, width)],
            stages.at[side, i],
        )

    def rs_y(ch, col, width, j):
        return send(
            g_h.at[dp_rows(j), pl.ds(col, width)], ry_h.at[j - 1, :, pl.ds(col, width)],
            ys.at[ch, j - 1], yr.at[ch, j - 1], me.dp_peer(j),
        )

    pending = []
    made_terms = [0]

    def flush():
        side, ch, col, width = pending.pop()
        for i in range(D // CB):
            staged(side, i, col, width).wait()
        for j in range(1, me.dp):
            rs_y(ch, col, width, j).start()

    def weight_term(ch, left, right, at, col, width):
        side = made_terms[0] % 2
        made_terms[0] += 1

        def body(i, carry):
            stage[side, i, :, pl.ds(0, width)] = tn(
                left[:, pl.ds(pl.multiple_of(i * CB, BLK), CB)], right[:, at : at + width]
            ).astype(BF)
            staged(side, i, col, width).start()
            return carry

        lax.fori_loop(0, D // CB, body, 0)
        if pending:
            flush()
        pending.append((side, ch, col, width))

    def ffn_terms(left, right, col):
        for n in range(FL // FW):
            weight_term(6 + (col - FB) // FW + n, left, right, n * FW, col + n * FW, FW)

    for m in range(NB):
        ffn(m)
    ffn_terms(cotf, act, DC)
    flush()
    advance(len(events))
    for i in range(ND, NF):
        late(i).finish()

    def normed_back(m):
        return lambda b: nt(gg[rows_of(m), :], W[block(b), GC : GC + FL]) + nt(
            ug[rows_of(m), :], W[block(b), UC : UC + FL]
        )

    def down(m):
        return lambda b: nt(act[rows_of(m), :], W[block(b), DC : DC + FL])

    ffn_back(0)
    first_hop(1, 0, normed_back(0))
    ffn_back(1)
    second_hop(1, 0)
    for m in range(1, NB):
        first_hop(1, m, normed_back(m))
        if m + 1 < NB:
            ffn_back(m + 1)
        second_hop(1, m)
    for g in first:
        g.drain()

    for i in range(NF):
        late(i).drain()
    ffn_terms(n2, gg, GC)
    ffn_terms(n2, ug, UC)
    flush()

    def hop2_out(m):
        return send(t2.at[m], q2.at[m], s2s.at[2, m, 0], s2r.at[2, m, 0], me.xpeer)

    for m in range(NB):
        first_hop(2, m, down(m))
    other = 1 - me.x
    for m in range(NB):
        for j in range(2):
            hop1(2, m, j).wait()
        t2[m] = (acc[m, other] + r1[1, m, other].astype(F32)).astype(BF)
        hop2_out(m).start()

    gm = W.at[0:DR, FB : FB + FW]
    peer_term = W.at[DR : 2 * DR, FB : FB + FW]
    inbox = W.at[DR : 2 * DR, FB + FW : FB + 2 * FW]

    def to_wid(slot):
        return W.at[0:DR, FB + FW + slot * FW : FB + 2 * FW + slot * FW]

    near = me.w + 1 - 2 * lax.rem(me.w, 2)
    far = 2 - 2 * lax.div(me.w, 2)
    inner = (me.w == 1) | (me.w == 2)
    outer = jnp.logical_not(inner)

    def block_rows(o, count=1):
        return pl.ds(pl.multiple_of(o * RS, 16), count * RS)

    def to_near(ch, col, width, slot):
        return send(
            to_wid(slot).at[block_rows(near), pl.ds(0, width)], z_h.at[1, :, pl.ds(col, width)],
            zs.at[ch, 0], zr.at[ch, 0], me.at(w=near),
        )

    def to_inner(ch, col, width, slot):
        return send(
            to_wid(slot).at[block_rows(far, 2), pl.ds(0, width)], zt_h.at[:, pl.ds(col, width)],
            zs.at[ch, 1], zr.at[ch, 1], me.at(w=near),
        )

    def to_far(ch, col, width, slot, i):
        return send(
            to_wid(slot).at[block_rows(far + i), pl.ds(0, width)], z_h.at[2, :, pl.ds(col, width)],
            zs.at[ch, 2 + i], zr.at[ch, 2], me.at(w=far + i),
        )

    def rs_free(ch, col, width, slot):
        to_near(ch, col, width, slot).wait_send()

        @pl.when(outer)
        def _():
            to_inner(ch, col, width, slot).wait_send()

        @pl.when(inner)
        def _():
            for i in range(2):
                to_far(ch, col, width, slot, i).wait_send()

    def rs_across(ch, col, width, slot):
        @pl.when(inner)
        def _():
            to_inner(ch, col, width, slot).wait_recv()
            load = pltpu.make_async_copy(
                zt_h.at[:, pl.ds(col, width)], inbox.at[pl.ds(0, 2 * RS), pl.ds(0, width)], ld.at[2]
            )
            load.start()
            load.wait()
            for i in range(2):
                rows = block_rows(far + i)
                to_wid(slot)[rows, 0:width] = (
                    to_wid(slot)[rows, 0:width].astype(F32) + inbox[i * RS : (i + 1) * RS, 0:width].astype(F32)
                ).astype(BF)
                to_far(ch, col, width, slot, i).start()

    def rs_end(ch, col, width):
        to_near(ch, col, width, 0).wait_recv()
        to_far(ch, col, width, 0, 0).wait_recv()

    def rs_stage(ch, col, width, slot):
        here = pltpu.make_async_copy(g_h.at[dp_rows(0), pl.ds(col, width)], gm.at[:, pl.ds(0, width)], ld.at[0])
        here.start()
        mine_out = pltpu.make_async_copy(
            to_wid(slot).at[block_rows(me.w), pl.ds(0, width)], z_h.at[0, :, pl.ds(col, width)], zo.at[ch]
        )
        for j in range(1, me.dp):
            rs_y(ch, col, width, j).wait_recv()
            there = pltpu.make_async_copy(
                ry_h.at[j - 1, :, pl.ds(col, width)], peer_term.at[:, pl.ds(0, width)], ld.at[1]
            )
            there.start()
            if j == 1:
                here.wait()
            there.wait()
            for i, o in enumerate((far, far + 1, near, me.w)):
                rows = block_rows(o)
                so_far = gm if j == 1 else to_wid(slot)
                to_wid(slot)[rows, 0:width] = (
                    so_far[rows, 0:width].astype(F32) + peer_term[rows, 0:width].astype(F32)
                ).astype(BF)
                if j == me.dp - 1:
                    if i == 1:

                        @pl.when(outer)
                        def _():
                            to_inner(ch, col, width, slot).start()

                    if i == 2:
                        to_near(ch, col, width, slot).start()
                    if i == 3:
                        mine_out.start()
        mine_out.wait()

    places_of = [(3 * HD, HD), (BC, BLK), (0, HD), (HD, HD), (2 * HD, HD), (OC, HD)]
    order = [(6 + (i + ND) % NF, FB + (i + ND) % NF * FW, FW) for i in range(NF)]
    order += [(k, *places_of[k]) for k in (5, 2, 3, 4, 0, 1)]
    taken = [0]

    def take():
        n = taken[0]
        taken[0] += 1
        if n >= 4:
            rs_free(*order[n - 4], n % 4)
        rs_stage(*order[n], n % 4)
        if n >= 1:
            rs_across(*order[n - 1], (n - 1) % 4)
        if n == len(order) - 1:
            rs_across(*order[n], n % 4)

    def spread_back(m):
        for j in range(2):
            hop2(1, m, j).wait()
            ng[rows_of(m), block(c + 2 * j)] = total(1, m, j).astype(BF)
            third(1, ng, m, j, c).start()

    def branch_back(m):
        def body(i, carry):
            rows = spans(m * BUF + i * RB, RB)
            low = hlow[rows, :].astype(F32)
            scale = lax.rsqrt(jnp.mean(low * low, axis=1, keepdims=True) + EPSILON)
            scaled = ng[rows, :].astype(F32) * gf[8:9, :]
            row_total = jnp.sum(low * scaled, axis=1, keepdims=True)
            cube = scale * scale * scale * row_total / D
            low_own = hlow[rows, own_cols].astype(F32)
            ng_own = ng[rows, own_cols].astype(F32)
            hgrad[rows, :] = (
                cotf[rows, own_cols].astype(F32) + scale * gf[8:9, own_cols] * ng_own - low_own * cube
            )
            gbuf[slot_here, 8:16, :] += jnp.broadcast_to(
                jnp.sum(low_own * scale * ng_own, axis=0, keepdims=True), (8, CB)
            )
            ng[rows, :] = (cotf[rows, :].astype(F32) + scale * scaled - low * cube).astype(BF)
            return carry

        lax.fori_loop(0, BUF // RB, body, 0)
        made = nn(ng[rows_of(m), :], W[:, OC : OC + HD])
        for hd in range(HL):
            mgrad[m * HL + hd] = made[:, hd * BLK : (hd + 1) * BLK].astype(BF)

    slot_here = me.d * me.wid + me.w
    gbuf[slot_here] = jnp.zeros((16, CB), F32)
    dbeta[...] = jnp.zeros_like(dbeta)
    dA = n2

    def fetch_res(u):
        slot = lax.rem(u, 2)
        return pltpu.make_async_copy(res_h.at[u], resb.at[slot], ress.at[slot])

    fetch_res(0).start()

    def attend_back(u, carry):
        m, hd = lax.div(u, HL), lax.rem(u, HL)
        slot = lax.rem(u, 2)
        parts = [slice(a * BLK, (a + 1) * BLK) for a in range(3)]

        fetch_res(u).wait()

        @pl.when(u + 1 < U)
        def _():
            fetch_res(u + 1).start()

        dq, dk, dv, dh, db = bwd_unit(
            [qs[u, p, :] for p in parts], [ks[u, p, :] for p in parts], [vs[u, p, :] for p in parts],
            [hs[u, p, :] for p in parts], [mgrad[u, p, :] for p in parts], [xs[u, a] for a in range(3)],
            [resb[slot, i] for i in range(NRES)],
        )
        for a in range(3):
            rows = spans(m * BUF + a * BLK, BLK)
            for n, value in enumerate((dq[a], dk[a], dv[a])):
                dA[rows, pl.ds(pl.multiple_of(n * HD + hd * BLK, BLK), BLK)] = value.astype(BF)
            raw = hraw[u, parts[a], :]
            scale = lax.rsqrt(jnp.sum(raw * raw, axis=1, keepdims=True) + EPSILON)
            along = jnp.sum(raw * dh[a], axis=1, keepdims=True)
            dA[rows, pl.ds(pl.multiple_of(3 * HD + hd * BLK, BLK), BLK)] = (
                scale * dh[a] - raw * (scale * scale * scale * along)
            ).astype(BF)
            strength = column(beta[rows, :], hd)
            pull = db[a] * (1.0 / jnp.maximum(strength, 1e-30) - 0.5)
            lanes = lax.broadcasted_iota(jnp.int32, (BLK, BLK), 1)
            dbeta[rows, :] += jnp.where(lanes == hd, pull, 0.0)

        return carry

    take()
    for m in range(NB):
        spread_back(m)
        wait_third(1, ng, m)
        branch_back(m)
        if m == 0:
            take()
    lax.fori_loop(0, U, attend_back, 0)
    dB[...] = dbeta[...].astype(BF)
    weight_term(5, ng, mix, 0, OC, HD)
    take()
    for a in range(3):
        weight_term(2 + a, n1, dA, a * HD, a * HD, HD)
    weight_term(0, n1, dA, 3 * HD, 3 * HD, HD)
    weight_term(1, n1, dB, 0, BC, BLK)
    flush()

    rt[...] = jnp.zeros_like(rt)

    def first_back(m):
        def partial(b):
            made = nt(dA[rows_of(m), :], W[block(b), 0 : 4 * HD]) + nt(dB[rows_of(m), :], W[block(b), BC:])
            along = jnp.sum(made * tokf[rows_of(m), block(b)].astype(F32) * gf[0:1, block(b)], axis=1, keepdims=True)
            rt[rows_of(m), :] += jnp.broadcast_to(along, (BUF, BLK))
            return made

        return partial

    for m in range(NB):
        hop2_out(m).wait()
        layer_out[rows_of(m), :] = (
            hidown[rows_of(m), :] + (acc[m, me.x] + r1[1, m, me.x].astype(F32) + q2[m].astype(F32))
        ).astype(BF)
    for m in range(NB):
        first_hop(3, m, first_back(m))
    for i in range(T // BLK):
        rts[:, i * BLK : (i + 1) * BLK] = rt[i * BLK : (i + 1) * BLK, :].T[0:8, :]
    rt_copies = [send(rts, rtr.at[k - 1], rs_s.at[k - 1], rs_r.at[k - 1], me.hid_peer(k)) for k in range(1, 4)]
    for copy in rt_copies:
        copy.start()

    def hop2_in(m):
        return send(t2.at[m], r2.at[0, m, 0], s2s.at[3, m, 0], s2r.at[3, m, 0], me.xpeer)

    for m in range(NB):
        for j in range(2):
            hop1(3, m, j).wait()
        t2[m] = (acc[m, other] + r1[0, m, other].astype(F32)).astype(BF)
        hop2_in(m).start()

    take()
    for m in range(NB):
        hop2_in(m).wait()
    for copy in rt_copies:
        copy.wait()

    def token_rows(i, carry):
        rows = spans(i * BLK, BLK)
        m = lax.div(i, BUF // BLK)
        part = spans(lax.rem(i, BUF // BLK) * BLK, BLK)
        lane = rts[0:1, rows] + rtr[0, 0:1, rows] + rtr[1, 0:1, rows] + rtr[2, 0:1, rows]
        row_total = jnp.broadcast_to(lane, (BLK, BLK)).T[:, 0:1]
        wide = tokf[rows, :].astype(F32)
        scale = lax.rsqrt(jnp.mean(wide * wide, axis=1, keepdims=True) + EPSILON)
        made = acc[m, me.x, part, :] + r1[0, m, me.x, part, :].astype(F32) + r2[0, m, 0, part, :].astype(F32)
        own_tok = tokf[rows, own_cols].astype(F32)
        back = scale * gf[0:1, own_cols] * made - own_tok * (scale * scale * scale * row_total / D)
        tgrad[rows, :] = (hgrad[rows, :] + back).astype(BF)
        gbuf[slot_here, 0:8, :] += jnp.broadcast_to(jnp.sum(own_tok * scale * made, axis=0, keepdims=True), (8, CB))
        return carry

    lax.fori_loop(0, T // BLK, token_rows, 0)
    gain_copies = []
    for n, peer in enumerate(me.group()):
        copy = send(gbuf.at[slot_here], gbuf.at[slot_here], gs_s.at[n], gs_r.at[n], peer)
        copy.start()
        gain_copies.append(copy)
    while taken[0] < len(order):
        take()
    for copy in gain_copies:
        copy.wait()
    both = gbuf[0]
    for n in range(1, me.dp * me.wid):
        both = both + gbuf[n]
    gsum[...] = both
    for ch, col, width in order:
        rs_end(ch, col, width)
    for n in range(len(order) - 4, len(order)):
        rs_free(*order[n], n % 4)
    for ch, col, width in order:
        for j in range(1, me.dp):
            rs_y(ch, col, width, j).wait_send()


def final_kernel(
    cfg, z_h, layer_in, tgrad_in, gsum,
    layer_out, tgrad, one, two, o_q, o_k, o_v, o_h, o_b, o_o, o_g, o_u, o_d,
    zbuf, total, gb, loads, stores, through,
):
    HD, FL, RS = cfg["HD"], cfg["FL"], cfg["RS"]
    FB = 5 * HD
    targets = [(o_g, FB, FL), (o_u, FB + FL, FL), (o_d, FB + 2 * FL, FL), (o_q, 0, HD), (o_k, HD, HD), (o_v, 2 * HD, HD)]
    targets += [(o_h, 3 * HD, HD), (o_o, 4 * HD, HD), (None, FB + 3 * FL, BLK)]
    passed = [
        pltpu.make_async_copy(layer_in, layer_out, through.at[0]),
        pltpu.make_async_copy(tgrad_in, tgrad, through.at[1]),
        pltpu.make_async_copy(gsum, gb, through.at[2]),
    ]
    copies = [
        pltpu.make_async_copy(z_h.at[:, :, pl.ds(col, w)], zbuf.at[:, :, pl.ds(col, w)], loads.at[i])
        for i, (_, col, w) in enumerate(targets)
    ]
    for copy in copies + passed:
        copy.start()
    written = []
    for i, (out, col, w) in enumerate(targets):
        copies[i].wait()
        value = zbuf[0, :, col : col + w].astype(F32)
        for k in range(1, 3):
            value = value + zbuf[k, :, col : col + w].astype(F32)
        if out is None:
            o_b[...] = value[:, 0 : o_b.shape[1]]
        else:
            total[:, col : col + w] = value
            copy = pltpu.make_async_copy(total.at[:, pl.ds(col, w)], out, stores.at[i])
            copy.start()
            written.append(copy)
    passed[2].wait()
    one[...] = gb[0:1, :]
    two[...] = gb[8:9, :]
    for copy in passed[:2] + written:
        copy.wait()


def solution(mesh):
    names = tuple(mesh.axis_names)
    sizes = {n: mesh.shape[n] for n in names}
    dp, wid = sizes["dp"], sizes["wid"]
    assert sizes["hid"] == 4 and wid == 4

    def shards(
        tokens, cotangent, lengths, keep, norm_one, w_query, w_key, w_value, w_house, w_beta, w_out, norm_two,
        w_gate, w_up, w_down,
    ):
        micro, rows, CB = tokens.shape
        T, D, HD, FL, RS = micro * rows, CB * 4, w_query.shape[1], w_gate.shape[1], w_query.shape[0]
        HL, NB, FW = HD // BLK, T // BUF, 512
        U, NF, DR = NB * HL, 3 * FL // FW, D // dp
        CT = 5 * HD + 3 * FL + BLK
        heads = w_beta.shape[1]
        cfg = dict(names=names, sizes=sizes, T=T, D=D, CB=CB, HL=HL, HD=HD, FL=FL, RS=RS, FW=FW, across=[4, 5])
        gains = jnp.concatenate([jnp.broadcast_to(g, (8, CB)) for g in (norm_one, norm_two)], axis=0).astype(F32)
        sd = jax.ShapeDtypeStruct
        nch = 6 + NF
        vm = pltpu.VMEM
        unit = lambda t: vm((U, BUF, BLK), t)
        pair = vm((NB, 2, BUF, CB), BF)
        outs = pl.pallas_call(
            functools.partial(layer_kernel, cfg),
            out_shape=(
                sd((T, CB), BF), sd((T, CB), BF), sd((16, CB), F32),
                sd((D, CT), BF), sd((dp - 1, DR, CT), BF), sd((3, RS, CT), BF), sd((2 * RS, CT), BF),
                sd((U, NRES, BLK, BLK), BF),
            ),
            in_specs=[SM, VM] + [ANY] * 12,
            out_specs=(VM,) * 3 + (ANY,) * 5,
            scratch_shapes=[
                vm((D, CT), BF), *[vm((T, D), BF)] * 6, vm((T, HD), BF), *[vm((T, FL), BF)] * 3,
                *[unit(BF)] * 4, unit(F32), unit(BF), vm((U, 3, BLK, BLK), BF), vm((T, BLK), F32), vm((T, BLK), F32), vm((T, BLK), BF),
                vm((16, D), F32), vm((2, NRES, BLK, BLK), BF),
                pair, vm((2, NB, 2, BUF, CB), BF), pair, vm((2, NB, 2, BUF, CB), BF), vm((NB, 2, BUF, CB), F32),
                vm((NB, BUF, CB), BF), vm((NB, BUF, CB), BF), vm((T, CB), F32), vm((T, CB), F32),
                vm((2, 4, CB, FW), BF),
                vm((8, T), F32), vm((3, 8, T), F32), vm((T, BLK), F32), vm((dp * wid, 16, CB), F32),
                DMA((3,)), DMA((9,)), DMA((3, 3)), DMA((3, 3)), *[DMA((nch + len(cfg["across"]) * (dp - 1), 2, wid))] * 2,
                DMA((nch, wid, dp - 1)), DMA((nch, wid, dp - 1)),
                *[DMA((4, NB, 2))] * 4, *[DMA((2, NB, 2))] * 2, DMA((2,)), DMA((2, 4)),
                DMA((nch, dp - 1)), DMA((nch, dp - 1)), DMA((nch, 4)), DMA((nch, 3)), DMA((nch,)),
                DMA((3,)), DMA((3,)), DMA((3,)), DMA((dp * wid - 1,)), DMA((dp * wid - 1,)),
            ],
            compiler_params=pltpu.CompilerParams(
                collective_id=0, has_side_effects=True, vmem_limit_bytes=cfg.get("limit", 63 << 20)
            ),
            name="layer",
        )(
            lengths.reshape(NB, lengths.shape[2]), keep.reshape(NB, 1, BUF), tokens.reshape(T, CB),
            cotangent.reshape(T, CB), gains, w_query, w_key, w_value, w_house,
            jnp.pad(w_beta, ((0, 0), (0, BLK - heads))), w_out.T, w_gate, w_up, w_down.T,
        )
        done = pl.pallas_call(
            functools.partial(final_kernel, cfg),
            out_shape=(
                sd((T, CB), BF), sd((T, CB), BF), sd((1, CB), F32), sd((1, CB), F32),
                *[sd((RS, HD), F32)] * 4, sd((RS, heads), F32), sd((RS, HD), F32), *[sd((RS, FL), F32)] * 3,
            ),
            in_specs=[ANY] * 4,
            out_specs=(ANY, ANY, VM, VM) + (ANY,) * 4 + (VM,) + (ANY,) * 4,
            scratch_shapes=[
                vm((3, RS, CT), BF), vm((RS, CT), F32), vm((16, CB), F32), DMA((9,)), DMA((9,)), DMA((3,)),
            ],
            compiler_params=pltpu.CompilerParams(vmem_limit_bytes=32 << 20),
            name="final",
        )(outs[5], outs[0], outs[1], outs[2])
        layer_out, tgrad, one, two, gq, gk, gv, gh, gb, go, g_gate, g_up, g_down = done
        return (
            layer_out.reshape(tokens.shape), tgrad.reshape(tokens.shape), one, gq, gk, gv, gh, gb, go.T, two,
            g_gate, g_up, g_down.T,
        )

    rows = P(("dp", "wid"), "hid")
    cols = P("hid", ("dp", "wid"))
    wide = P(None, ("dp", "wid"), "hid")
    gain = P(None, "hid")
    return jax.shard_map(
        shards,
        mesh=mesh,
        in_specs=(
            wide, wide, P(None, ("dp", "wid"), None), P(None, ("dp", "wid")), gain, rows, rows, rows, rows, rows,
            cols, gain, rows, rows, cols,
        ),
        out_specs=(wide, wide, gain, rows, rows, rows, rows, rows, cols, gain, rows, rows, cols),
        check_vma=False,
    )
```

```python
import functools
import math

import jax
import jax.numpy as jnp
from jax import lax
from jax.experimental import pallas as pl
from jax.experimental.pallas import tpu as pltpu
from jax.sharding import PartitionSpec as P

BLK = 128
BUF = 384
EPSILON = 1e-06
F32 = jnp.float32
BF = jnp.bfloat16
MESH = pl.DeviceIdType.MESH
ANY = pl.BlockSpec(memory_space=pl.ANY)
VM = pl.BlockSpec(memory_space=pltpu.VMEM)
SM = pl.BlockSpec(memory_space=pltpu.SMEM)
DMA = pltpu.SemaphoreType.DMA
NRES = 27


def _dot(a,b,ca,cb): return lax.dot_general(a,b,(((ca,),(cb,)),((),())),preferred_element_type=F32)
def nn(a,b): return _dot(a.astype(BF),b.astype(BF),1,0)
def nt(a,b): return _dot(a.astype(BF),b.astype(BF),1,1)
def tn(a,b): return _dot(a.astype(BF),b.astype(BF),0,0)
def split(a):
    hi=a.astype(BF); return hi,(a-hi.astype(F32)).astype(BF)
def nn3(a,b):
    ah,al=split(a); bh,bl=split(b)
    return _dot(ah,bh,1,0)+(_dot(ah,bl,1,0)+_dot(al,bh,1,0))
INV=nn3
def iotas():
    return lax.broadcasted_iota(jnp.int32,(BLK,BLK),0), lax.broadcasted_iota(jnp.int32,(BLK,BLK),1)
def tri_inverse(inners, betas, row, col, between):
    first=((row>>1)==(col>>1))&(row>col)
    xs=[]
    for inner,beta_col in zip(inners,betas):
        diag=jnp.where(row==col, beta_col, 0.0)
        beta_lane=jnp.sum(diag,axis=0,keepdims=True)
        xs.append(diag-jnp.where(first, inner*beta_col*beta_lane, 0.0))
    lb=1
    while (1<<lb)<BLK:
        m=((row>>(lb+1))==(col>>(lb+1)))&((row>>lb)>(col>>lb))
        half=[INV(x,jnp.where(m,inner,0.0)) for x,inner in zip(xs,inners)]
        xs=[x-INV(y,x) for x,y in zip(xs,half)]
        between(lb)
        lb+=1
    return xs
def masks(a,c,e0,e1,keep_row,row,col):
    qp=row+BLK*a; kp=col+BLK*c
    segq=(qp>=e0).astype(jnp.int32)+(qp>=e1).astype(jnp.int32)
    segk=(kp>=e0).astype(jnp.int32)+(kp>=e1).astype(jnp.int32)
    ok=(segq==segk)
    if a==c: return ok&(row>=col)&((keep_row==1)|(row==col))
    return ok&(keep_row==1)
def fwd_unit(q,k,v,h,X,keep,e0,e1):
    nb=len(q); row,col=iotas(); le=row>=col; st=row>col
    A1,L,W,R,Qm,Km=[],[],[],[],[],[]
    for a in range(nb):
        x=X[a]
        a1=jnp.where(le,nt(q[a],h[a]),0.0).astype(BF)
        w=jnp.where(st,nt(h[a],k[a]),0.0).astype(BF)
        l=nn(a1,x).astype(BF); r=nn(x,w).astype(BF)
        A1.append(a1);W.append(w);L.append(l);R.append(r)
        Qm.append((q[a].astype(F32)-nn(l,h[a])).astype(BF))
        Km.append((k[a].astype(F32)-tn(r,h[a])).astype(BF))
    scale=1.0/math.sqrt(BLK)
    S={}
    for a in range(nb):
        S[a,a]=nt(q[a],k[a])-nn(L[a],W[a])
    S[1,0]=nt(Qm[1],Km[0]); S[2,1]=nt(Qm[2],Km[1])
    u=nt(Qm[2],h[1]).astype(BF); ux=nn(u,X[1]).astype(BF)
    cq=(Qm[2].astype(F32)-nn(ux,h[1])).astype(BF)
    S[2,0]=nt(cq,Km[0])
    P={}; out=[]
    for a in range(nb):
        sc={c:jnp.where(masks(a,c,e0,e1,keep[c],row,col),S[a,c]*scale,-1e30) for c in range(a+1)}
        top=jnp.max(sc[0],axis=1,keepdims=True)
        for c in range(1,a+1): top=jnp.maximum(top,jnp.max(sc[c],axis=1,keepdims=True))
        ex={c:jnp.exp(sc[c]-top) for c in sc}
        tot=sum(jnp.sum(e,axis=1,keepdims=True) for e in ex.values())
        inv=1.0/tot
        o=0.0
        for c in sc:
            P[a,c]=(ex[c]*inv).astype(BF); o=o+nn(P[a,c],v[c])
        out.append(o)
    res=A1+L+W+R+Qm+Km+[u,ux,cq]+[P[0,0],P[1,0],P[1,1],P[2,0],P[2,1],P[2,2]]
    return out,res
def bwd_unit(q,k,v,h,do,X,res):
    nb=3; row,col=iotas(); le=row>=col; st=row>col
    A1,L,W,R,Qm,Km=[res[3*i:3*i+3] for i in range(6)]
    u,ux,cq=res[18:21]; pl_=res[21:27]
    P={(0,0):pl_[0],(1,0):pl_[1],(1,1):pl_[2],(2,0):pl_[3],(2,1):pl_[4],(2,2):pl_[5]}
    scale=1.0/math.sqrt(BLK)
    G={}; dv=[0.0]*nb
    for a in range(nb):
        dp={c:nt(do[a],v[c]) for c in range(a+1)}
        delta=sum(jnp.sum(P[a,c].astype(F32)*dp[c],axis=1,keepdims=True) for c in range(a+1))
        for c in range(a+1):
            G[a,c]=(P[a,c].astype(F32)*(dp[c]-delta)*scale).astype(BF)
            dv[c]=dv[c]+tn(P[a,c],do[a])
    dq=[nn(G[a,a],k[a]) for a in range(nb)]
    dk=[tn(G[a,a],q[a]) for a in range(nb)]
    dL=[-nt(G[a,a],W[a]) for a in range(nb)]
    dW=[-tn(L[a],G[a,a]) for a in range(nb)]
    dh=[0.0]*nb; dX=[0.0]*nb
    dcq=nn(G[2,0],Km[0]).astype(BF)
    dQm=[None, nn(G[1,0],Km[0]), nn(G[2,1],Km[1])+dcq.astype(F32)]
    dKm=[tn(G[1,0],Qm[1])+tn(G[2,0],cq), tn(G[2,1],Qm[2]), None]
    dux=(-nt(dcq,h[1])).astype(BF)
    dh[1]=dh[1]-tn(ux,dcq)
    du=nt(dux,X[1]).astype(BF)
    dX[1]=dX[1]+tn(u,dux)
    dQm[2]=dQm[2]+nn(du,h[1])
    dh[1]=dh[1]+tn(du,Qm[2])
    dbeta=[]
    for a in range(nb):
        if dQm[a] is not None:
            d_=dQm[a].astype(BF)
            dq[a]=dq[a]+d_.astype(F32); dL[a]=dL[a]-nt(d_,h[a]); dh[a]=dh[a]-tn(L[a],d_)
        if dKm[a] is not None:
            d_=dKm[a].astype(BF)
            dk[a]=dk[a]+d_.astype(F32); dR=(-nt(h[a],d_)).astype(BF); dh[a]=dh[a]-nn(R[a],d_)
            dX[a]=dX[a]+nt(dR,W[a]); dW[a]=dW[a]+tn(X[a],dR)
        dl=dL[a].astype(BF)
        dA=jnp.where(le,nt(dl,X[a]),0.0).astype(BF)
        dX[a]=dX[a]+tn(A1[a],dl)
        dw=jnp.where(st,dW[a],0.0).astype(BF)
        dh[a]=dh[a]+nn(dw,k[a]); dk[a]=dk[a]+tn(dw,h[a])
        dq[a]=dq[a]+nn(dA,h[a]); dh[a]=dh[a]+tn(dA,q[a])
        dM=nt(tn(X[a],dX[a]),X[a])
        dn=jnp.where(st,-dM,0.0).astype(BF)
        dh[a]=dh[a]+nn(dn,h[a])+tn(dn,h[a])
        dbeta.append(jnp.sum(jnp.where(row==col,dM,0.0),axis=1,keepdims=True))
    return dq,dk,dv,dh,dbeta


def spans(rows, step):
    return pl.ds(pl.multiple_of(rows, step), step)


class Place:
    def __init__(self, names, sizes):
        self.names, self.sizes = names, sizes
        self.d, self.h, self.w = (lax.axis_index(n) for n in ("dp", "hid", "wid"))
        self.dp, self.wid = sizes["dp"], sizes["wid"]
        self.c = lax.rem(self.h, 2)
        self.x = lax.div(self.h, 2)
        self.sib = self.at(h=self.h + 1 - 2 * self.c)
        self.xpeer = self.at(h=lax.rem(self.h + 2, 4))

    def at(self, d=None, h=None, w=None):
        where = {"dp": self.d if d is None else d, "hid": self.h if h is None else h, "wid": self.w if w is None else w}
        return tuple(where[n] for n in self.names)

    def greet(self, peers):
        barrier = pltpu.get_barrier_semaphore()
        for peer in peers:
            pl.semaphore_signal(barrier, inc=1, device_id=peer, device_id_type=MESH)
        pl.semaphore_wait(barrier, len(peers))

    def dp_peer(self, j):
        return self.at(d=lax.rem(self.d + j, self.dp))

    def wid_peer(self, k):
        return self.at(w=lax.rem(self.w + k, self.wid))

    def hid_peer(self, k):
        return self.at(h=lax.rem(self.h + k, 4))

    def group(self):
        return [
            self.at(d=lax.rem(self.d + i, self.dp), w=lax.rem(self.w + k, self.wid))
            for i in range(self.dp)
            for k in range(self.wid)
            if i + k > 0
        ]


def send(src, dst, sent, got, peer):
    return pltpu.make_async_remote_copy(
        src_ref=src, dst_ref=dst, send_sem=sent, recv_sem=got, device_id=peer, device_id_type=MESH
    )


class Gather:
    def __init__(self, me, rows, full, col, width, ch, sz, rz, sy, ry):
        self.me, self.rows, self.full, self.ch = me, rows, full, ch
        self.col, self.width = col, width
        self.sz, self.rz, self.sy, self.ry = sz, rz, sy, ry

    def piece(self, d, o):
        return self.full.at[
            pl.ds(pl.multiple_of((d * self.me.wid + o) * self.rows, 16), self.rows), pl.ds(self.col, self.width)
        ]

    def origin(self, way, hop):
        return lax.clamp(0, self.me.w - way * hop, self.me.wid - 1)

    def zcopy(self, way, hop, sem):
        me, side = self.me, (way + 1) // 2
        part = self.piece(me.d, self.origin(way, hop))
        return send(
            part, part, self.sz.at[self.ch, side, sem], self.rz.at[self.ch, side, sem],
            me.at(w=lax.clamp(0, me.w + way, me.wid - 1)),
        )

    def ycopy(self, d, o, j):
        part = self.piece(d, o)
        return send(part, part, self.sy.at[self.ch, o, j - 1], self.ry.at[self.ch, o, j - 1], self.me.dp_peer(j))

    def has_next(self, way):
        return self.me.w < self.me.wid - 1 if way == 1 else self.me.w > 0

    def has_piece(self, way, hop):
        return self.me.w - hop >= 0 if way == 1 else self.me.w + hop < self.me.wid

    def start_z(self):
        for way in (1, -1):

            @pl.when(self.has_next(way))
            def _():
                self.zcopy(way, 0, 0).start()

    def start_y(self):
        for j in range(1, self.me.dp):
            self.ycopy(self.me.d, self.me.w, j).start()

    def hop(self, hop):
        me = self.me
        for way in (1, -1):

            @pl.when(self.has_piece(way, hop))
            def _():
                self.zcopy(way, hop, hop - 1).wait_recv()

                @pl.when(self.has_next(way))
                def _():
                    self.zcopy(way, hop, hop).start()

                for j in range(1, me.dp):
                    self.ycopy(me.d, self.origin(way, hop), j).start()

    def finish(self):
        me = self.me
        for j in range(1, me.dp):
            for o in range(me.wid):
                self.ycopy(lax.rem(me.d + me.dp - j, me.dp), o, j).wait_recv()

    def drain_z(self):
        me = self.me
        for way in (1, -1):
            for hop in range(me.wid):

                @pl.when(self.has_piece(way, hop) & self.has_next(way))
                def _():
                    self.zcopy(way, hop, hop).wait_send()

    def drain(self):
        self.drain_z()
        for j in range(1, self.me.dp):
            for o in range(self.me.wid):
                self.ycopy(self.me.d, o, j).wait_send()


class Line(Gather):
    def __init__(self, d, *args):
        super().__init__(*args)
        self.group = d

    def zcopy(self, way, hop, sem):
        me, side = self.me, (way + 1) // 2
        part = self.piece(self.group, self.origin(way, hop))
        return send(
            part, part, self.sz.at[self.ch, side, sem], self.rz.at[self.ch, side, sem],
            me.at(w=lax.clamp(0, me.w + way, me.wid - 1)),
        )

    def hop(self, hop):
        for way in (1, -1):

            @pl.when(self.has_piece(way, hop))
            def _():
                self.zcopy(way, hop, hop - 1).wait_recv()

                @pl.when(self.has_next(way))
                def _():
                    self.zcopy(way, hop, hop).start()


class Across(Gather):
    def __init__(self, extra, *args):
        super().__init__(*args)
        me, rows, full, col, width, ch = args[:6]
        self.lines = [
            Line(lax.rem(me.d + me.dp - j, me.dp), me, rows, full, col, width, ch if j == 0 else extra + j - 1, *args[6:])
            for j in range(me.dp)
        ]

    def start_z(self):
        self.lines[0].start_z()

    def hop(self, hop):
        me = self.me
        if hop == 0:
            for j in range(1, me.dp):
                self.ycopy(lax.rem(me.d + me.dp - j, me.dp), me.w, j).wait_recv()
                self.lines[j].start_z()
        else:
            for line in self.lines:
                line.hop(hop)

    def finish(self):
        pass

    def drain(self):
        for line in self.lines:
            line.drain_z()
        for j in range(1, self.me.dp):
            self.ycopy(self.me.d, self.me.w, j).wait_send()


def column(values, lane_index):
    lanes = lax.broadcasted_iota(jnp.int32, values.shape, 1)
    return jnp.sum(jnp.where(lanes == lane_index, values, 0.0), axis=1, keepdims=True)


def layer_kernel(
    cfg, lens, keep, tok, cot, gains, w_q, w_k, w_v, w_h, w_b, w_o, w_g, w_u, w_d,
    layer_out, tgrad, gsum, g_h, ry_h, z_h, zt_h, res_h,
    W, tokf, cotf, n1, n2, hlow, ng, mix, act, gg, ug, qs, ks, vs, hs, hraw, mgrad, xs, beta, dbeta, dB, gf, resb,
    s1, r1, s2, r2, acc, t2, q2, hidown, hgrad, stage, rts, rtr, rt, gbuf,
    local, own, hx_s, hx_r, sz, rz, sy, ry, s1s, s1r, s2s, s2r, s3s, s3r, ress, stages,
    ys, yr, zs, zr, zo, ld, rs_s, rs_r, gs_s, gs_r,
):
    me = Place(cfg["names"], cfg["sizes"])
    T, D, CB, HL, HD, FL, RS = (cfg[k] for k in ("T", "D", "CB", "HL", "HD", "FL", "RS"))
    FW = cfg["FW"]
    NF = 3 * FL // FW
    FB = 5 * HD
    BC = FB + 3 * FL
    GC, UC, DC, OC = FB, FB + FL, FB + 2 * FL, 4 * HD
    NB, U, DR = T // BUF, T // BUF * HL, RS * me.wid
    c = me.c
    own_cols = pl.ds(pl.multiple_of(me.h * CB, BLK), CB)
    own_rows = pl.ds(pl.multiple_of((me.d * me.wid + me.w) * RS, 16), RS)
    me.greet(me.group() + [me.hid_peer(k) for k in range(1, 4)])

    places = [(w_h, 3 * HD), (w_b, BC), (w_q, 0), (w_k, HD), (w_v, 2 * HD), (w_o, OC), (w_g, GC), (w_u, UC), (w_d, DC)]
    mine = [
        pltpu.make_async_copy(ref, W.at[own_rows, pl.ds(col, ref.shape[1])], own.at[i])
        for i, (ref, col) in enumerate(places)
    ]
    hid = []
    for i, (src, dst) in enumerate(((tok, tokf), (gains, gf), (cot, cotf))):
        here = pltpu.make_async_copy(src, dst.at[:, own_cols], local.at[i])
        away = [
            send(src, dst.at[:, own_cols], hx_s.at[i, k - 1], hx_r.at[i, k - 1], me.hid_peer(k)) for k in range(1, 4)
        ]
        hid.append([here] + away)
    for copy in mine[:6]:
        copy.start()
    for i in range(2):
        for copy in hid[i]:
            copy.start()
    for copy in mine[6:]:
        copy.start()
    sems = (sz, rz, sy, ry)
    first = [
        Gather(me, RS, W, col, ref.shape[1], i, *sems) for i, (ref, col) in enumerate(places[:6])
    ]

    def late(i):
        args = (me, RS, W, FB + i * FW, FW, 6 + i, *sems)
        if i in cfg["across"]:
            return Across(6 + NF + cfg["across"].index(i) * (me.dp - 1), *args)
        return Gather(*args)

    NG = len(first) + NF

    def chunk(n):
        return first[n] if n < len(first) else late(n - len(first))

    def begin(n):
        if n < NG:
            if n < len(first):
                mine[n].wait()
            elif n == len(first):
                for copy in mine[6:]:
                    copy.wait()
            chunk(n).start_z()
            chunk(n).start_y()

    events = [
        (k - hop + 1, hop) for k in range(NG + me.wid - 2) for hop in range(1, me.wid) if 0 <= k - hop + 1 < NG
    ]
    for i in cfg["across"]:
        events.insert(events.index((6 + i, 1)), (6 + i, 0))

    def advance(count):
        for _ in range(min(count, len(events))):
            n, hop = events.pop(0)
            chunk(n).hop(hop)

    for n in range(NG):
        begin(n)
    for copy in hid[2]:
        copy.start()
    for i in range(2):
        for copy in hid[i]:
            copy.wait()
    RB = 32

    def rows_of(m):
        return pl.ds(pl.multiple_of(m * BUF, BLK), BUF)

    def norm(src, dst, gain, base):
        def body(i, carry):
            rows = spans(base + i * RB, RB)
            wide = src[rows, :].astype(F32)
            scale = lax.rsqrt(jnp.mean(wide * wide, axis=1, keepdims=True) + EPSILON)
            dst[rows, :] = (wide * scale * gf[gain : gain + 1, :]).astype(BF)
            return carry

        lax.fori_loop(0, BUF // RB, body, 0)

    for m in range(NB):
        norm(tokf, n1, 0, m * BUF)

    def project(a):
        for m in range(NB):
            rows = n1[m * BUF : (m + 1) * BUF, :]
            made = nn(rows, W[:, a * HD : (a + 1) * HD])
            for hd in range(HL):
                part = made[:, hd * BLK : (hd + 1) * BLK]
                u = m * HL + hd
                if a < 3:
                    (qs, ks, vs)[a][u] = part.astype(BF)
                else:
                    hraw[u] = part
                    hs[u] = (part * lax.rsqrt(jnp.sum(part * part, axis=1, keepdims=True) + EPSILON)).astype(BF)
            if a == 3:
                beta[m * BUF : (m + 1) * BUF, :] = 2.0 * jax.nn.sigmoid(nn(rows, W[:, BC:]))

    advance(9)
    first[0].finish()
    first[1].finish()
    project(3)

    def invert(hd, carry):
        row, col = iotas()
        blocks = [(m, a) for m in range(NB) for a in range(3)]
        parts = [hs[m * HL + hd, a * BLK : (a + 1) * BLK, :] for m, a in blocks]
        strengths = [column(beta[m * BUF + a * BLK : m * BUF + (a + 1) * BLK, :], hd) for m, a in blocks]

        def between(level):
            for i in range(HL):
                later = slots[i].get(level, [])
                if later:

                    @pl.when(hd == i)
                    def _():
                        for n, hop in later:
                            chunk(n).hop(hop)

        made = tri_inverse([nt(part, part) for part in parts], strengths, row, col, between)
        for (m, a), x in zip(blocks, made):
            xs[m * HL + hd, a] = x.astype(BF)
        return carry

    advance(2)
    slots = [{level: [events.pop(0)] for level in (2, 4, 6) if events} for _ in range(HL)]
    lax.fori_loop(0, HL, invert, 0)
    for a in range(3):
        first[2 + a].finish()
        project(a)
        advance(2)

    def attend(u, carry):
        m, hd = lax.div(u, HL), lax.rem(u, HL)
        slot = lax.rem(u, 2)
        e0 = lens[m, 0]
        e1 = e0 + lens[m, 1]
        parts = [slice(a * BLK, (a + 1) * BLK) for a in range(3)]
        keys = [keep[0:1, p] for p in parts]
        for i in range(1, NB):
            keys = [jnp.where(m == i, keep[i : i + 1, p], key) for p, key in zip(parts, keys)]
        out, res = fwd_unit(
            [qs[u, p, :] for p in parts], [ks[u, p, :] for p in parts], [vs[u, p, :] for p in parts],
            [hs[u, p, :] for p in parts], [xs[u, a] for a in range(3)], keys, e0, e1,
        )
        for a in range(3):
            mix[spans(m * BUF + a * BLK, BLK), pl.ds(pl.multiple_of(hd * BLK, BLK), BLK)] = out[a].astype(BF)

        @pl.when(u >= 2)
        def _():
            pltpu.make_async_copy(resb.at[slot], res_h.at[u], ress.at[slot]).wait()

        for i, value in enumerate(res):
            resb[slot, i] = value
        pltpu.make_async_copy(resb.at[slot], res_h.at[u], ress.at[slot]).start()
        for m in range(NB):

            @pl.when(u == (m + 1) * HL - 1)
            def _():
                if m == 0:
                    first[5].finish()
                first_hop(0, m, branch(m))

            @pl.when(u == (m + 1) * HL)
            def _():
                second_hop(0, m)

        for i, (n, hop) in enumerate(during):

            @pl.when(u == i)
            def _():
                chunk(n).hop(hop)

        return carry

    def block(b):
        return pl.ds(pl.multiple_of(b * CB, BLK), CB)

    def hop1(tag, m, j):
        return send(s1.at[m, j], r1.at[tag % 3 // 2, m, j], s1s.at[tag, m, j], s1r.at[tag, m, j], me.sib)

    def hop2(tag, m, j):
        return send(s2.at[m, j], r2.at[tag, m, j], s2s.at[tag, m, j], s2r.at[tag, m, j], me.xpeer)

    def first_hop(tag, m, partial):
        for j in range(2):
            s1[m, j] = partial((1 - c) + 2 * j).astype(BF)
            hop1(tag, m, j).start()
        for j in range(2):
            acc[m, j] = partial(c + 2 * j)

    def second_hop(tag, m):
        for j in range(2):
            hop1(tag, m, j).wait()
            s2[m, j] = (acc[m, j] + r1[tag // 2, m, j].astype(F32)).astype(BF)
            hop2(tag, m, j).start()

    def total(tag, m, j):
        return s2[m, j].astype(F32) + r2[tag, m, j].astype(F32)

    def third(tag, full, m, j, core):
        part = full.at[rows_of(m), block(core + 2 * j)]
        return send(part, part, s3s.at[tag, m, j], s3r.at[tag, m, j], me.sib)

    def wait_third(tag, full, m):
        for j in range(2):
            third(tag, full, m, j, 1 - c).wait_recv()
            third(tag, full, m, j, c).wait_send()

    def branch(m):
        return lambda b: nt(mix[rows_of(m), :], W[block(b), OC : OC + HD])

    during = [events.pop(0) for _ in range(min(U, len(events)))]
    lax.fori_loop(0, U, attend, 0)
    for slot in range(2):
        pltpu.make_async_copy(resb.at[slot], res_h.at[0], ress.at[slot]).wait()
    second_hop(0, NB - 1)

    def residual(m):
        for j in range(2):
            hop2(0, m, j).wait()
            b = c + 2 * j
            hidden = tokf[rows_of(m), block(b)].astype(F32) + total(0, m, j)
            hlow[rows_of(m), block(b)] = hidden.astype(BF)
            third(0, hlow, m, j, c).start()
        hidown[rows_of(m), :] = tokf[rows_of(m), own_cols].astype(F32) + (
            s2[m, me.x].astype(F32) + r2[0, m, me.x].astype(F32)
        )

    for m in range(NB):
        residual(m)
        advance(2)
        wait_third(0, hlow, m)
        norm(hlow, n2, 8, m * BUF)
    for copy in hid[2]:
        copy.wait()

    NT = 256
    ND = 2 * FL // FW

    PER = FL // FW

    def ffn(m, part):
        def body(n, carry):
            at = pl.multiple_of(n * NT, NT)
            gate = nn(n2[rows_of(m), :], W[:, pl.ds(pl.multiple_of(GC + at, BLK), NT)])
            up = nn(n2[rows_of(m), :], W[:, pl.ds(pl.multiple_of(UC + at, BLK), NT)])
            sig = jax.nn.sigmoid(gate)
            silu = gate * sig
            cols = pl.ds(at, NT)
            act[rows_of(m), cols] = (silu * up).astype(BF)
            gg[rows_of(m), cols] = (up * sig * (1.0 + gate * (1.0 - sig))).astype(BF)
            ug[rows_of(m), cols] = silu.astype(BF)
            return carry

        lax.fori_loop(part * (FW // NT), (part + 1) * (FW // NT), body, 0)

    def ffn_back(m):
        def body(n, carry):
            at = pl.multiple_of(n * NT, NT)
            cols = pl.ds(at, NT)
            back = nn(cotf[rows_of(m), :], W[:, pl.ds(pl.multiple_of(DC + at, BLK), NT)])
            gg[rows_of(m), cols] = (back * gg[rows_of(m), cols].astype(F32)).astype(BF)
            ug[rows_of(m), cols] = (back * ug[rows_of(m), cols].astype(F32)).astype(BF)
            return carry

        lax.fori_loop(0, FL // NT, body, 0)

    def dp_rows(j):
        return pl.ds(pl.multiple_of(lax.rem(me.d + j, me.dp) * DR, 16), DR)

    def staged(side, i, col, width):
        return pltpu.make_async_copy(
            stage.at[side, i, :, pl.ds(0, width)],
            g_h.at[pl.ds(pl.multiple_of(i * CB, BLK), CB), pl.ds(col, width)],
            stages.at[side, i],
        )

    def rs_y(ch, col, width, j):
        return send(
            g_h.at[dp_rows(j), pl.ds(col, width)], ry_h.at[j - 1, :, pl.ds(col, width)],
            ys.at[ch, j - 1], yr.at[ch, j - 1], me.dp_peer(j),
        )

    pending = []
    made_terms = [0]

    def flush():
        side, ch, col, width = pending.pop()
        for i in range(D // CB):
            staged(side, i, col, width).wait()
        for j in range(1, me.dp):
            rs_y(ch, col, width, j).start()

    def weight_term(ch, left, right, at, col, width):
        side = made_terms[0] % 2
        made_terms[0] += 1

        def body(i, carry):
            stage[side, i, :, pl.ds(0, width)] = tn(
                left[:, pl.ds(pl.multiple_of(i * CB, BLK), CB)], right[:, at : at + width]
            ).astype(BF)
            staged(side, i, col, width).start()
            return carry

        lax.fori_loop(0, D // CB, body, 0)
        if pending:
            flush()
        pending.append((side, ch, col, width))

    def ffn_terms(left, right, col):
        for n in range(FL // FW):
            weight_term(6 + (col - FB) // FW + n, left, right, n * FW, col + n * FW, FW)

    for part in range(PER):
        advance(max([i + 1 for i, (n, _) in enumerate(events) if n <= 6 + PER + part], default=0))
        late(part).finish()
        late(PER + part).finish()
        for m in range(NB):
            ffn(m, part)
        weight_term(6 + 2 * PER + part, cotf, act, part * FW, DC + part * FW, FW)
        flush()
    advance(len(events))
    for i in range(ND, NF):
        late(i).finish()

    def normed_back(m):
        return lambda b: nt(gg[rows_of(m), :], W[block(b), GC : GC + FL]) + nt(
            ug[rows_of(m), :], W[block(b), UC : UC + FL]
        )

    def down(m):
        return lambda b: nt(act[rows_of(m), :], W[block(b), DC : DC + FL])

    ffn_back(0)
    first_hop(1, 0, normed_back(0))
    ffn_back(1)
    second_hop(1, 0)
    for m in range(1, NB):
        first_hop(1, m, normed_back(m))
        if m + 1 < NB:
            ffn_back(m + 1)
        second_hop(1, m)
    for g in first:
        g.drain()

    for i in range(NF):
        late(i).drain()
    ffn_terms(n2, gg, GC)
    ffn_terms(n2, ug, UC)
    flush()

    def hop2_out(m):
        return send(t2.at[m], q2.at[m], s2s.at[2, m, 0], s2r.at[2, m, 0], me.xpeer)

    for m in range(NB):
        first_hop(2, m, down(m))
    other = 1 - me.x
    for m in range(NB):
        for j in range(2):
            hop1(2, m, j).wait()
        t2[m] = (acc[m, other] + r1[1, m, other].astype(F32)).astype(BF)
        hop2_out(m).start()

    gm = W.at[0:DR, FB : FB + FW]
    peer_term = W.at[DR : 2 * DR, FB : FB + FW]
    inbox = W.at[DR : 2 * DR, FB + FW : FB + 2 * FW]

    def to_wid(slot):
        return W.at[0:DR, FB + FW + slot * FW : FB + 2 * FW + slot * FW]

    near = me.w + 1 - 2 * lax.rem(me.w, 2)
    far = 2 - 2 * lax.div(me.w, 2)
    inner = (me.w == 1) | (me.w == 2)
    outer = jnp.logical_not(inner)

    def block_rows(o, count=1):
        return pl.ds(pl.multiple_of(o * RS, 16), count * RS)

    def to_near(ch, col, width, slot):
        return send(
            to_wid(slot).at[block_rows(near), pl.ds(0, width)], z_h.at[1, :, pl.ds(col, width)],
            zs.at[ch, 0], zr.at[ch, 0], me.at(w=near),
        )

    def to_inner(ch, col, width, slot):
        return send(
            to_wid(slot).at[block_rows(far, 2), pl.ds(0, width)], zt_h.at[:, pl.ds(col, width)],
            zs.at[ch, 1], zr.at[ch, 1], me.at(w=near),
        )

    def to_far(ch, col, width, slot, i):
        return send(
            to_wid(slot).at[block_rows(far + i), pl.ds(0, width)], z_h.at[2, :, pl.ds(col, width)],
            zs.at[ch, 2 + i], zr.at[ch, 2], me.at(w=far + i),
        )

    def rs_free(ch, col, width, slot):
        to_near(ch, col, width, slot).wait_send()

        @pl.when(outer)
        def _():
            to_inner(ch, col, width, slot).wait_send()

        @pl.when(inner)
        def _():
            for i in range(2):
                to_far(ch, col, width, slot, i).wait_send()

    def rs_across(ch, col, width, slot):
        @pl.when(inner)
        def _():
            to_inner(ch, col, width, slot).wait_recv()
            load = pltpu.make_async_copy(
                zt_h.at[:, pl.ds(col, width)], inbox.at[pl.ds(0, 2 * RS), pl.ds(0, width)], ld.at[2]
            )
            load.start()
            load.wait()
            for i in range(2):
                rows = block_rows(far + i)
                to_wid(slot)[rows, 0:width] = (
                    to_wid(slot)[rows, 0:width].astype(F32) + inbox[i * RS : (i + 1) * RS, 0:width].astype(F32)
                ).astype(BF)
                to_far(ch, col, width, slot, i).start()

    def rs_end(ch, col, width):
        to_near(ch, col, width, 0).wait_recv()
        to_far(ch, col, width, 0, 0).wait_recv()

    def rs_stage(ch, col, width, slot):
        here = pltpu.make_async_copy(g_h.at[dp_rows(0), pl.ds(col, width)], gm.at[:, pl.ds(0, width)], ld.at[0])
        here.start()
        mine_out = pltpu.make_async_copy(
            to_wid(slot).at[block_rows(me.w), pl.ds(0, width)], z_h.at[0, :, pl.ds(col, width)], zo.at[ch]
        )
        for j in range(1, me.dp):
            rs_y(ch, col, width, j).wait_recv()
            there = pltpu.make_async_copy(
                ry_h.at[j - 1, :, pl.ds(col, width)], peer_term.at[:, pl.ds(0, width)], ld.at[1]
            )
            there.start()
            if j == 1:
                here.wait()
            there.wait()
            for i, o in enumerate((far, far + 1, near, me.w)):
                rows = block_rows(o)
                so_far = gm if j == 1 else to_wid(slot)
                to_wid(slot)[rows, 0:width] = (
                    so_far[rows, 0:width].astype(F32) + peer_term[rows, 0:width].astype(F32)
                ).astype(BF)
                if j == me.dp - 1:
                    if i == 1:

                        @pl.when(outer)
                        def _():
                            to_inner(ch, col, width, slot).start()

                    if i == 2:
                        to_near(ch, col, width, slot).start()
                    if i == 3:
                        mine_out.start()
        mine_out.wait()

    places_of = [(3 * HD, HD), (BC, BLK), (0, HD), (HD, HD), (2 * HD, HD), (OC, HD)]
    order = [(6 + (i + ND) % NF, FB + (i + ND) % NF * FW, FW) for i in range(NF)]
    order += [(k, *places_of[k]) for k in (5, 2, 3, 4)]
    order += [(0, 3 * HD, HD - BLK), (6 + NF, 4 * HD - BLK, BLK), (1, BC, BLK)]
    taken = [0]

    def take():
        n = taken[0]
        taken[0] += 1
        if n >= 4:
            rs_free(*order[n - 4], n % 4)
        rs_stage(*order[n], n % 4)
        if n >= 1:
            rs_across(*order[n - 1], (n - 1) % 4)
        if n == len(order) - 1:
            rs_across(*order[n], n % 4)

    def spread_back(m):
        for j in range(2):
            hop2(1, m, j).wait()
            ng[rows_of(m), block(c + 2 * j)] = total(1, m, j).astype(BF)
            third(1, ng, m, j, c).start()

    def branch_back(m):
        def body(i, carry):
            rows = spans(m * BUF + i * RB, RB)
            low = hlow[rows, :].astype(F32)
            scale = lax.rsqrt(jnp.mean(low * low, axis=1, keepdims=True) + EPSILON)
            scaled = ng[rows, :].astype(F32) * gf[8:9, :]
            row_total = jnp.sum(low * scaled, axis=1, keepdims=True)
            cube = scale * scale * scale * row_total / D
            low_own = hlow[rows, own_cols].astype(F32)
            ng_own = ng[rows, own_cols].astype(F32)
            hgrad[rows, :] = (
                cotf[rows, own_cols].astype(F32) + scale * gf[8:9, own_cols] * ng_own - low_own * cube
            )
            gbuf[slot_here, 8:16, :] += jnp.broadcast_to(
                jnp.sum(low_own * scale * ng_own, axis=0, keepdims=True), (8, CB)
            )
            ng[rows, :] = (cotf[rows, :].astype(F32) + scale * scaled - low * cube).astype(BF)
            return carry

        lax.fori_loop(0, BUF // RB, body, 0)
        made = nn(ng[rows_of(m), :], W[:, OC : OC + HD])
        for hd in range(HL):
            mgrad[m * HL + hd] = made[:, hd * BLK : (hd + 1) * BLK].astype(BF)

    slot_here = me.d * me.wid + me.w
    gbuf[slot_here] = jnp.zeros((16, CB), F32)
    dbeta[...] = jnp.zeros_like(dbeta)
    dA = n2

    def fetch_res(u):
        slot = lax.rem(u, 2)
        return pltpu.make_async_copy(res_h.at[u], resb.at[slot], ress.at[slot])

    fetch_res(0).start()

    def attend_back(u, carry):
        m, hd = lax.div(u, HL), lax.rem(u, HL)
        slot = lax.rem(u, 2)
        parts = [slice(a * BLK, (a + 1) * BLK) for a in range(3)]

        fetch_res(u).wait()

        @pl.when(u + 1 < U)
        def _():
            fetch_res(u + 1).start()

        dq, dk, dv, dh, db = bwd_unit(
            [qs[u, p, :] for p in parts], [ks[u, p, :] for p in parts], [vs[u, p, :] for p in parts],
            [hs[u, p, :] for p in parts], [mgrad[u, p, :] for p in parts], [xs[u, a] for a in range(3)],
            [resb[slot, i] for i in range(NRES)],
        )
        for a in range(3):
            rows = spans(m * BUF + a * BLK, BLK)
            for n, value in enumerate((dq[a], dk[a], dv[a])):
                dA[rows, pl.ds(pl.multiple_of(n * HD + hd * BLK, BLK), BLK)] = value.astype(BF)
            raw = hraw[u, parts[a], :]
            scale = lax.rsqrt(jnp.sum(raw * raw, axis=1, keepdims=True) + EPSILON)
            along = jnp.sum(raw * dh[a], axis=1, keepdims=True)
            dA[rows, pl.ds(pl.multiple_of(3 * HD + hd * BLK, BLK), BLK)] = (
                scale * dh[a] - raw * (scale * scale * scale * along)
            ).astype(BF)
            strength = column(beta[rows, :], hd)
            pull = db[a] * (1.0 / jnp.maximum(strength, 1e-30) - 0.5)
            lanes = lax.broadcasted_iota(jnp.int32, (BLK, BLK), 1)
            dbeta[rows, :] += jnp.where(lanes == hd, pull, 0.0)

        return carry

    take()
    for m in range(NB):
        spread_back(m)
        wait_third(1, ng, m)
        branch_back(m)
        if m == 0:
            take()
    lax.fori_loop(0, U, attend_back, 0)
    dB[...] = dbeta[...].astype(BF)
    weight_term(5, ng, mix, 0, OC, HD)
    take()
    for a in range(3):
        weight_term(2 + a, n1, dA, a * HD, a * HD, HD)
    weight_term(0, n1, dA, 3 * HD, 3 * HD, HD - BLK)
    weight_term(6 + NF, n1, dA, 4 * HD - BLK, 4 * HD - BLK, BLK)
    weight_term(1, n1, dB, 0, BC, BLK)
    flush()

    rt[...] = jnp.zeros_like(rt)

    def first_back(m):
        def partial(b):
            made = nt(dA[rows_of(m), :], W[block(b), 0 : 4 * HD]) + nt(dB[rows_of(m), :], W[block(b), BC:])
            along = jnp.sum(made * tokf[rows_of(m), block(b)].astype(F32) * gf[0:1, block(b)], axis=1, keepdims=True)
            rt[rows_of(m), :] += jnp.broadcast_to(along, (BUF, BLK))
            return made

        return partial

    for m in range(NB):
        hop2_out(m).wait()
        layer_out[rows_of(m), :] = (
            hidown[rows_of(m), :] + (acc[m, me.x] + r1[1, m, me.x].astype(F32) + q2[m].astype(F32))
        ).astype(BF)
    for m in range(NB):
        first_hop(3, m, first_back(m))
    for i in range(T // BLK):
        rts[:, i * BLK : (i + 1) * BLK] = rt[i * BLK : (i + 1) * BLK, :].T[0:8, :]
    rt_copies = [send(rts, rtr.at[k - 1], rs_s.at[k - 1], rs_r.at[k - 1], me.hid_peer(k)) for k in range(1, 4)]
    for copy in rt_copies:
        copy.start()

    def hop2_in(m):
        return send(t2.at[m], r2.at[0, m, 0], s2s.at[3, m, 0], s2r.at[3, m, 0], me.xpeer)

    for m in range(NB):
        for j in range(2):
            hop1(3, m, j).wait()
        t2[m] = (acc[m, other] + r1[0, m, other].astype(F32)).astype(BF)
        hop2_in(m).start()

    take()
    for m in range(NB):
        hop2_in(m).wait()
    for copy in rt_copies:
        copy.wait()

    def token_rows(i, carry):
        rows = spans(i * BLK, BLK)
        m = lax.div(i, BUF // BLK)
        part = spans(lax.rem(i, BUF // BLK) * BLK, BLK)
        lane = rts[0:1, rows] + rtr[0, 0:1, rows] + rtr[1, 0:1, rows] + rtr[2, 0:1, rows]
        row_total = jnp.broadcast_to(lane, (BLK, BLK)).T[:, 0:1]
        wide = tokf[rows, :].astype(F32)
        scale = lax.rsqrt(jnp.mean(wide * wide, axis=1, keepdims=True) + EPSILON)
        made = acc[m, me.x, part, :] + r1[0, m, me.x, part, :].astype(F32) + r2[0, m, 0, part, :].astype(F32)
        own_tok = tokf[rows, own_cols].astype(F32)
        back = scale * gf[0:1, own_cols] * made - own_tok * (scale * scale * scale * row_total / D)
        tgrad[rows, :] = (hgrad[rows, :] + back).astype(BF)
        gbuf[slot_here, 0:8, :] += jnp.broadcast_to(jnp.sum(own_tok * scale * made, axis=0, keepdims=True), (8, CB))
        return carry

    lax.fori_loop(0, T // BLK, token_rows, 0)
    gain_copies = []
    for n, peer in enumerate(me.group()):
        copy = send(gbuf.at[slot_here], gbuf.at[slot_here], gs_s.at[n], gs_r.at[n], peer)
        copy.start()
        gain_copies.append(copy)
    while taken[0] < len(order):
        take()
    for copy in gain_copies:
        copy.wait()
    both = gbuf[0]
    for n in range(1, me.dp * me.wid):
        both = both + gbuf[n]
    gsum[...] = both
    for ch, col, width in order:
        rs_end(ch, col, width)
    for n in range(len(order) - 4, len(order)):
        rs_free(*order[n], n % 4)
    for ch, col, width in order:
        for j in range(1, me.dp):
            rs_y(ch, col, width, j).wait_send()


def final_kernel(
    cfg, z_h, layer_in, tgrad_in, gsum,
    layer_out, tgrad, one, two, o_q, o_k, o_v, o_h, o_b, o_o, o_g, o_u, o_d,
    zbuf, total, gb, loads, stores, through,
):
    HD, FL, RS = cfg["HD"], cfg["FL"], cfg["RS"]
    FB = 5 * HD
    targets = [(o_g, FB, FL), (o_u, FB + FL, FL), (o_d, FB + 2 * FL, FL), (o_q, 0, HD), (o_k, HD, HD), (o_v, 2 * HD, HD)]
    targets += [(o_h, 3 * HD, HD), (o_o, 4 * HD, HD), (None, FB + 3 * FL, BLK)]
    passed = [
        pltpu.make_async_copy(layer_in, layer_out, through.at[0]),
        pltpu.make_async_copy(tgrad_in, tgrad, through.at[1]),
        pltpu.make_async_copy(gsum, gb, through.at[2]),
    ]
    copies = [
        pltpu.make_async_copy(z_h.at[:, :, pl.ds(col, w)], zbuf.at[:, :, pl.ds(col, w)], loads.at[i])
        for i, (_, col, w) in enumerate(targets)
    ]
    for copy in copies + passed:
        copy.start()
    written = []
    for i, (out, col, w) in enumerate(targets):
        copies[i].wait()
        value = zbuf[0, :, col : col + w].astype(F32)
        for k in range(1, 3):
            value = value + zbuf[k, :, col : col + w].astype(F32)
        if out is None:
            o_b[...] = value[:, 0 : o_b.shape[1]]
        else:
            total[:, col : col + w] = value
            copy = pltpu.make_async_copy(total.at[:, pl.ds(col, w)], out, stores.at[i])
            copy.start()
            written.append(copy)
    passed[2].wait()
    one[...] = gb[0:1, :]
    two[...] = gb[8:9, :]
    for copy in passed[:2] + written:
        copy.wait()


def solution(mesh):
    names = tuple(mesh.axis_names)
    sizes = {n: mesh.shape[n] for n in names}
    dp, wid = sizes["dp"], sizes["wid"]
    assert sizes["hid"] == 4 and wid == 4

    def shards(
        tokens, cotangent, lengths, keep, norm_one, w_query, w_key, w_value, w_house, w_beta, w_out, norm_two,
        w_gate, w_up, w_down,
    ):
        micro, rows, CB = tokens.shape
        T, D, HD, FL, RS = micro * rows, CB * 4, w_query.shape[1], w_gate.shape[1], w_query.shape[0]
        HL, NB, FW = HD // BLK, T // BUF, 512
        U, NF, DR = NB * HL, 3 * FL // FW, D // dp
        CT = 5 * HD + 3 * FL + BLK
        heads = w_beta.shape[1]
        cfg = dict(names=names, sizes=sizes, T=T, D=D, CB=CB, HL=HL, HD=HD, FL=FL, RS=RS, FW=FW, across=[4, 5])
        gains = jnp.concatenate([jnp.broadcast_to(g, (8, CB)) for g in (norm_one, norm_two)], axis=0).astype(F32)
        sd = jax.ShapeDtypeStruct
        nch = 6 + NF
        vm = pltpu.VMEM
        unit = lambda t: vm((U, BUF, BLK), t)
        pair = vm((NB, 2, BUF, CB), BF)
        outs = pl.pallas_call(
            functools.partial(layer_kernel, cfg),
            out_shape=(
                sd((T, CB), BF), sd((T, CB), BF), sd((16, CB), F32),
                sd((D, CT), BF), sd((dp - 1, DR, CT), BF), sd((3, RS, CT), BF), sd((2 * RS, CT), BF),
                sd((U, NRES, BLK, BLK), BF),
            ),
            in_specs=[SM, VM] + [ANY] * 12,
            out_specs=(VM,) * 3 + (ANY,) * 5,
            scratch_shapes=[
                vm((D, CT), BF), *[vm((T, D), BF)] * 6, vm((T, HD), BF), *[vm((T, FL), BF)] * 3,
                *[unit(BF)] * 4, unit(F32), unit(BF), vm((U, 3, BLK, BLK), BF), vm((T, BLK), F32), vm((T, BLK), F32), vm((T, BLK), BF),
                vm((16, D), F32), vm((2, NRES, BLK, BLK), BF),
                pair, vm((2, NB, 2, BUF, CB), BF), pair, vm((2, NB, 2, BUF, CB), BF), vm((NB, 2, BUF, CB), F32),
                vm((NB, BUF, CB), BF), vm((NB, BUF, CB), BF), vm((T, CB), F32), vm((T, CB), F32),
                vm((2, 4, CB, FW), BF),
                vm((8, T), F32), vm((3, 8, T), F32), vm((T, BLK), F32), vm((dp * wid, 16, CB), F32),
                DMA((3,)), DMA((9,)), DMA((3, 3)), DMA((3, 3)), *[DMA((nch + len(cfg["across"]) * (dp - 1), 2, wid))] * 2,
                DMA((nch, wid, dp - 1)), DMA((nch, wid, dp - 1)),
                *[DMA((4, NB, 2))] * 4, *[DMA((2, NB, 2))] * 2, DMA((2,)), DMA((2, 4)),
                DMA((nch + 1, dp - 1)), DMA((nch + 1, dp - 1)), DMA((nch + 1, 4)), DMA((nch + 1, 3)), DMA((nch + 1,)),
                DMA((3,)), DMA((3,)), DMA((3,)), DMA((dp * wid - 1,)), DMA((dp * wid - 1,)),
            ],
            compiler_params=pltpu.CompilerParams(
                collective_id=0, has_side_effects=True, vmem_limit_bytes=cfg.get("limit", 63 << 20)
            ),
            name="layer",
        )(
            lengths.reshape(NB, lengths.shape[2]), keep.reshape(NB, BUF), tokens.reshape(T, CB),
            cotangent.reshape(T, CB), gains, w_query, w_key, w_value, w_house,
            jnp.pad(w_beta, ((0, 0), (0, BLK - heads))), w_out.T, w_gate, w_up, w_down.T,
        )
        done = pl.pallas_call(
            functools.partial(final_kernel, cfg),
            out_shape=(
                sd((T, CB), BF), sd((T, CB), BF), sd((1, CB), F32), sd((1, CB), F32),
                *[sd((RS, HD), F32)] * 4, sd((RS, heads), F32), sd((RS, HD), F32), *[sd((RS, FL), F32)] * 3,
            ),
            in_specs=[ANY] * 4,
            out_specs=(ANY, ANY, VM, VM) + (ANY,) * 4 + (VM,) + (ANY,) * 4,
            scratch_shapes=[
                vm((3, RS, CT), BF), vm((RS, CT), F32), vm((16, CB), F32), DMA((9,)), DMA((9,)), DMA((3,)),
            ],
            compiler_params=pltpu.CompilerParams(vmem_limit_bytes=32 << 20),
            name="final",
        )(outs[5], outs[0], outs[1], outs[2])
        layer_out, tgrad, one, two, gq, gk, gv, gh, gb, go, g_gate, g_up, g_down = done
        return (
            layer_out.reshape(tokens.shape), tgrad.reshape(tokens.shape), one, gq, gk, gv, gh, gb, go.T, two,
            g_gate, g_up, g_down.T,
        )

    rows = P(("dp", "wid"), "hid")
    cols = P("hid", ("dp", "wid"))
    wide = P(None, ("dp", "wid"), "hid")
    gain = P(None, "hid")
    return jax.shard_map(
        shards,
        mesh=mesh,
        in_specs=(
            wide, wide, P(None, ("dp", "wid"), None), P(None, ("dp", "wid")), gain, rows, rows, rows, rows, rows,
            cols, gain, rows, rows, cols,
        ),
        out_specs=(wide, wide, gain, rows, rows, rows, rows, rows, cols, gain, rows, rows, cols),
        check_vma=False,
    )
```

```python
import functools
import math

import jax
import jax.numpy as jnp
from jax import lax
from jax.experimental import pallas as pl
from jax.experimental.pallas import tpu as pltpu
from jax.sharding import PartitionSpec as P

BLK = 128
BUF = 384
EPSILON = 1e-06
F32 = jnp.float32
BF = jnp.bfloat16
MESH = pl.DeviceIdType.MESH
ANY = pl.BlockSpec(memory_space=pl.ANY)
VM = pl.BlockSpec(memory_space=pltpu.VMEM)
SM = pl.BlockSpec(memory_space=pltpu.SMEM)
DMA = pltpu.SemaphoreType.DMA
NRES = 27


def _dot(a,b,ca,cb): return lax.dot_general(a,b,(((ca,),(cb,)),((),())),preferred_element_type=F32)
def nn(a,b): return _dot(a.astype(BF),b.astype(BF),1,0)
def nt(a,b): return _dot(a.astype(BF),b.astype(BF),1,1)
def tn(a,b): return _dot(a.astype(BF),b.astype(BF),0,0)
def split(a):
    hi=a.astype(BF); return hi,(a-hi.astype(F32)).astype(BF)
def nn3(a,b):
    ah,al=split(a); bh,bl=split(b)
    return _dot(ah,bh,1,0)+(_dot(ah,bl,1,0)+_dot(al,bh,1,0))
INV=nn3
def iotas():
    return lax.broadcasted_iota(jnp.int32,(BLK,BLK),0), lax.broadcasted_iota(jnp.int32,(BLK,BLK),1)
def tri_inverse(inners, betas, row, col, between):
    first=((row>>1)==(col>>1))&(row>col)
    xs=[]
    for inner,beta_col in zip(inners,betas):
        diag=jnp.where(row==col, beta_col, 0.0)
        beta_lane=jnp.sum(diag,axis=0,keepdims=True)
        xs.append(diag-jnp.where(first, inner*beta_col*beta_lane, 0.0))
    lb=1
    while (1<<lb)<BLK:
        m=((row>>(lb+1))==(col>>(lb+1)))&((row>>lb)>(col>>lb))
        half=[INV(x,jnp.where(m,inner,0.0)) for x,inner in zip(xs,inners)]
        xs=[x-INV(y,x) for x,y in zip(xs,half)]
        between(lb)
        lb+=1
    return xs
def masks(a,c,e0,e1,keep_row,row,col):
    qp=row+BLK*a; kp=col+BLK*c
    segq=(qp>=e0).astype(jnp.int32)+(qp>=e1).astype(jnp.int32)
    segk=(kp>=e0).astype(jnp.int32)+(kp>=e1).astype(jnp.int32)
    ok=(segq==segk)
    if a==c: return ok&(row>=col)&((keep_row==1)|(row==col))
    return ok&(keep_row==1)
def fwd_unit(q,k,v,h,X,keep,e0,e1):
    nb=len(q); row,col=iotas(); le=row>=col; st=row>col
    A1,L,W,R,Qm,Km=[],[],[],[],[],[]
    for a in range(nb):
        x=X[a]
        a1=jnp.where(le,nt(q[a],h[a]),0.0).astype(BF)
        w=jnp.where(st,nt(h[a],k[a]),0.0).astype(BF)
        l=nn(a1,x).astype(BF); r=nn(x,w).astype(BF)
        A1.append(a1);W.append(w);L.append(l);R.append(r)
        Qm.append((q[a].astype(F32)-nn(l,h[a])).astype(BF))
        Km.append((k[a].astype(F32)-tn(r,h[a])).astype(BF))
    scale=1.0/math.sqrt(BLK)
    S={}
    for a in range(nb):
        S[a,a]=nt(q[a],k[a])-nn(L[a],W[a])
    S[1,0]=nt(Qm[1],Km[0]); S[2,1]=nt(Qm[2],Km[1])
    u=nt(Qm[2],h[1]).astype(BF); ux=nn(u,X[1]).astype(BF)
    cq=(Qm[2].astype(F32)-nn(ux,h[1])).astype(BF)
    S[2,0]=nt(cq,Km[0])
    P={}; out=[]
    for a in range(nb):
        sc={c:jnp.where(masks(a,c,e0,e1,keep[c],row,col),S[a,c]*scale,-1e30) for c in range(a+1)}
        top=jnp.max(sc[0],axis=1,keepdims=True)
        for c in range(1,a+1): top=jnp.maximum(top,jnp.max(sc[c],axis=1,keepdims=True))
        ex={c:jnp.exp(sc[c]-top) for c in sc}
        tot=sum(jnp.sum(e,axis=1,keepdims=True) for e in ex.values())
        inv=1.0/tot
        o=0.0
        for c in sc:
            P[a,c]=(ex[c]*inv).astype(BF); o=o+nn(P[a,c],v[c])
        out.append(o)
    res=A1+L+W+R+Qm+Km+[u,ux,cq]+[P[0,0],P[1,0],P[1,1],P[2,0],P[2,1],P[2,2]]
    return out,res
def bwd_unit(q,k,v,h,do,X,res):
    nb=3; row,col=iotas(); le=row>=col; st=row>col
    A1,L,W,R,Qm,Km=[res[3*i:3*i+3] for i in range(6)]
    u,ux,cq=res[18:21]; pl_=res[21:27]
    P={(0,0):pl_[0],(1,0):pl_[1],(1,1):pl_[2],(2,0):pl_[3],(2,1):pl_[4],(2,2):pl_[5]}
    scale=1.0/math.sqrt(BLK)
    G={}; dv=[0.0]*nb
    for a in range(nb):
        dp={c:nt(do[a],v[c]) for c in range(a+1)}
        delta=sum(jnp.sum(P[a,c].astype(F32)*dp[c],axis=1,keepdims=True) for c in range(a+1))
        for c in range(a+1):
            G[a,c]=(P[a,c].astype(F32)*(dp[c]-delta)*scale).astype(BF)
            dv[c]=dv[c]+tn(P[a,c],do[a])
    dq=[nn(G[a,a],k[a]) for a in range(nb)]
    dk=[tn(G[a,a],q[a]) for a in range(nb)]
    dL=[-nt(G[a,a],W[a]) for a in range(nb)]
    dW=[-tn(L[a],G[a,a]) for a in range(nb)]
    dh=[0.0]*nb; dX=[0.0]*nb
    dcq=nn(G[2,0],Km[0]).astype(BF)
    dQm=[None, nn(G[1,0],Km[0]), nn(G[2,1],Km[1])+dcq.astype(F32)]
    dKm=[tn(G[1,0],Qm[1])+tn(G[2,0],cq), tn(G[2,1],Qm[2]), None]
    dux=(-nt(dcq,h[1])).astype(BF)
    dh[1]=dh[1]-tn(ux,dcq)
    du=nt(dux,X[1]).astype(BF)
    dX[1]=dX[1]+tn(u,dux)
    dQm[2]=dQm[2]+nn(du,h[1])
    dh[1]=dh[1]+tn(du,Qm[2])
    dbeta=[]
    for a in range(nb):
        if dQm[a] is not None:
            d_=dQm[a].astype(BF)
            dq[a]=dq[a]+d_.astype(F32); dL[a]=dL[a]-nt(d_,h[a]); dh[a]=dh[a]-tn(L[a],d_)
        if dKm[a] is not None:
            d_=dKm[a].astype(BF)
            dk[a]=dk[a]+d_.astype(F32); dR=(-nt(h[a],d_)).astype(BF); dh[a]=dh[a]-nn(R[a],d_)
            dX[a]=dX[a]+nt(dR,W[a]); dW[a]=dW[a]+tn(X[a],dR)
        dl=dL[a].astype(BF)
        dA=jnp.where(le,nt(dl,X[a]),0.0).astype(BF)
        dX[a]=dX[a]+tn(A1[a],dl)
        dw=jnp.where(st,dW[a],0.0).astype(BF)
        dh[a]=dh[a]+nn(dw,k[a]); dk[a]=dk[a]+tn(dw,h[a])
        dq[a]=dq[a]+nn(dA,h[a]); dh[a]=dh[a]+tn(dA,q[a])
        dM=nt(tn(X[a],dX[a]),X[a])
        dn=jnp.where(st,-dM,0.0).astype(BF)
        dh[a]=dh[a]+nn(dn,h[a])+tn(dn,h[a])
        dbeta.append(jnp.sum(jnp.where(row==col,dM,0.0),axis=1,keepdims=True))
    return dq,dk,dv,dh,dbeta


def spans(rows, step):
    return pl.ds(pl.multiple_of(rows, step), step)


class Place:
    def __init__(self, names, sizes):
        self.names, self.sizes = names, sizes
        self.d, self.h, self.w = (lax.axis_index(n) for n in ("dp", "hid", "wid"))
        self.dp, self.wid = sizes["dp"], sizes["wid"]
        self.c = lax.rem(self.h, 2)
        self.x = lax.div(self.h, 2)
        self.sib = self.at(h=self.h + 1 - 2 * self.c)
        self.xpeer = self.at(h=lax.rem(self.h + 2, 4))

    def at(self, d=None, h=None, w=None):
        where = {"dp": self.d if d is None else d, "hid": self.h if h is None else h, "wid": self.w if w is None else w}
        return tuple(where[n] for n in self.names)

    def greet(self, peers):
        barrier = pltpu.get_barrier_semaphore()
        for peer in peers:
            pl.semaphore_signal(barrier, inc=1, device_id=peer, device_id_type=MESH)
        pl.semaphore_wait(barrier, len(peers))

    def dp_peer(self, j):
        return self.at(d=lax.rem(self.d + j, self.dp))

    def wid_peer(self, k):
        return self.at(w=lax.rem(self.w + k, self.wid))

    def hid_peer(self, k):
        return self.at(h=lax.rem(self.h + k, 4))

    def group(self):
        return [
            self.at(d=lax.rem(self.d + i, self.dp), w=lax.rem(self.w + k, self.wid))
            for i in range(self.dp)
            for k in range(self.wid)
            if i + k > 0
        ]


def send(src, dst, sent, got, peer):
    return pltpu.make_async_remote_copy(
        src_ref=src, dst_ref=dst, send_sem=sent, recv_sem=got, device_id=peer, device_id_type=MESH
    )


class Gather:
    def __init__(self, me, rows, full, col, width, ch, sz, rz, sy, ry):
        self.me, self.rows, self.full, self.ch = me, rows, full, ch
        self.col, self.width = col, width
        self.sz, self.rz, self.sy, self.ry = sz, rz, sy, ry

    def piece(self, d, o):
        return self.full.at[
            pl.ds(pl.multiple_of((d * self.me.wid + o) * self.rows, 16), self.rows), pl.ds(self.col, self.width)
        ]

    def origin(self, way, hop):
        return lax.clamp(0, self.me.w - way * hop, self.me.wid - 1)

    def zcopy(self, way, hop, sem):
        me, side = self.me, (way + 1) // 2
        part = self.piece(me.d, self.origin(way, hop))
        return send(
            part, part, self.sz.at[self.ch, side, sem], self.rz.at[self.ch, side, sem],
            me.at(w=lax.clamp(0, me.w + way, me.wid - 1)),
        )

    def ycopy(self, d, o, j):
        part = self.piece(d, o)
        return send(part, part, self.sy.at[self.ch, o, j - 1], self.ry.at[self.ch, o, j - 1], self.me.dp_peer(j))

    def has_next(self, way):
        return self.me.w < self.me.wid - 1 if way == 1 else self.me.w > 0

    def has_piece(self, way, hop):
        return self.me.w - hop >= 0 if way == 1 else self.me.w + hop < self.me.wid

    def start_z(self):
        for way in (1, -1):

            @pl.when(self.has_next(way))
            def _():
                self.zcopy(way, 0, 0).start()

    def start_y(self):
        for j in range(1, self.me.dp):
            self.ycopy(self.me.d, self.me.w, j).start()

    def hop(self, hop):
        me = self.me
        for way in (1, -1):

            @pl.when(self.has_piece(way, hop))
            def _():
                self.zcopy(way, hop, hop - 1).wait_recv()

                @pl.when(self.has_next(way))
                def _():
                    self.zcopy(way, hop, hop).start()

                for j in range(1, me.dp):
                    self.ycopy(me.d, self.origin(way, hop), j).start()

    def finish(self):
        me = self.me
        for j in range(1, me.dp):
            for o in range(me.wid):
                self.ycopy(lax.rem(me.d + me.dp - j, me.dp), o, j).wait_recv()

    def drain_z(self):
        me = self.me
        for way in (1, -1):
            for hop in range(me.wid):

                @pl.when(self.has_piece(way, hop) & self.has_next(way))
                def _():
                    self.zcopy(way, hop, hop).wait_send()

    def drain(self):
        self.drain_z()
        for j in range(1, self.me.dp):
            for o in range(self.me.wid):
                self.ycopy(self.me.d, o, j).wait_send()


class Line(Gather):
    def __init__(self, d, *args):
        super().__init__(*args)
        self.group = d

    def zcopy(self, way, hop, sem):
        me, side = self.me, (way + 1) // 2
        part = self.piece(self.group, self.origin(way, hop))
        return send(
            part, part, self.sz.at[self.ch, side, sem], self.rz.at[self.ch, side, sem],
            me.at(w=lax.clamp(0, me.w + way, me.wid - 1)),
        )

    def hop(self, hop):
        for way in (1, -1):

            @pl.when(self.has_piece(way, hop))
            def _():
                self.zcopy(way, hop, hop - 1).wait_recv()

                @pl.when(self.has_next(way))
                def _():
                    self.zcopy(way, hop, hop).start()


class Across(Gather):
    def __init__(self, extra, *args):
        super().__init__(*args)
        me, rows, full, col, width, ch = args[:6]
        self.lines = [
            Line(lax.rem(me.d + me.dp - j, me.dp), me, rows, full, col, width, ch if j == 0 else extra + j - 1, *args[6:])
            for j in range(me.dp)
        ]

    def start_z(self):
        self.lines[0].start_z()

    def hop(self, hop):
        me = self.me
        if hop == 0:
            for j in range(1, me.dp):
                self.ycopy(lax.rem(me.d + me.dp - j, me.dp), me.w, j).wait_recv()
                self.lines[j].start_z()
        else:
            for line in self.lines:
                line.hop(hop)

    def finish(self):
        pass

    def drain(self):
        for line in self.lines:
            line.drain_z()
        for j in range(1, self.me.dp):
            self.ycopy(self.me.d, self.me.w, j).wait_send()


def column(values, lane_index):
    lanes = lax.broadcasted_iota(jnp.int32, values.shape, 1)
    return jnp.sum(jnp.where(lanes == lane_index, values, 0.0), axis=1, keepdims=True)


def layer_kernel(
    cfg, lens, keep, tok, cot, gains, w_q, w_k, w_v, w_h, w_b, w_o, w_g, w_u, w_d,
    layer_out, tgrad, gsum, g_h, ry_h, z_h, zt_h, res_h,
    W, tokf, cotf, n1, n2, hlow, ng, mix, act, gg, ug, qs, ks, vs, hs, hraw, mgrad, xs, beta, dbeta, dB, gf, resb,
    s1, r1, s2, r2, acc, t2, q2, hidown, hgrad, stage, rts, rtr, rt, gbuf,
    local, own, hx_s, hx_r, sz, rz, sy, ry, s1s, s1r, s2s, s2r, s3s, s3r, ress, stages,
    ys, yr, zs, zr, zo, ld, rs_s, rs_r, gs_s, gs_r,
):
    me = Place(cfg["names"], cfg["sizes"])
    T, D, CB, HL, HD, FL, RS = (cfg[k] for k in ("T", "D", "CB", "HL", "HD", "FL", "RS"))
    FW = cfg["FW"]
    NF = 3 * FL // FW
    FB = 5 * HD
    BC = FB + 3 * FL
    GC, UC, DC, OC = FB, FB + FL, FB + 2 * FL, 4 * HD
    NB, U, DR = T // BUF, T // BUF * HL, RS * me.wid
    c = me.c
    own_cols = pl.ds(pl.multiple_of(me.h * CB, BLK), CB)
    own_rows = pl.ds(pl.multiple_of((me.d * me.wid + me.w) * RS, 16), RS)
    me.greet(me.group() + [me.hid_peer(k) for k in range(1, 4)])

    places = [(w_h, 3 * HD), (w_b, BC), (w_q, 0), (w_k, HD), (w_v, 2 * HD), (w_o, OC), (w_g, GC), (w_u, UC), (w_d, DC)]
    mine = [
        pltpu.make_async_copy(ref, W.at[own_rows, pl.ds(col, ref.shape[1])], own.at[i])
        for i, (ref, col) in enumerate(places)
    ]
    hid = []
    for i, (src, dst) in enumerate(((tok, tokf), (gains, gf), (cot, cotf))):
        here = pltpu.make_async_copy(src, dst.at[:, own_cols], local.at[i])
        away = [
            send(src, dst.at[:, own_cols], hx_s.at[i, k - 1], hx_r.at[i, k - 1], me.hid_peer(k)) for k in range(1, 4)
        ]
        hid.append([here] + away)
    for copy in mine[:6]:
        copy.start()
    for i in range(2):
        for copy in hid[i]:
            copy.start()
    for copy in mine[6:]:
        copy.start()
    sems = (sz, rz, sy, ry)
    first = [
        Gather(me, RS, W, col, ref.shape[1], i, *sems) for i, (ref, col) in enumerate(places[:6])
    ]

    def late(i):
        args = (me, RS, W, FB + i * FW, FW, 6 + i, *sems)
        if i in cfg["across"]:
            return Across(6 + NF + cfg["across"].index(i) * (me.dp - 1), *args)
        return Gather(*args)

    NG = len(first) + NF

    def chunk(n):
        return first[n] if n < len(first) else late(n - len(first))

    def begin(n):
        if n < NG:
            if n < len(first):
                mine[n].wait()
            elif n == len(first):
                for copy in mine[6:]:
                    copy.wait()
            chunk(n).start_z()
            chunk(n).start_y()

    events = [
        (k - hop + 1, hop) for k in range(NG + me.wid - 2) for hop in range(1, me.wid) if 0 <= k - hop + 1 < NG
    ]
    for i in cfg["across"]:
        events.insert(events.index((6 + i, 1)), (6 + i, 0))

    def advance(count):
        for _ in range(min(count, len(events))):
            n, hop = events.pop(0)
            chunk(n).hop(hop)

    for n in range(NG):
        begin(n)
    for copy in hid[2]:
        copy.start()
    for i in range(2):
        for copy in hid[i]:
            copy.wait()
    RB = 32

    def rows_of(m):
        return pl.ds(pl.multiple_of(m * BUF, BLK), BUF)

    def norm(src, dst, gain, base):
        def body(i, carry):
            rows = spans(base + i * RB, RB)
            wide = src[rows, :].astype(F32)
            scale = lax.rsqrt(jnp.mean(wide * wide, axis=1, keepdims=True) + EPSILON)
            dst[rows, :] = (wide * scale * gf[gain : gain + 1, :]).astype(BF)
            return carry

        lax.fori_loop(0, BUF // RB, body, 0)

    for m in range(NB):
        norm(tokf, n1, 0, m * BUF)

    def project(a):
        for m in range(NB):
            rows = n1[m * BUF : (m + 1) * BUF, :]
            made = nn(rows, W[:, a * HD : (a + 1) * HD])
            for hd in range(HL):
                part = made[:, hd * BLK : (hd + 1) * BLK]
                u = m * HL + hd
                if a < 3:
                    (qs, ks, vs)[a][u] = part.astype(BF)
                else:
                    hraw[u] = part
                    hs[u] = (part * lax.rsqrt(jnp.sum(part * part, axis=1, keepdims=True) + EPSILON)).astype(BF)
            if a == 3:
                beta[m * BUF : (m + 1) * BUF, :] = 2.0 * jax.nn.sigmoid(nn(rows, W[:, BC:]))

    advance(9)
    first[0].finish()
    first[1].finish()
    project(3)

    def invert(hd, carry):
        row, col = iotas()
        blocks = [(m, a) for m in range(NB) for a in range(3)]
        parts = [hs[m * HL + hd, a * BLK : (a + 1) * BLK, :] for m, a in blocks]
        strengths = [column(beta[m * BUF + a * BLK : m * BUF + (a + 1) * BLK, :], hd) for m, a in blocks]

        def between(level):
            for i in range(HL):
                later = slots[i].get(level, [])
                if later:

                    @pl.when(hd == i)
                    def _():
                        for n, hop in later:
                            chunk(n).hop(hop)

        made = tri_inverse([nt(part, part) for part in parts], strengths, row, col, between)
        for (m, a), x in zip(blocks, made):
            xs[m * HL + hd, a] = x.astype(BF)
        return carry

    advance(2)
    slots = [{level: [events.pop(0)] for level in (2, 4, 6) if events} for _ in range(HL)]
    lax.fori_loop(0, HL, invert, 0)
    for a in range(3):
        first[2 + a].finish()
        project(a)
        advance(2)

    def attend(u, carry):
        m, hd = lax.div(u, HL), lax.rem(u, HL)
        slot = lax.rem(u, 2)
        e0 = lens[m, 0]
        e1 = e0 + lens[m, 1]
        parts = [slice(a * BLK, (a + 1) * BLK) for a in range(3)]
        keys = [keep[0:1, p] for p in parts]
        for i in range(1, NB):
            keys = [jnp.where(m == i, keep[i : i + 1, p], key) for p, key in zip(parts, keys)]
        out, res = fwd_unit(
            [qs[u, p, :] for p in parts], [ks[u, p, :] for p in parts], [vs[u, p, :] for p in parts],
            [hs[u, p, :] for p in parts], [xs[u, a] for a in range(3)], keys, e0, e1,
        )
        for a in range(3):
            mix[spans(m * BUF + a * BLK, BLK), pl.ds(pl.multiple_of(hd * BLK, BLK), BLK)] = out[a].astype(BF)

        @pl.when(u >= 2)
        def _():
            pltpu.make_async_copy(resb.at[slot], res_h.at[u], ress.at[slot]).wait()

        for i, value in enumerate(res):
            resb[slot, i] = value
        pltpu.make_async_copy(resb.at[slot], res_h.at[u], ress.at[slot]).start()
        for m in range(NB):

            @pl.when(u == (m + 1) * HL - 1)
            def _():
                if m == 0:
                    first[5].finish()
                first_hop(0, m, branch(m))

            @pl.when(u == (m + 1) * HL)
            def _():
                second_hop(0, m)

        for i, (n, hop) in enumerate(during):

            @pl.when(u == i)
            def _():
                chunk(n).hop(hop)

        return carry

    def block(b):
        return pl.ds(pl.multiple_of(b * CB, BLK), CB)

    def hop1(tag, m, j):
        return send(s1.at[m, j], r1.at[tag % 3 // 2, m, j], s1s.at[tag, m, j], s1r.at[tag, m, j], me.sib)

    def hop2(tag, m, j):
        return send(s2.at[m, j], r2.at[tag, m, j], s2s.at[tag, m, j], s2r.at[tag, m, j], me.xpeer)

    def first_hop(tag, m, partial):
        for j in range(2):
            s1[m, j] = partial((1 - c) + 2 * j).astype(BF)
            hop1(tag, m, j).start()
        for j in range(2):
            acc[m, j] = partial(c + 2 * j)

    def second_hop(tag, m):
        for j in range(2):
            hop1(tag, m, j).wait()
            s2[m, j] = (acc[m, j] + r1[tag // 2, m, j].astype(F32)).astype(BF)
            hop2(tag, m, j).start()

    def total(tag, m, j):
        return s2[m, j].astype(F32) + r2[tag, m, j].astype(F32)

    def third(tag, full, m, j, core):
        part = full.at[rows_of(m), block(core + 2 * j)]
        return send(part, part, s3s.at[tag, m, j], s3r.at[tag, m, j], me.sib)

    def wait_third(tag, full, m):
        for j in range(2):
            third(tag, full, m, j, 1 - c).wait_recv()
            third(tag, full, m, j, c).wait_send()

    def branch(m):
        return lambda b: nt(mix[rows_of(m), :], W[block(b), OC : OC + HD])

    during = [events.pop(0) for _ in range(min(U, len(events)))]
    lax.fori_loop(0, U, attend, 0)
    for slot in range(2):
        pltpu.make_async_copy(resb.at[slot], res_h.at[0], ress.at[slot]).wait()
    second_hop(0, NB - 1)

    def residual(m):
        for j in range(2):
            hop2(0, m, j).wait()
            b = c + 2 * j
            hidden = tokf[rows_of(m), block(b)].astype(F32) + total(0, m, j)
            hlow[rows_of(m), block(b)] = hidden.astype(BF)
            third(0, hlow, m, j, c).start()
        hidown[rows_of(m), :] = tokf[rows_of(m), own_cols].astype(F32) + (
            s2[m, me.x].astype(F32) + r2[0, m, me.x].astype(F32)
        )

    for m in range(NB):
        residual(m)
        advance(2)
        wait_third(0, hlow, m)
        norm(hlow, n2, 8, m * BUF)
    for copy in hid[2]:
        copy.wait()

    NT = 256
    ND = 2 * FL // FW

    PER = FL // FW

    def ffn(m, part):
        def body(n, carry):
            at = pl.multiple_of(n * NT, NT)
            gate = nn(n2[rows_of(m), :], W[:, pl.ds(pl.multiple_of(GC + at, BLK), NT)])
            up = nn(n2[rows_of(m), :], W[:, pl.ds(pl.multiple_of(UC + at, BLK), NT)])
            sig = jax.nn.sigmoid(gate)
            silu = gate * sig
            cols = pl.ds(at, NT)
            act[rows_of(m), cols] = (silu * up).astype(BF)
            gg[rows_of(m), cols] = (up * sig * (1.0 + gate * (1.0 - sig))).astype(BF)
            ug[rows_of(m), cols] = silu.astype(BF)
            return carry

        lax.fori_loop(part * (FW // NT), (part + 1) * (FW // NT), body, 0)

    def ffn_back(m):
        def body(n, carry):
            at = pl.multiple_of(n * NT, NT)
            cols = pl.ds(at, NT)
            back = nn(cotf[rows_of(m), :], W[:, pl.ds(pl.multiple_of(DC + at, BLK), NT)])
            gg[rows_of(m), cols] = (back * gg[rows_of(m), cols].astype(F32)).astype(BF)
            ug[rows_of(m), cols] = (back * ug[rows_of(m), cols].astype(F32)).astype(BF)
            return carry

        lax.fori_loop(0, FL // NT, body, 0)

    def dp_rows(j):
        return pl.ds(pl.multiple_of(lax.rem(me.d + j, me.dp) * DR, 16), DR)

    def staged(side, i, col, width):
        return pltpu.make_async_copy(
            stage.at[side, i, :, pl.ds(0, width)],
            g_h.at[pl.ds(pl.multiple_of(i * CB, BLK), CB), pl.ds(col, width)],
            stages.at[side, i],
        )

    def rs_y(ch, col, width, j):
        return send(
            g_h.at[dp_rows(j), pl.ds(col, width)], ry_h.at[j - 1, :, pl.ds(col, width)],
            ys.at[ch, j - 1], yr.at[ch, j - 1], me.dp_peer(j),
        )

    pending = []
    made_terms = [0]

    def flush():
        side, ch, col, width = pending.pop()
        for i in range(D // CB):
            staged(side, i, col, width).wait()
        for j in range(1, me.dp):
            rs_y(ch, col, width, j).start()

    def weight_term(ch, left, right, at, col, width):
        side = made_terms[0] % 2
        made_terms[0] += 1

        def body(i, carry):
            stage[side, i, :, pl.ds(0, width)] = tn(
                left[:, pl.ds(pl.multiple_of(i * CB, BLK), CB)], right[:, at : at + width]
            ).astype(BF)
            staged(side, i, col, width).start()
            return carry

        lax.fori_loop(0, D // CB, body, 0)
        if pending:
            flush()
        pending.append((side, ch, col, width))

    def ffn_terms(left, right, col):
        for n in range(FL // FW):
            weight_term(6 + (col - FB) // FW + n, left, right, n * FW, col + n * FW, FW)

    for part in range(PER):
        advance(max([i + 1 for i, (n, _) in enumerate(events) if n <= 6 + PER + part], default=0))
        late(part).finish()
        late(PER + part).finish()
        for m in range(NB):
            ffn(m, part)
        weight_term(6 + 2 * PER + part, cotf, act, part * FW, DC + part * FW, FW)
        flush()
    advance(len(events))
    for i in range(ND, NF):
        late(i).finish()

    def normed_back(m):
        return lambda b: nt(gg[rows_of(m), :], W[block(b), GC : GC + FL]) + nt(
            ug[rows_of(m), :], W[block(b), UC : UC + FL]
        )

    def down(m):
        return lambda b: nt(act[rows_of(m), :], W[block(b), DC : DC + FL])

    ffn_back(0)
    first_hop(1, 0, normed_back(0))
    ffn_back(1)
    second_hop(1, 0)
    for m in range(1, NB):
        first_hop(1, m, normed_back(m))
        if m + 1 < NB:
            ffn_back(m + 1)
        second_hop(1, m)
    for g in first:
        g.drain()

    for i in range(NF):
        late(i).drain()
    ffn_terms(n2, gg, GC)
    ffn_terms(n2, ug, UC)
    flush()

    def hop2_out(m):
        return send(t2.at[m], q2.at[m], s2s.at[2, m, 0], s2r.at[2, m, 0], me.xpeer)

    for m in range(NB):
        first_hop(2, m, down(m))
    other = 1 - me.x
    for m in range(NB):
        for j in range(2):
            hop1(2, m, j).wait()
        t2[m] = (acc[m, other] + r1[1, m, other].astype(F32)).astype(BF)
        hop2_out(m).start()

    gm = W.at[0:DR, FB : FB + FW]
    peer_term = W.at[DR : 2 * DR, FB : FB + FW]
    inbox = W.at[DR : 2 * DR, FB + FW : FB + 2 * FW]

    def to_wid(slot):
        return W.at[0:DR, FB + FW + slot * FW : FB + 2 * FW + slot * FW]

    near = me.w + 1 - 2 * lax.rem(me.w, 2)
    far = 2 - 2 * lax.div(me.w, 2)
    inner = (me.w == 1) | (me.w == 2)
    outer = jnp.logical_not(inner)

    def block_rows(o, count=1):
        return pl.ds(pl.multiple_of(o * RS, 16), count * RS)

    def to_near(ch, col, width, slot):
        return send(
            to_wid(slot).at[block_rows(near), pl.ds(0, width)], z_h.at[1, :, pl.ds(col, width)],
            zs.at[ch, 0], zr.at[ch, 0], me.at(w=near),
        )

    def to_inner(ch, col, width, slot):
        return send(
            to_wid(slot).at[block_rows(far, 2), pl.ds(0, width)], zt_h.at[:, pl.ds(col, width)],
            zs.at[ch, 1], zr.at[ch, 1], me.at(w=near),
        )

    def to_far(ch, col, width, slot, i):
        return send(
            to_wid(slot).at[block_rows(far + i), pl.ds(0, width)], z_h.at[2, :, pl.ds(col, width)],
            zs.at[ch, 2 + i], zr.at[ch, 2], me.at(w=far + i),
        )

    def rs_free(ch, col, width, slot):
        to_near(ch, col, width, slot).wait_send()

        @pl.when(outer)
        def _():
            to_inner(ch, col, width, slot).wait_send()

        @pl.when(inner)
        def _():
            for i in range(2):
                to_far(ch, col, width, slot, i).wait_send()

    def rs_across(ch, col, width, slot):
        @pl.when(inner)
        def _():
            to_inner(ch, col, width, slot).wait_recv()
            load = pltpu.make_async_copy(
                zt_h.at[:, pl.ds(col, width)], inbox.at[pl.ds(0, 2 * RS), pl.ds(0, width)], ld.at[2]
            )
            load.start()
            load.wait()
            for i in range(2):
                rows = block_rows(far + i)
                to_wid(slot)[rows, 0:width] = (
                    to_wid(slot)[rows, 0:width].astype(F32) + inbox[i * RS : (i + 1) * RS, 0:width].astype(F32)
                ).astype(BF)
                to_far(ch, col, width, slot, i).start()

    def rs_end(ch, col, width):
        to_near(ch, col, width, 0).wait_recv()
        to_far(ch, col, width, 0, 0).wait_recv()

    def rs_stage(ch, col, width, slot):
        here = pltpu.make_async_copy(g_h.at[dp_rows(0), pl.ds(col, width)], gm.at[:, pl.ds(0, width)], ld.at[0])
        here.start()
        mine_out = pltpu.make_async_copy(
            to_wid(slot).at[block_rows(me.w), pl.ds(0, width)], z_h.at[0, :, pl.ds(col, width)], zo.at[ch]
        )
        for j in range(1, me.dp):
            rs_y(ch, col, width, j).wait_recv()
            there = pltpu.make_async_copy(
                ry_h.at[j - 1, :, pl.ds(col, width)], peer_term.at[:, pl.ds(0, width)], ld.at[1]
            )
            there.start()
            if j == 1:
                here.wait()
            there.wait()
            for i, o in enumerate((far, far + 1, near, me.w)):
                rows = block_rows(o)
                so_far = gm if j == 1 else to_wid(slot)
                to_wid(slot)[rows, 0:width] = (
                    so_far[rows, 0:width].astype(F32) + peer_term[rows, 0:width].astype(F32)
                ).astype(BF)
                if j == me.dp - 1:
                    if i == 1:

                        @pl.when(outer)
                        def _():
                            to_inner(ch, col, width, slot).start()

                    if i == 2:
                        to_near(ch, col, width, slot).start()
                    if i == 3:
                        mine_out.start()
        mine_out.wait()

    places_of = [(3 * HD, HD), (BC, BLK), (0, HD), (HD, HD), (2 * HD, HD), (OC, HD)]
    order = [(6 + (i + ND) % NF, FB + (i + ND) % NF * FW, FW) for i in range(NF)]
    order += [(k, *places_of[k]) for k in (5, 2, 3, 4)]
    order += [(0, 3 * HD, HD - BLK), (6 + NF, 4 * HD - BLK, BLK), (1, BC, BLK)]
    taken = [0]

    def take():
        n = taken[0]
        taken[0] += 1
        if n >= 4:
            rs_free(*order[n - 4], n % 4)
        rs_stage(*order[n], n % 4)
        if n >= 1:
            rs_across(*order[n - 1], (n - 1) % 4)
        if n == len(order) - 1:
            rs_across(*order[n], n % 4)

    def spread_back(m):
        for j in range(2):
            hop2(1, m, j).wait()
            ng[rows_of(m), block(c + 2 * j)] = total(1, m, j).astype(BF)
            third(1, ng, m, j, c).start()

    def branch_back(m):
        def body(i, carry):
            rows = spans(m * BUF + i * RB, RB)
            low = hlow[rows, :].astype(F32)
            scale = lax.rsqrt(jnp.mean(low * low, axis=1, keepdims=True) + EPSILON)
            scaled = ng[rows, :].astype(F32) * gf[8:9, :]
            row_total = jnp.sum(low * scaled, axis=1, keepdims=True)
            cube = scale * scale * scale * row_total / D
            low_own = hlow[rows, own_cols].astype(F32)
            ng_own = ng[rows, own_cols].astype(F32)
            hgrad[rows, :] = (
                cotf[rows, own_cols].astype(F32) + scale * gf[8:9, own_cols] * ng_own - low_own * cube
            )
            gbuf[slot_here, 8:16, :] += jnp.broadcast_to(
                jnp.sum(low_own * scale * ng_own, axis=0, keepdims=True), (8, CB)
            )
            ng[rows, :] = (cotf[rows, :].astype(F32) + scale * scaled - low * cube).astype(BF)
            return carry

        lax.fori_loop(0, BUF // RB, body, 0)
        made = nn(ng[rows_of(m), :], W[:, OC : OC + HD])
        for hd in range(HL):
            mgrad[m * HL + hd] = made[:, hd * BLK : (hd + 1) * BLK].astype(BF)

    slot_here = me.d * me.wid + me.w
    gbuf[slot_here] = jnp.zeros((16, CB), F32)
    dbeta[...] = jnp.zeros_like(dbeta)
    dA = n2

    def fetch_res(u):
        slot = lax.rem(u, 2)
        return pltpu.make_async_copy(res_h.at[u], resb.at[slot], ress.at[slot])

    fetch_res(0).start()

    def attend_back(u, carry):
        m, hd = lax.div(u, HL), lax.rem(u, HL)
        slot = lax.rem(u, 2)
        parts = [slice(a * BLK, (a + 1) * BLK) for a in range(3)]

        fetch_res(u).wait()

        @pl.when(u + 1 < U)
        def _():
            fetch_res(u + 1).start()

        dq, dk, dv, dh, db = bwd_unit(
            [qs[u, p, :] for p in parts], [ks[u, p, :] for p in parts], [vs[u, p, :] for p in parts],
            [hs[u, p, :] for p in parts], [mgrad[u, p, :] for p in parts], [xs[u, a] for a in range(3)],
            [resb[slot, i] for i in range(NRES)],
        )
        for a in range(3):
            rows = spans(m * BUF + a * BLK, BLK)
            for n, value in enumerate((dq[a], dk[a], dv[a])):
                dA[rows, pl.ds(pl.multiple_of(n * HD + hd * BLK, BLK), BLK)] = value.astype(BF)
            raw = hraw[u, parts[a], :]
            scale = lax.rsqrt(jnp.sum(raw * raw, axis=1, keepdims=True) + EPSILON)
            along = jnp.sum(raw * dh[a], axis=1, keepdims=True)
            dA[rows, pl.ds(pl.multiple_of(3 * HD + hd * BLK, BLK), BLK)] = (
                scale * dh[a] - raw * (scale * scale * scale * along)
            ).astype(BF)
            strength = column(beta[rows, :], hd)
            pull = db[a] * (1.0 / jnp.maximum(strength, 1e-30) - 0.5)
            lanes = lax.broadcasted_iota(jnp.int32, (BLK, BLK), 1)
            dbeta[rows, :] += jnp.where(lanes == hd, pull, 0.0)

        return carry

    take()
    for m in range(NB):
        spread_back(m)
        wait_third(1, ng, m)
        branch_back(m)
        if m < 2:
            take()
    lax.fori_loop(0, U, attend_back, 0)
    dB[...] = dbeta[...].astype(BF)
    weight_term(5, ng, mix, 0, OC, HD)
    take()
    for a in range(3):
        weight_term(2 + a, n1, dA, a * HD, a * HD, HD)
    take()
    weight_term(0, n1, dA, 3 * HD, 3 * HD, HD - BLK)
    weight_term(6 + NF, n1, dA, 4 * HD - BLK, 4 * HD - BLK, BLK)
    weight_term(1, n1, dB, 0, BC, BLK)
    flush()

    rt[...] = jnp.zeros_like(rt)

    def first_back(m):
        def partial(b):
            made = nt(dA[rows_of(m), :], W[block(b), 0 : 4 * HD]) + nt(dB[rows_of(m), :], W[block(b), BC:])
            along = jnp.sum(made * tokf[rows_of(m), block(b)].astype(F32) * gf[0:1, block(b)], axis=1, keepdims=True)
            rt[rows_of(m), :] += jnp.broadcast_to(along, (BUF, BLK))
            return made

        return partial

    for m in range(NB):
        hop2_out(m).wait()
        layer_out[rows_of(m), :] = (
            hidown[rows_of(m), :] + (acc[m, me.x] + r1[1, m, me.x].astype(F32) + q2[m].astype(F32))
        ).astype(BF)
    for m in range(NB):
        first_hop(3, m, first_back(m))
    for i in range(T // BLK):
        rts[:, i * BLK : (i + 1) * BLK] = rt[i * BLK : (i + 1) * BLK, :].T[0:8, :]
    rt_copies = [send(rts, rtr.at[k - 1], rs_s.at[k - 1], rs_r.at[k - 1], me.hid_peer(k)) for k in range(1, 4)]
    for copy in rt_copies:
        copy.start()

    def hop2_in(m):
        return send(t2.at[m], r2.at[0, m, 0], s2s.at[3, m, 0], s2r.at[3, m, 0], me.xpeer)

    for m in range(NB):
        for j in range(2):
            hop1(3, m, j).wait()
        t2[m] = (acc[m, other] + r1[0, m, other].astype(F32)).astype(BF)
        hop2_in(m).start()

    take()
    for m in range(NB):
        hop2_in(m).wait()
    for copy in rt_copies:
        copy.wait()

    def token_rows(i, carry):
        rows = spans(i * BLK, BLK)
        m = lax.div(i, BUF // BLK)
        part = spans(lax.rem(i, BUF // BLK) * BLK, BLK)
        lane = rts[0:1, rows] + rtr[0, 0:1, rows] + rtr[1, 0:1, rows] + rtr[2, 0:1, rows]
        row_total = jnp.broadcast_to(lane, (BLK, BLK)).T[:, 0:1]
        wide = tokf[rows, :].astype(F32)
        scale = lax.rsqrt(jnp.mean(wide * wide, axis=1, keepdims=True) + EPSILON)
        made = acc[m, me.x, part, :] + r1[0, m, me.x, part, :].astype(F32) + r2[0, m, 0, part, :].astype(F32)
        own_tok = tokf[rows, own_cols].astype(F32)
        back = scale * gf[0:1, own_cols] * made - own_tok * (scale * scale * scale * row_total / D)
        tgrad[rows, :] = (hgrad[rows, :] + back).astype(BF)
        gbuf[slot_here, 0:8, :] += jnp.broadcast_to(jnp.sum(own_tok * scale * made, axis=0, keepdims=True), (8, CB))
        return carry

    lax.fori_loop(0, T // BLK, token_rows, 0)
    gain_copies = []
    for n, peer in enumerate(me.group()):
        copy = send(gbuf.at[slot_here], gbuf.at[slot_here], gs_s.at[n], gs_r.at[n], peer)
        copy.start()
        gain_copies.append(copy)
    while taken[0] < len(order):
        take()
    for copy in gain_copies:
        copy.wait()
    both = gbuf[0]
    for n in range(1, me.dp * me.wid):
        both = both + gbuf[n]
    gsum[...] = both
    for ch, col, width in order:
        rs_end(ch, col, width)
    for n in range(len(order) - 4, len(order)):
        rs_free(*order[n], n % 4)
    for ch, col, width in order:
        for j in range(1, me.dp):
            rs_y(ch, col, width, j).wait_send()


def final_kernel(
    cfg, z_h, layer_in, tgrad_in, gsum,
    layer_out, tgrad, one, two, o_q, o_k, o_v, o_h, o_b, o_o, o_g, o_u, o_d,
    zbuf, total, gb, loads, stores, through,
):
    HD, FL, RS = cfg["HD"], cfg["FL"], cfg["RS"]
    FB = 5 * HD
    targets = [(o_g, FB, FL), (o_u, FB + FL, FL), (o_d, FB + 2 * FL, FL), (o_q, 0, HD), (o_k, HD, HD), (o_v, 2 * HD, HD)]
    targets += [(o_h, 3 * HD, HD), (o_o, 4 * HD, HD), (None, FB + 3 * FL, BLK)]
    passed = [
        pltpu.make_async_copy(layer_in, layer_out, through.at[0]),
        pltpu.make_async_copy(tgrad_in, tgrad, through.at[1]),
        pltpu.make_async_copy(gsum, gb, through.at[2]),
    ]
    copies = [
        pltpu.make_async_copy(z_h.at[:, :, pl.ds(col, w)], zbuf.at[:, :, pl.ds(col, w)], loads.at[i])
        for i, (_, col, w) in enumerate(targets)
    ]
    for copy in copies + passed:
        copy.start()
    written = []
    for i, (out, col, w) in enumerate(targets):
        copies[i].wait()
        value = zbuf[0, :, col : col + w].astype(F32)
        for k in range(1, 3):
            value = value + zbuf[k, :, col : col + w].astype(F32)
        if out is None:
            o_b[...] = value[:, 0 : o_b.shape[1]]
        else:
            total[:, col : col + w] = value
            copy = pltpu.make_async_copy(total.at[:, pl.ds(col, w)], out, stores.at[i])
            copy.start()
            written.append(copy)
    passed[2].wait()
    one[...] = gb[0:1, :]
    two[...] = gb[8:9, :]
    for copy in passed[:2] + written:
        copy.wait()


def solution(mesh):
    names = tuple(mesh.axis_names)
    sizes = {n: mesh.shape[n] for n in names}
    dp, wid = sizes["dp"], sizes["wid"]
    assert sizes["hid"] == 4 and wid == 4

    def shards(
        tokens, cotangent, lengths, keep, norm_one, w_query, w_key, w_value, w_house, w_beta, w_out, norm_two,
        w_gate, w_up, w_down,
    ):
        micro, rows, CB = tokens.shape
        T, D, HD, FL, RS = micro * rows, CB * 4, w_query.shape[1], w_gate.shape[1], w_query.shape[0]
        HL, NB, FW = HD // BLK, T // BUF, 512
        U, NF, DR = NB * HL, 3 * FL // FW, D // dp
        CT = 5 * HD + 3 * FL + BLK
        heads = w_beta.shape[1]
        cfg = dict(names=names, sizes=sizes, T=T, D=D, CB=CB, HL=HL, HD=HD, FL=FL, RS=RS, FW=FW, across=[4, 5])
        gains = jnp.concatenate([jnp.broadcast_to(g, (8, CB)) for g in (norm_one, norm_two)], axis=0).astype(F32)
        sd = jax.ShapeDtypeStruct
        nch = 6 + NF
        vm = pltpu.VMEM
        unit = lambda t: vm((U, BUF, BLK), t)
        pair = vm((NB, 2, BUF, CB), BF)
        outs = pl.pallas_call(
            functools.partial(layer_kernel, cfg),
            out_shape=(
                sd((T, CB), BF), sd((T, CB), BF), sd((16, CB), F32),
                sd((D, CT), BF), sd((dp - 1, DR, CT), BF), sd((3, RS, CT), BF), sd((2 * RS, CT), BF),
                sd((U, NRES, BLK, BLK), BF),
            ),
            in_specs=[SM, VM] + [ANY] * 12,
            out_specs=(VM,) * 3 + (ANY,) * 5,
            scratch_shapes=[
                vm((D, CT), BF), *[vm((T, D), BF)] * 6, vm((T, HD), BF), *[vm((T, FL), BF)] * 3,
                *[unit(BF)] * 4, unit(F32), unit(BF), vm((U, 3, BLK, BLK), BF), vm((T, BLK), F32), vm((T, BLK), F32), vm((T, BLK), BF),
                vm((16, D), F32), vm((2, NRES, BLK, BLK), BF),
                pair, vm((2, NB, 2, BUF, CB), BF), pair, vm((2, NB, 2, BUF, CB), BF), vm((NB, 2, BUF, CB), F32),
                vm((NB, BUF, CB), BF), vm((NB, BUF, CB), BF), vm((T, CB), F32), vm((T, CB), F32),
                vm((2, 4, CB, FW), BF),
                vm((8, T), F32), vm((3, 8, T), F32), vm((T, BLK), F32), vm((dp * wid, 16, CB), F32),
                DMA((3,)), DMA((9,)), DMA((3, 3)), DMA((3, 3)), *[DMA((nch + len(cfg["across"]) * (dp - 1), 2, wid))] * 2,
                DMA((nch, wid, dp - 1)), DMA((nch, wid, dp - 1)),
                *[DMA((4, NB, 2))] * 4, *[DMA((2, NB, 2))] * 2, DMA((2,)), DMA((2, 4)),
                DMA((nch + 1, dp - 1)), DMA((nch + 1, dp - 1)), DMA((nch + 1, 4)), DMA((nch + 1, 3)), DMA((nch + 1,)),
                DMA((3,)), DMA((3,)), DMA((3,)), DMA((dp * wid - 1,)), DMA((dp * wid - 1,)),
            ],
            compiler_params=pltpu.CompilerParams(
                collective_id=0, has_side_effects=True, vmem_limit_bytes=cfg.get("limit", 63 << 20)
            ),
            name="layer",
        )(
            lengths.reshape(NB, lengths.shape[2]), keep.reshape(NB, BUF), tokens.reshape(T, CB),
            cotangent.reshape(T, CB), gains, w_query, w_key, w_value, w_house,
            jnp.pad(w_beta, ((0, 0), (0, BLK - heads))), w_out.T, w_gate, w_up, w_down.T,
        )
        done = pl.pallas_call(
            functools.partial(final_kernel, cfg),
            out_shape=(
                sd((T, CB), BF), sd((T, CB), BF), sd((1, CB), F32), sd((1, CB), F32),
                *[sd((RS, HD), F32)] * 4, sd((RS, heads), F32), sd((RS, HD), F32), *[sd((RS, FL), F32)] * 3,
            ),
            in_specs=[ANY] * 4,
            out_specs=(ANY, ANY, VM, VM) + (ANY,) * 4 + (VM,) + (ANY,) * 4,
            scratch_shapes=[
                vm((3, RS, CT), BF), vm((RS, CT), F32), vm((16, CB), F32), DMA((9,)), DMA((9,)), DMA((3,)),
            ],
            compiler_params=pltpu.CompilerParams(vmem_limit_bytes=32 << 20),
            name="final",
        )(outs[5], outs[0], outs[1], outs[2])
        layer_out, tgrad, one, two, gq, gk, gv, gh, gb, go, g_gate, g_up, g_down = done
        return (
            layer_out.reshape(tokens.shape), tgrad.reshape(tokens.shape), one, gq, gk, gv, gh, gb, go.T, two,
            g_gate, g_up, g_down.T,
        )

    rows = P(("dp", "wid"), "hid")
    cols = P("hid", ("dp", "wid"))
    wide = P(None, ("dp", "wid"), "hid")
    gain = P(None, "hid")
    return jax.shard_map(
        shards,
        mesh=mesh,
        in_specs=(
            wide, wide, P(None, ("dp", "wid"), None), P(None, ("dp", "wid")), gain, rows, rows, rows, rows, rows,
            cols, gain, rows, rows, cols,
        ),
        out_specs=(wide, wide, gain, rows, rows, rows, rows, rows, cols, gain, rows, rows, cols),
        check_vma=False,
    )
```
